128 devices in a mesh: seq: 32 (over y, z, core), head: 4 (over x).
Axes of the slice: x: 4, y: 4, z: 4, core: 2. Of those that a mesh axis runs over, the one named last changes fastest.
Arguments:
- hidden_in: bfloat16 [8192, 2048], P('seq'), may hold values from -6 to 6
- attn_gain: float32 [2048], replicated, may hold values from 0.1 to 1.9
- w_qkv: bfloat16 [2048, 3, 2048], P(None, None, 'head'), may hold values from -0.125 to 0.125
- out_gain: float32 [2048], P('head'), may hold values from 0.1 to 1.9
- w_out: bfloat16 [2048, 2048], P('head'), may hold values from -0.125 to 0.125
- moe_gain: float32 [2048], replicated, may hold values from 0.1 to 1.9
- routes: int32 [8192, 8], P(('seq', 'head')), may hold values from 0 to 63, all different within a row; in each aligned block of 64 rows (0 to 63, 64 to 127, ...) at most 9 rows name the same one
- gate_weights: float32 [8192, 8], P(('seq', 'head')), may hold values from 0.1 to 0.6
- w_gate_up: bfloat16 [64, 2, 2048, 1024], P('seq', None, None, 'head'), may hold values from -0.125 to 0.125
- w_down: bfloat16 [64, 1024, 2048], P('seq', 'head'), may hold values from -0.1875 to 0.1875
Outputs:
- layer_out: bfloat16 [8192, 2048], P(('seq', 'head'))
The draws below stay inside these ranges and needn't reach their ends.
Inputs may be any that keep to these rules, and one draw needn't show every extreme that they name: `routes`: each row names 8 different experts; within each aligned block of 64 rows (the rows of one device) no expert is named more than 9 times, a bound that some block reaches.
All inputs are finite; a program needn't handle non-finite values.
Results may differ from the reference program's by a relative error of at most 0.015.
Values may be sent and summed in bfloat16 or wider, within the bound.
No kernel may reach another device: no remote copies, remote signals or barrier semaphores. Data moves between devices by JAX's collectives and lax.ppermute only.
A program may use at most 128 MiB of HBM per device.

```python
import math
import jax
import jax.numpy as jnp
import numpy as np
from jax import lax

D = 2048
H = 16
DH = 128
FF = 1024
EXPERTS = 64
TOP = 8
TOK_DEV = 256
HD = 2048
ROWS = 64
CAP = 9
TOKENS = 8192
N_HEAD = 4


def level_of(key, shape, split, least, top_value):
    level = 1.0
    for dim, shards_of in split:
        draws = jax.random.uniform(jax.random.fold_in(jax.random.fold_in(key, 6), dim), (shards_of,), jnp.float32, least / len(split), top_value / len(split))
        level = level * jnp.repeat(jnp.exp(draws), shape[dim] // shards_of).reshape((-1,) + (1,) * (len(shape) - 1 - dim))
    return level


def assign_block(key, own, number, rows, number_of, top, limit, skew):
    order = jax.random.permutation(key, number_of)
    packed, common = shares(number_of, rows * top, limit, skew, True), shares(number_of, rows * top, limit, skew, False)
    places = jnp.arange(number_of)

    def named(lengths, offset_by):
        used = int((lengths > 0).sum())
        fixed = max(1, used // 4)
        shifted = fixed + (places - fixed + offset_by * (used - fixed)) % max(1, number_of - fixed)
        return jnp.zeros((number_of,), jnp.int32).at[order[jnp.where(places < fixed, places, shifted)]].set(jnp.asarray(lengths, jnp.int32))

    lengths = jnp.where(number % 4 == 0, named(packed, number // 4), named(common, number - number // 4 - 1))
    mixed = jax.random.permutation(jax.random.fold_in(own, 3), number_of)
    source_of, sink = mixed[0:number_of // 2 * 2:2], mixed[1:number_of // 2 * 2:2]
    margin = jnp.minimum(lengths[source_of] - 1, limit - lengths[sink]) // 2
    margin = jnp.where((source_of == order[0]) | (sink == order[0]) | (lengths[sink] == 0), 0, jnp.maximum(margin, 0))
    shifted = jax.random.randint(jax.random.fold_in(own, 4), (number_of // 2,), 0, 1 << 20) % (margin + 1)
    lengths = lengths.at[source_of].add(-shifted).at[sink].add(shifted)
    labels = jnp.searchsorted(jnp.cumsum(lengths), jnp.arange(rows * top), side="right").astype(jnp.int32)
    table = labels.reshape(top, rows).T
    table = table[jax.random.permutation(jax.random.fold_in(own, 1), rows)]
    offset_by = jax.random.randint(jax.random.fold_in(own, 2), (rows, 1), 0, top)
    return jnp.take_along_axis(table, (jnp.arange(top)[None, :] + offset_by) % top, axis=1)


def shares(number_of, total, reach, lean, full):
    loads = [(1 << 20) // math.isqrt(standing ** lean) + 1 for standing in range(1, number_of + 1)]
    largest = reach if full else min(reach, max(-(-total // number_of), total * loads[0] // sum(loads)))
    least = 1 if total - largest >= number_of - 1 else 0
    holding, spare = [largest] + [least] * (number_of - 1), total - largest - least * (number_of - 1)
    while spare > 0:
        movable = [i for i in range(1, number_of) if holding[i] < largest] or [i for i in range(1, number_of) if holding[i] < reach]
        whole, left = sum([loads[i] for i in movable]), spare
        for i in movable:
            addition = min(reach - holding[i], max(1, left * loads[i] // whole), spare)
            holding[i] = holding[i] + addition
            spare = spare - addition
    return np.array(holding)


def gaussian(stream_key, dims, width, bound, pieces=(), kind=jnp.bfloat16):
    drawn = width * jax.random.normal(stream_key, dims, jnp.float32)
    if pieces:
        drawn = drawn * level_of(stream_key, dims, pieces, -0.22, 0.18)
    return jnp.clip(drawn, -bound, bound).astype(kind)


def setup_inputs(seed: int = 0) -> dict:
    keys = jax.random.split(jax.random.key(seed), 11)
    hidden_in = gaussian(keys[0], (TOKENS, D), 1.0, 6.0, ((0, 32),))
    attn_gain = jnp.clip(1.0 + 0.18 * jax.random.normal(keys[1], (D,), jnp.float32), 0.1, 1.9)
    w_qkv = gaussian(keys[2], (D, 3, HD), D ** -0.5, 0.125, ((2, 4),))
    out_gain = jnp.clip(1.0 + 0.18 * jax.random.normal(keys[3], (HD,), jnp.float32), 0.1, 1.9)
    w_out = gaussian(keys[4], (HD, D), HD ** -0.5, 0.125, ((0, 4),))
    moe_gain = jnp.clip(1.0 + 0.18 * jax.random.normal(keys[5], (D,), jnp.float32), 0.1, 1.9)
    routes_keys = jax.random.split(jax.random.fold_in(keys[6], 1), TOKENS // ROWS)
    routes_turns = jax.random.permutation(jax.random.fold_in(keys[6], 3), TOKENS // ROWS)
    routes = jax.vmap(lambda own, number: assign_block(jax.random.fold_in(keys[6], 2), own, number, ROWS, EXPERTS, TOP, CAP, 2))(routes_keys, routes_turns).reshape((TOKENS, TOP))
    gate_weights = jnp.clip(jnp.exp(math.log(0.6) - 1.7917595 * jax.random.uniform(keys[7], (TOKENS, TOP), jnp.float32) ** level_of(keys[7], (TOKENS, TOP), ((0, 128),), -0.2, 0.2)), 0.1, 0.6)
    w_gate_up = gaussian(keys[8], (EXPERTS, 2, D, FF), D ** -0.5, 0.125, ((0, 32), (3, 4)))
    w_down = gaussian(keys[9], (EXPERTS, FF, D), FF ** -0.5, 0.1875, ((0, 32), (1, 4)))
    return {"hidden_in": hidden_in, "attn_gain": attn_gain, "w_qkv": w_qkv, "out_gain": out_gain, "w_out": w_out, "moe_gain": moe_gain, "routes": routes, "gate_weights": gate_weights, "w_gate_up": w_gate_up, "w_down": w_down}


EPSILON = 1e-06

def rms_norm(values, gain):
    mean_square = lax.optimization_barrier(jnp.mean(values * values, axis=-1, keepdims=True))
    return values * lax.rsqrt(mean_square + EPSILON) * gain

def slot_table(route_rows):
    flat_routes = route_rows.reshape(-1)
    experts_iota = jnp.arange(EXPERTS, dtype=jnp.int32)
    onehot = (flat_routes[:, None] == experts_iota[None, :]).astype(jnp.int32)
    before = jnp.cumsum(onehot, axis=0) - onehot
    position = lax.optimization_barrier(jnp.sum(before * onehot, axis=1))
    return position.reshape(route_rows.shape)

def reference(hidden_in, attn_gain, w_qkv, out_gain, w_out, moe_gain, routes, gate_weights, w_gate_up, w_down):
    highest = lax.Precision.HIGHEST
    resid_in = hidden_in.astype(jnp.float32)
    normed = rms_norm(resid_in, attn_gain).astype(jnp.bfloat16)
    projected = jnp.dot(normed, w_qkv.reshape(D, 3 * HD), preferred_element_type=jnp.float32)
    projected = projected.astype(jnp.bfloat16).reshape(TOKENS, 3, H, DH)
    block_total = TOKENS // TOK_DEV
    query = projected[:, 0].reshape(block_total, TOK_DEV, H, DH)
    keys_all = projected[:, 1].reshape(block_total, TOK_DEV, H, DH)
    values_all = projected[:, 2].reshape(block_total, TOK_DEV, H, DH)
    causal = jnp.tril(jnp.ones((TOK_DEV, TOK_DEV), jnp.float32))

    def block_step(carried, inputs):
        query_blk, key_blk, value_blk = inputs
        query32 = query_blk.astype(jnp.float32)
        key32 = key_blk.astype(jnp.float32)
        value32 = value_blk.astype(jnp.float32)
        scores = jnp.einsum('thd,shd->hts', query32, key32, precision=highest) * causal
        scores = scores.astype(jnp.bfloat16).astype(jnp.float32)
        local_part = jnp.einsum('hts,shd->thd', scores, value32, precision=highest)
        remote_part = jnp.einsum('thd,hde->the', query32, carried, precision=highest)
        new_state = carried + jnp.einsum('thd,the->hde', key32, value32, precision=highest)
        return (new_state, local_part + remote_part)
    start_state = jnp.zeros((H, DH, DH), jnp.float32)
    final_state, attended = lax.scan(block_step, start_state, (query, keys_all, values_all))
    attended = attended.reshape(TOKENS, H, DH)
    head_square = lax.optimization_barrier(jnp.mean(attended * attended, axis=-1, keepdims=True))
    mixed = (attended * lax.rsqrt(head_square + EPSILON)).reshape(TOKENS, HD) * out_gain
    mixed = mixed.astype(jnp.bfloat16)
    resid = resid_in + jnp.dot(mixed, w_out, preferred_element_type=jnp.float32)
    normed2 = rms_norm(resid, moe_gain).astype(jnp.bfloat16)
    group_count = TOKENS // ROWS
    position = jax.vmap(slot_table)(routes.reshape(group_count, ROWS, TOP)).reshape(TOKENS, TOP)
    group_ids = (jnp.arange(TOKENS, dtype=jnp.int32) // ROWS)[:, None]
    flat_index = (routes * (group_count * CAP) + group_ids * CAP + position).astype(jnp.int32)
    token_ids = jnp.repeat(jnp.arange(TOKENS, dtype=jnp.int32), TOP)
    table = jnp.full((EXPERTS * group_count * CAP,), TOKENS, jnp.int32)
    table = table.at[flat_index.reshape(-1)].set(token_ids)
    padded = jnp.concatenate([normed2, jnp.zeros((1, D), jnp.bfloat16)], axis=0)
    quarter = FF // N_HEAD

    def run_expert(inputs):
        table_rows, gate_up, down_rows = inputs
        rows_in = padded[table_rows]
        gate_val = jnp.dot(rows_in, gate_up[0], preferred_element_type=jnp.float32)
        up_val = jnp.dot(rows_in, gate_up[1], preferred_element_type=jnp.float32)
        hidden_units = (jax.nn.silu(gate_val) * up_val).astype(jnp.bfloat16)
        total = jnp.zeros((rows_in.shape[0], D), jnp.float32)
        for group_idx in range(N_HEAD):
            part = jnp.dot(hidden_units[:, group_idx * quarter:(group_idx + 1) * quarter], down_rows[group_idx * quarter:(group_idx + 1) * quarter], preferred_element_type=jnp.float32)
            total = total + part.astype(jnp.bfloat16).astype(jnp.float32)
        return total.astype(jnp.bfloat16)
    expert_rows = lax.map(run_expert, (table.reshape(EXPERTS, group_count * CAP), w_gate_up, w_down))
    picked = expert_rows.reshape(EXPERTS * group_count * CAP, D)[flat_index]
    moe_sum = lax.optimization_barrier(jnp.sum(gate_weights[:, :, None] * picked.astype(jnp.float32), axis=1))
    return (resid + moe_sum).astype(jnp.bfloat16)
```

```python
import jax
import jax.numpy as jnp
from jax import lax
from jax.sharding import PartitionSpec as P

D = 2048
DH = 128
EXPERTS = 64
TOP = 8
CAP = 9
ROWS = 64
EPSILON = 1e-06
BF = jnp.bfloat16
F32 = jnp.float32


def rms_norm(values, gain):
    mean_square = jnp.mean(values * values, axis=-1, keepdims=True)
    return values * lax.rsqrt(mean_square + EPSILON) * gain


def dot(first, second):
    return jnp.dot(first, second, preferred_element_type=F32)


def seq_perm(dy, dz, dc):
    return [
        ((y * 4 + z) * 2 + c, (((y + dy) % 4) * 4 + (z + dz) % 4) * 2 + (c ^ dc))
        for y in range(4)
        for z in range(4)
        for c in range(2)
    ]


def head_perm(shift):
    return [(h, (h + shift) % 4) for h in range(4)]


def device_perm(target):
    pairs = []
    for chip in range(16):
        for c in range(2):
            for h in range(4):
                to = target(c, h)
                if to is not None:
                    pairs.append(((chip * 2 + c) * 4 + h, (chip * 2 + to[0]) * 4 + to[1]))
    return pairs


def near_target(c, h):
    chip = 2 * c + 1 - (h & 1)
    return (c, chip) if (chip - 1) % 4 == h else (1 - c, chip)


def far_target(c, h):
    return None if h // 2 == c else (1 - c, (h + 2) % 4)


def permute_all(arrays, axes, perm):
    return [lax.ppermute(a, axes, perm) for a in arrays]


def gather_weights(w_gate_up, w_down, core, head):
    odd = head & 1

    def pick(index):
        return [
            lax.dynamic_index_in_dim(w_gate_up, index, 0, False),
            lax.dynamic_index_in_dim(w_down, index, 0, False),
        ]

    both = ("seq", "head")
    near = permute_all(pick(1 - odd), both, device_perm(near_target))
    rest = pick(odd)
    far = permute_all(rest, both, device_perm(far_target))
    keep = head // 2 == core
    rest = [jnp.where(keep, a, b) for a, b in zip(rest, far)]
    swap = seq_perm(0, 0, 1)
    near_other = permute_all(near, "seq", swap)
    rest_other = permute_all(rest, "seq", swap)
    return [near, near_other, rest, rest_other]


def earlier_state(own, core, z, y):
    sibling = lax.ppermute(own.astype(BF), "seq", seq_perm(0, 0, 1)).astype(F32)
    prefix = jnp.where(core == 1, sibling, 0.0)
    total = own + sibling
    for place, step in ((z, (0, 1)), (y, (1, 0))):
        sent = total.astype(BF)
        for k in range(1, 4):
            got = lax.ppermute(sent, "seq", seq_perm(step[0] * k, step[1] * k, 0)).astype(F32)
            prefix = prefix + jnp.where(place >= k, got, 0.0)
            total = total + got
    return prefix


def gather_head(array):
    head = lax.axis_index("head")
    out = jnp.zeros((4,) + array.shape, array.dtype)
    out = lax.dynamic_update_index_in_dim(out, array, head, 0)
    for k in range(1, 4):
        got = lax.ppermute(array, "head", head_perm(k))
        out = lax.dynamic_update_index_in_dim(out, got, (head - k) % 4, 0)
    return out


def scatter_head(blocks):
    head = lax.axis_index("head")
    total = lax.dynamic_index_in_dim(blocks, head, 0, False)
    for k in range(1, 4):
        sent = lax.dynamic_index_in_dim(blocks, (head + k) % 4, 0, False).astype(BF)
        total = total + lax.ppermute(sent, "head", head_perm(k)).astype(F32)
    return total


def pack(main, tail):
    tail = tail.reshape(32, 2, 16, 128).transpose(0, 2, 1, 3).reshape(32, 16, 256)
    return jnp.concatenate([main.reshape(32, 16, D), tail], axis=2)


def unpack(packed):
    main = packed[:, :, :D].reshape(512, D)
    tail = packed[:, :, D:].reshape(32, 16, 2, 128).transpose(0, 2, 1, 3).reshape(64, D)
    return main, tail


def on_device(
    hidden_in, attn_gain, w_qkv, out_gain, w_out, moe_gain, routes, gate_weights, w_gate_up, w_down
):
    seq = lax.axis_index("seq")
    head = lax.axis_index("head")
    core = seq % 2
    z = (seq // 2) % 4
    y = seq // 8

    pieces = gather_weights(w_gate_up, w_down, core, head)

    tables = gather_head(jnp.concatenate([routes.astype(F32), gate_weights], axis=1))
    tables = tables.reshape(4 * ROWS, 2 * TOP)

    resid_in = hidden_in.astype(F32)
    normed = rms_norm(resid_in, attn_gain).astype(BF)
    projected = dot(normed, w_qkv.reshape(D, 3 * 4 * DH)).astype(BF).reshape(256, 3, 4, DH)
    query = projected[:, 0]
    key = projected[:, 1]
    value = projected[:, 2]
    own_state = jnp.einsum("thd,the->hde", key, value, preferred_element_type=F32)
    earlier = earlier_state(own_state, core, z, y)
    causal = jnp.tril(jnp.ones((256, 256), F32))
    scores = jnp.einsum("thd,shd->hts", query, key, preferred_element_type=F32) * causal
    local_part = jnp.einsum(
        "hts,shd->thd", scores.astype(BF), value, preferred_element_type=F32
    )
    high = earlier.astype(BF)
    low = (earlier - high.astype(F32)).astype(BF)
    remote_part = jnp.einsum("thd,hde->the", query, high, preferred_element_type=F32) + jnp.einsum(
        "thd,hde->the", query, low, preferred_element_type=F32
    )
    attended = local_part + remote_part
    head_square = jnp.mean(attended * attended, axis=-1, keepdims=True)
    mixed = (attended * lax.rsqrt(head_square + EPSILON)).reshape(256, 4 * DH) * out_gain
    attn_rows = scatter_head(dot(mixed.astype(BF), w_out).reshape(4, ROWS, D))
    resid = lax.dynamic_slice_in_dim(resid_in, head * ROWS, ROWS, 0) + attn_rows
    normed2 = rms_norm(resid, moe_gain).astype(BF)
    tokens = gather_head(normed2).reshape(4 * ROWS, D)

    named = tables[:, :TOP].astype(jnp.int32)
    wanted = jnp.arange(16, dtype=jnp.int32) * 4 + head
    hit = named[:, :, None] == wanted[None, None, :]
    chosen = jnp.sum(hit.astype(F32), axis=1)
    gates = jnp.sum(jnp.where(hit, tables[:, TOP:, None], 0.0), axis=1)
    index = jnp.arange(256, dtype=jnp.int32)
    block = index // ROWS
    before = (block[:, None] == block[None, :]) & (index[None, :] < index[:, None])
    rank = dot(before.astype(BF), chosen.astype(BF)).astype(jnp.int32)
    slot = jnp.where(chosen > 0, (block // 2 * 18 + block % 2 * CAP)[:, None] + rank, -1)
    rows = jnp.arange(36, dtype=jnp.int32)
    place = slot.T[:, None, :] == rows[None, :, None]
    weight = jnp.where(place, gates.T[:, None, :], 0.0).reshape(32, 18, 256)
    place = place.astype(BF).reshape(32, 18, 256)

    def split(array):
        return array[:, :16].reshape(512, 256), array[:, 16:].reshape(64, 256)

    place_main, place_tail = split(place)
    weight_main, weight_tail = split(weight)

    sent = pack(dot(place_main, tokens).astype(BF), dot(place_tail, tokens).astype(BF))
    got_main, got_tail = unpack(lax.all_to_all(sent, "seq", 0, 0, tiled=True))
    rows_in = jnp.concatenate([got_main, got_tail], axis=0)
    total = jnp.zeros((576, D), F32)
    for gate_up, down in pieces:
        gate_val = dot(rows_in, gate_up[0])
        up_val = dot(rows_in, gate_up[1])
        total = total + dot((jax.nn.silu(gate_val) * up_val).astype(BF), down)
    total = total.astype(BF)
    back = lax.all_to_all(pack(total[:512], total[512:]), "seq", 0, 0, tiled=True)
    back_main, back_tail = unpack(back)

    def combine(weights, values):
        hi = weights.astype(BF)
        lo = (weights - hi.astype(F32)).astype(BF)
        return dot(hi.T, values) + dot(lo.T, values)

    moe = combine(weight_main, back_main) + combine(weight_tail, back_tail)
    moe_sum = scatter_head(moe.reshape(4, ROWS, D))
    return (resid + moe_sum).astype(BF)


def solution(mesh):
    placed = (
        P("seq", None),
        P(),
        P(None, None, "head"),
        P("head"),
        P("head", None),
        P(),
        P(("seq", "head"), None),
        P(("seq", "head"), None),
        P("seq", None, None, "head"),
        P("seq", "head", None),
    )
    return jax.shard_map(
        on_device, mesh=mesh, in_specs=placed, out_specs=P(("seq", "head"), None), check_vma=False
    )
```

```python
import jax
import jax.numpy as jnp
from jax import lax
from jax.experimental import pallas as pl
from jax.experimental.pallas import tpu as pltpu
from jax.sharding import PartitionSpec as P

D = 2048
DH = 128
HEADS = 4
WIDE = HEADS * DH
TOP = 8
CAP = 9
ROWS = 64
TOK = 256
MAIN = 512
SLOTS = 576
PACKED = D + 256
EPSILON = 1e-06
BF = jnp.bfloat16
F32 = jnp.float32


VMEM = pl.BlockSpec(memory_space=pltpu.VMEM)
SMEM = pl.BlockSpec(memory_space=pltpu.SMEM)
ANY = pl.BlockSpec(memory_space=pl.ANY)


def out(shape, dtype):
    return jax.ShapeDtypeStruct(shape, dtype)


def call(kernel, ins, outs, scratch=()):
    return pl.pallas_call(
        kernel,
        in_specs=ins,
        out_specs=[VMEM] * len(outs),
        out_shape=outs,
        scratch_shapes=list(scratch),
        compiler_params=pltpu.CompilerParams(vmem_limit_bytes=56 << 20),
    )


def rms_norm(values, gain):
    mean_square = jnp.mean(values * values, axis=-1, keepdims=True)
    return values * lax.rsqrt(mean_square + EPSILON) * gain


def dot(first, second):
    return jnp.dot(first, second, preferred_element_type=F32)


def dot_rows(first, second):
    return lax.dot_general(first, second, (((0,), (0,)), ((), ())), preferred_element_type=F32)


def dot_cols(first, second):
    return lax.dot_general(first, second, (((1,), (1,)), ((), ())), preferred_element_type=F32)


def of_head(h):
    return slice(h * DH, (h + 1) * DH)


def front_kernel(x_ref, gain_ref, wk_ref, wv_ref, normed_ref, k_ref, v_ref, state_ref, send_ref, wk, wv, sems):
    copy_k = pltpu.make_async_copy(wk_ref, wk, sems.at[0])
    copy_v = pltpu.make_async_copy(wv_ref, wv, sems.at[1])
    copy_k.start()
    copy_v.start()
    normed = rms_norm(x_ref[...].astype(F32), gain_ref[...]).astype(BF)
    normed_ref[...] = normed
    copy_k.wait()
    key = dot(normed, wk[...]).astype(BF)
    k_ref[...] = key
    copy_v.wait()
    value = dot(normed, wv[...]).astype(BF)
    v_ref[...] = value
    for h in range(HEADS):
        state = dot_rows(key[:, of_head(h)], value[:, of_head(h)])
        state_ref[h] = state
        send_ref[h] = state.astype(BF)


def local_kernel(normed_ref, wq_ref, k_ref, v_ref, q_ref, local_ref):
    query = dot(normed_ref[...], wq_ref[...]).astype(BF)
    q_ref[...] = query
    row = lax.broadcasted_iota(jnp.int32, (TOK, TOK), 0)
    causal = lax.broadcasted_iota(jnp.int32, (TOK, TOK), 1) <= row
    for h in range(HEADS):
        scores = dot_cols(query[:, of_head(h)], k_ref[:, of_head(h)])
        scores = jnp.where(causal, scores, 0.0).astype(BF)
        local_ref[:, of_head(h)] = dot(scores, v_ref[:, of_head(h)])


def attend_kernel(
    place_ref, prefix_ref, g1, g2, g3, q_ref, local_ref, gain_ref, w_ref,
    own_ref, s1, s2, s3, mixed_ref, turned_ref,
):
    y = place_ref[0]
    head = place_ref[1]
    for h in range(HEADS):
        earlier = prefix_ref[h]
        for k, got in ((1, g1), (2, g2), (3, g3)):
            earlier = earlier + jnp.where(y >= k, got[h].astype(F32), 0.0)
        high = earlier.astype(BF)
        low = (earlier - high.astype(F32)).astype(BF)
        query = q_ref[:, of_head(h)]
        attended = local_ref[:, of_head(h)] + (dot(query, high) + dot(query, low))
        mixed_ref[:, of_head(h)] = rms_norm(attended, gain_ref[:, of_head(h)]).astype(BF)
    for k in range(4):
        start = pl.multiple_of(((head - k) % 4) * ROWS, ROWS)
        turned_ref[k * ROWS:(k + 1) * ROWS, :] = mixed_ref[pl.ds(start, ROWS), :]
    for n in range(4):
        cols = slice(n * 512, (n + 1) * 512)
        rows = dot(turned_ref[...], w_ref[:, cols])
        own_ref[:, cols] = rows[:ROWS]
        s3[:, cols] = rows[ROWS:2 * ROWS].astype(BF)
        s2[:, cols] = rows[2 * ROWS:3 * ROWS].astype(BF)
        s1[:, cols] = rows[3 * ROWS:].astype(BF)


def dispatch_kernel(place_ref, t0, t1, t2, t3, out_ref, tokens):
    for k, ref in enumerate((t0, t1, t2, t3)):
        tokens[k * ROWS:(k + 1) * ROWS, :] = ref[...]
    tail = []
    for n in range(4):
        cols = slice(n * 512, (n + 1) * 512)
        rows = dot(place_ref[...], tokens[:, cols])
        out_ref[:, cols] = rows[:MAIN].astype(BF)
        tail.append(rows[MAIN:])
    tail = jnp.concatenate(tail, axis=1)
    for t in range(2):
        piece = tail[t * 32:(t + 1) * 32].reshape(MAIN, 128).astype(BF)
        out_ref[:, D + t * 128:D + (t + 1) * 128] = piece


def expert_kernel(x_ref, gu0, gu1, gu2, gu3, dn0, dn1, dn2, dn3, out_ref, rows, ends, gate_up, down, act, tail, sems):
    copies = [
        pltpu.make_async_copy(x_ref.at[:, :D], rows.at[:MAIN], sems.at[8]),
        pltpu.make_async_copy(x_ref.at[:, D:], ends, sems.at[9]),
    ]
    for q, (gu, dn) in enumerate(((gu0, dn0), (gu1, dn1), (gu2, dn2), (gu3, dn3))):
        copies.append(pltpu.make_async_copy(gu, gate_up.at[q], sems.at[q]))
        copies.append(pltpu.make_async_copy(dn, down.at[q * 256:(q + 1) * 256], sems.at[4 + q]))
    for copy in copies:
        copy.start()
    copies[1].wait()
    for t in range(2):
        piece = ends[:, t * 128:(t + 1) * 128].astype(F32).reshape(32, D)
        rows[MAIN + t * 32:MAIN + (t + 1) * 32, :] = piece.astype(BF)
    copies[0].wait()
    for q in range(4):
        copies[2 + 2 * q].wait()
        gate = dot(rows[...], gate_up[q, 0])
        up = dot(rows[...], gate_up[q, 1])
        act[:, q * 256:(q + 1) * 256] = (jax.nn.silu(gate) * up).astype(BF)
    for q in range(4):
        copies[3 + 2 * q].wait()
    for n in range(4):
        cols = slice(n * 512, (n + 1) * 512)
        result = dot(act[...], down[:, cols])
        out_ref[:, cols] = result[:MAIN].astype(BF)
        tail[:, cols] = result[MAIN:]
    for t in range(2):
        piece = tail[t * 32:(t + 1) * 32, :].reshape(MAIN, 128).astype(BF)
        out_ref[:, D + t * 128:D + (t + 1) * 128] = piece


def combine_kernel(weight_ref, y_ref, own_ref, s1, s2, s3, tail):
    for t in range(2):
        piece = y_ref[:, D + t * 128:D + (t + 1) * 128].astype(F32).reshape(32, D)
        tail[t * 32:(t + 1) * 32, :] = piece.astype(BF)
    for n in range(4):
        cols = slice(n * 512, (n + 1) * 512)
        rows = dot(weight_ref[:, :MAIN], y_ref[:, cols]) + dot(weight_ref[:, MAIN:], tail[:, cols])
        rows = rows[:TOK] + rows[TOK:]
        own_ref[:, cols] = rows[:ROWS]
        s3[:, cols] = rows[ROWS:2 * ROWS].astype(BF)
        s2[:, cols] = rows[2 * ROWS:3 * ROWS].astype(BF)
        s1[:, cols] = rows[3 * ROWS:].astype(BF)


BLOCKS_OUT = [out((ROWS, D), F32)] + [out((ROWS, D), BF)] * 3


def seq_perm(dy, dz, dc):
    return [
        ((y * 4 + z) * 2 + c, (((y + dy) % 4) * 4 + (z + dz) % 4) * 2 + (c ^ dc))
        for y in range(4)
        for z in range(4)
        for c in range(2)
    ]


def head_perm(shift):
    return [(h, (h + shift) % 4) for h in range(4)]


def device_perm(target):
    pairs = []
    for chip in range(16):
        for c in range(2):
            for h in range(4):
                to = target(c, h)
                pairs.append(((chip * 2 + c) * 4 + h, (chip * 2 + to[0]) * 4 + to[1]))
    return pairs


def near_target(c, h):
    chip = 2 * c + 1 - (h & 1)
    return (c, chip) if (chip - 1) % 4 == h else (1 - c, chip)


def far_target(c, h):
    return (c, h) if h // 2 == c else (1 - c, (h + 2) % 4)


def permute_all(arrays, axes, perm):
    return [lax.ppermute(a, axes, perm) for a in arrays]


def gather_weights(w_gate_up, w_down, head):
    odd = head & 1

    def pick(index):
        return [
            lax.dynamic_index_in_dim(w_gate_up, index, 0, False),
            lax.dynamic_index_in_dim(w_down, index, 0, False),
        ]

    both = ("seq", "head")
    swap = seq_perm(0, 0, 1)
    near = permute_all(pick(1 - odd), both, device_perm(near_target))
    far = permute_all(pick(odd), both, device_perm(far_target))
    near_other = permute_all(near, "seq", swap)
    far_other = permute_all(far, "seq", swap)
    return [near, near_other, far, far_other]


def exchange(array, step):
    dy, dz = step
    return [lax.ppermute(array, "seq", seq_perm(dy * k, dz * k, 0)) for k in range(1, 4)]


def gather_head(array):
    return [array] + [lax.ppermute(array, "head", head_perm(k)) for k in range(1, 4)]


def scatter_head(blocks):
    total = blocks[0]
    for k in range(1, 4):
        total = total + lax.ppermute(blocks[k], "head", head_perm(k)).astype(F32)
    return total


def on_device(
    hidden_in, attn_gain, w_qkv, out_gain, w_out, moe_gain, routes, gate_weights, w_gate_up, w_down
):
    seq = lax.axis_index("seq")
    head = lax.axis_index("head")
    core = seq % 2
    z = (seq // 2) % 4
    y = seq // 8

    pieces = gather_weights(w_gate_up, w_down, head)
    tables = gather_head(jnp.concatenate([routes.astype(F32), gate_weights], axis=1))
    tables = jnp.concatenate(tables, axis=0)

    normed, key, value, own_state, send_state = call(
        front_kernel,
        [VMEM, VMEM, ANY, ANY],
        [
            out((TOK, D), BF),
            out((TOK, WIDE), BF),
            out((TOK, WIDE), BF),
            out((HEADS, DH, DH), F32),
            out((HEADS, DH, DH), BF),
        ],
        [pltpu.VMEM((D, WIDE), BF), pltpu.VMEM((D, WIDE), BF), pltpu.SemaphoreType.DMA((2,))],
    )(hidden_in, attn_gain[None, :], w_qkv[:, 1], w_qkv[:, 2])
    sibling = lax.ppermute(send_state, "seq", seq_perm(0, 0, 1)).astype(F32)
    prefix = jnp.where(core == 1, sibling, 0.0)
    total = own_state + sibling
    rows_z = exchange(total.astype(BF), (0, 1))
    for k, got in enumerate(rows_z):
        prefix = prefix + jnp.where(z > k, got.astype(F32), 0.0)
        total = total + got.astype(F32)
    rows_y = exchange(total.astype(BF), (1, 0))

    query, local = call(
        local_kernel, [VMEM] * 4, [out((TOK, WIDE), BF), out((TOK, WIDE), F32)]
    )(normed, w_qkv[:, 0], key, value)
    place = jnp.stack([y, head]).astype(jnp.int32)
    blocks = call(
        attend_kernel,
        [SMEM] + [VMEM] * 8,
        BLOCKS_OUT,
        [pltpu.VMEM((TOK, WIDE), BF), pltpu.VMEM((TOK, WIDE), BF)],
    )(place, prefix, *rows_y, query, local, out_gain[None, :], w_out)
    attn_rows = scatter_head(blocks)
    resid = lax.dynamic_slice_in_dim(hidden_in, head * ROWS, ROWS, 0).astype(F32) + attn_rows
    normed2 = rms_norm(resid, moe_gain).astype(BF)
    tokens = gather_head(normed2)

    named = tables[:, :TOP].astype(jnp.int32)
    wanted = jnp.arange(16, dtype=jnp.int32) * 4 + head
    hit = named[:, :, None] == wanted[None, None, :]
    chosen = jnp.sum(hit.astype(F32), axis=1)
    gates = jnp.sum(jnp.where(hit, tables[:, TOP:, None], 0.0), axis=1)
    index = jnp.arange(TOK, dtype=jnp.int32)
    group = index // ROWS
    block = (head - group) % 4
    before = (group[:, None] == group[None, :]) & (index[None, :] < index[:, None])
    rank = dot(before.astype(BF), chosen.astype(BF)).astype(jnp.int32)
    slot = jnp.where(chosen > 0, (block // 2 * 18 + block % 2 * CAP)[:, None] + rank, -1).T
    gates = gates.T
    first = (jnp.arange(2, dtype=jnp.int32) * 18)[:, None] + jnp.arange(16, dtype=jnp.int32)
    last = jnp.arange(2, dtype=jnp.int32)[:, None] + jnp.array([16, 34], jnp.int32)
    main = slot[:, None, None, :] == first[None, :, :, None]
    ends = slot[None, :, None, :] == last[:, None, :, None]
    place_rows = jnp.concatenate([main.reshape(MAIN, TOK), ends.reshape(64, TOK)], axis=0)
    weight = jnp.concatenate(
        [
            jnp.where(main, gates[:, None, None, :], 0.0).reshape(MAIN, TOK),
            jnp.where(ends, gates[None, :, None, :], 0.0).reshape(64, TOK),
        ],
        axis=0,
    ).T
    high = weight.astype(BF)
    low = (weight - high.astype(F32)).astype(BF)
    weight = jnp.concatenate([high, low], axis=0)

    sent = call(
        dispatch_kernel, [VMEM] * 5, [out((MAIN, PACKED), BF)], [pltpu.VMEM((TOK, D), BF)]
    )(place_rows.astype(BF), *tokens)[0]
    received = lax.all_to_all(sent.reshape(32, 16, PACKED), "seq", 0, 0, tiled=True)
    results = call(
        expert_kernel,
        [ANY] * 9,
        [out((MAIN, PACKED), BF)],
        [
            pltpu.VMEM((SLOTS, D), BF),
            pltpu.VMEM((MAIN, 256), BF),
            pltpu.VMEM((4, 2, D, 256), BF),
            pltpu.VMEM((1024, D), BF),
            pltpu.VMEM((SLOTS, 1024), BF),
            pltpu.VMEM((64, D), F32),
            pltpu.SemaphoreType.DMA((10,)),
        ],
    )(received.reshape(MAIN, PACKED), *[p[0] for p in pieces], *[p[1] for p in pieces])[0]
    back = lax.all_to_all(results.reshape(32, 16, PACKED), "seq", 0, 0, tiled=True)
    blocks = call(
        combine_kernel, [VMEM] * 2, BLOCKS_OUT, [pltpu.VMEM((64, D), BF)]
    )(weight, back.reshape(MAIN, PACKED))
    moe_sum = scatter_head(blocks)
    return (resid + moe_sum).astype(BF)


def solution(mesh):
    placed = (
        P("seq", None),
        P(),
        P(None, None, "head"),
        P("head"),
        P("head", None),
        P(),
        P(("seq", "head"), None),
        P(("seq", "head"), None),
        P("seq", None, None, "head"),
        P("seq", "head", None),
    )

    return jax.shard_map(
        on_device, mesh=mesh, in_specs=placed, out_specs=P(("seq", "head"), None), check_vma=False
    )
```

```python
import jax
import jax.numpy as jnp
from jax import lax
from jax.experimental import pallas as pl
from jax.experimental.pallas import tpu as pltpu
from jax.sharding import PartitionSpec as P

D = 2048
DH = 128
HEADS = 4
WIDE = HEADS * DH
TOP = 8
CAP = 9
ROWS = 64
TOK = 256
MAIN = 512
SLOTS = 576
PACKED = D + 256
EPSILON = 1e-06
BF = jnp.bfloat16
F32 = jnp.float32


VMEM = pl.BlockSpec(memory_space=pltpu.VMEM)
SMEM = pl.BlockSpec(memory_space=pltpu.SMEM)
ANY = pl.BlockSpec(memory_space=pl.ANY)


def out(shape, dtype):
    return jax.ShapeDtypeStruct(shape, dtype)


def call(kernel, ins, outs, scratch=()):
    return pl.pallas_call(
        kernel,
        in_specs=ins,
        out_specs=[VMEM] * len(outs),
        out_shape=outs,
        scratch_shapes=list(scratch),
        compiler_params=pltpu.CompilerParams(vmem_limit_bytes=56 << 20),
    )


def rms_norm(values, gain):
    mean_square = jnp.mean(values * values, axis=-1, keepdims=True)
    return values * lax.rsqrt(mean_square + EPSILON) * gain


def dot(first, second):
    return jnp.dot(first, second, preferred_element_type=F32)


def dot_rows(first, second):
    return lax.dot_general(first, second, (((0,), (0,)), ((), ())), preferred_element_type=F32)


def dot_cols(first, second):
    return lax.dot_general(first, second, (((1,), (1,)), ((), ())), preferred_element_type=F32)


def of_head(h):
    return slice(h * DH, (h + 1) * DH)


def front_kernel(x_ref, gain_ref, wk_ref, wv_ref, normed_ref, k_ref, v_ref, state_ref, send_ref, wk, wv, sems):
    copy_k = pltpu.make_async_copy(wk_ref, wk, sems.at[0])
    copy_v = pltpu.make_async_copy(wv_ref, wv, sems.at[1])
    copy_k.start()
    copy_v.start()
    normed = rms_norm(x_ref[...].astype(F32), gain_ref[...]).astype(BF)
    normed_ref[...] = normed
    copy_k.wait()
    key = dot(normed, wk[...]).astype(BF)
    k_ref[...] = key
    copy_v.wait()
    value = dot(normed, wv[...]).astype(BF)
    v_ref[...] = value
    for h in range(HEADS):
        state = dot_rows(key[:, of_head(h)], value[:, of_head(h)])
        state_ref[h] = state
        send_ref[h] = state.astype(BF)


def local_kernel(normed_ref, wq_ref, k_ref, v_ref, q_ref, local_ref):
    query = dot(normed_ref[...], wq_ref[...]).astype(BF)
    q_ref[...] = query
    row = lax.broadcasted_iota(jnp.int32, (TOK, TOK), 0)
    causal = lax.broadcasted_iota(jnp.int32, (TOK, TOK), 1) <= row
    for h in range(HEADS):
        scores = dot_cols(query[:, of_head(h)], k_ref[:, of_head(h)])
        scores = jnp.where(causal, scores, 0.0).astype(BF)
        local_ref[:, of_head(h)] = dot(scores, v_ref[:, of_head(h)])


def attend_kernel(
    place_ref, prefix_ref, g1, g2, g3, q_ref, local_ref, gain_ref, w_ref,
    own_ref, s1, s2, s3, mixed_ref, turned_ref,
):
    y = place_ref[0]
    head = place_ref[1]
    for h in range(HEADS):
        earlier = prefix_ref[h]
        for k, got in ((1, g1), (2, g2), (3, g3)):
            earlier = earlier + jnp.where(y >= k, got[h].astype(F32), 0.0)
        high = earlier.astype(BF)
        low = (earlier - high.astype(F32)).astype(BF)
        query = q_ref[:, of_head(h)]
        attended = local_ref[:, of_head(h)] + (dot(query, high) + dot(query, low))
        mixed_ref[:, of_head(h)] = rms_norm(attended, gain_ref[:, of_head(h)]).astype(BF)
    for k in range(4):
        start = pl.multiple_of(((head - k) % 4) * ROWS, ROWS)
        turned_ref[k * ROWS:(k + 1) * ROWS, :] = mixed_ref[pl.ds(start, ROWS), :]
    for n in range(4):
        cols = slice(n * 512, (n + 1) * 512)
        rows = dot(turned_ref[...], w_ref[:, cols])
        own_ref[:, cols] = rows[:ROWS]
        s3[:, cols] = rows[ROWS:2 * ROWS].astype(BF)
        s2[:, cols] = rows[2 * ROWS:3 * ROWS].astype(BF)
        s1[:, cols] = rows[3 * ROWS:].astype(BF)


def dispatch_kernel(place_ref, t0, t1, t2, t3, out_ref, tokens):
    for k, ref in enumerate((t0, t1, t2, t3)):
        tokens[k * ROWS:(k + 1) * ROWS, :] = ref[...]
    tail = []
    for n in range(4):
        cols = slice(n * 512, (n + 1) * 512)
        rows = dot(place_ref[...], tokens[:, cols])
        out_ref[:, cols] = rows[:MAIN].astype(BF)
        tail.append(rows[MAIN:])
    tail = jnp.concatenate(tail, axis=1)
    for t in range(2):
        piece = tail[t * 32:(t + 1) * 32].reshape(MAIN, 128).astype(BF)
        out_ref[:, D + t * 128:D + (t + 1) * 128] = piece


def expert_kernel(
    keep_ref, x_ref, gu0, gu1, gu2, gu3, gu4, gu5, dn0, dn1, dn2, dn3, dn4, dn5,
    out_ref, rows, ends, gate_up, down, act, tail, sems,
):
    copies = [
        pltpu.make_async_copy(x_ref.at[:, :D], rows.at[:MAIN], sems.at[8]),
        pltpu.make_async_copy(x_ref.at[:, D:], ends, sems.at[9]),
    ]

    def load(q, gu, dn):
        return [
            pltpu.make_async_copy(gu, gate_up.at[q], sems.at[q]),
            pltpu.make_async_copy(dn, down.at[q * 256:(q + 1) * 256], sems.at[4 + q]),
        ]

    copies += load(0, gu0, dn0) + load(1, gu1, dn1)
    for copy in copies:
        copy.start()
    keep = keep_ref[0] == 1

    @pl.when(keep)
    def _():
        for copy in load(2, gu2, dn2) + load(3, gu5, dn5):
            copy.start()

    @pl.when(jnp.logical_not(keep))
    def _():
        for copy in load(2, gu3, dn3) + load(3, gu4, dn4):
            copy.start()

    copies += load(2, gu2, dn2) + load(3, gu4, dn4)
    copies[1].wait()
    for t in range(2):
        piece = ends[:, t * 128:(t + 1) * 128].astype(F32).reshape(32, D)
        rows[MAIN + t * 32:MAIN + (t + 1) * 32, :] = piece.astype(BF)
    copies[0].wait()
    for q in range(4):
        copies[2 + 2 * q].wait()
        gate = dot(rows[...], gate_up[q, 0])
        up = dot(rows[...], gate_up[q, 1])
        act[:, q * 256:(q + 1) * 256] = (jax.nn.silu(gate) * up).astype(BF)
    for q in range(4):
        copies[3 + 2 * q].wait()
    for n in range(4):
        cols = slice(n * 512, (n + 1) * 512)
        result = dot(act[...], down[:, cols])
        out_ref[:, cols] = result[:MAIN].astype(BF)
        tail[:, cols] = result[MAIN:]
    for t in range(2):
        piece = tail[t * 32:(t + 1) * 32, :].reshape(MAIN, 128).astype(BF)
        out_ref[:, D + t * 128:D + (t + 1) * 128] = piece


def combine_kernel(weight_ref, y_ref, own_ref, s1, s2, s3, tail):
    for t in range(2):
        piece = y_ref[:, D + t * 128:D + (t + 1) * 128].astype(F32).reshape(32, D)
        tail[t * 32:(t + 1) * 32, :] = piece.astype(BF)
    for n in range(4):
        cols = slice(n * 512, (n + 1) * 512)
        rows = dot(weight_ref[:, :MAIN], y_ref[:, cols]) + dot(weight_ref[:, MAIN:], tail[:, cols])
        rows = rows[:TOK] + rows[TOK:]
        own_ref[:, cols] = rows[:ROWS]
        s3[:, cols] = rows[ROWS:2 * ROWS].astype(BF)
        s2[:, cols] = rows[2 * ROWS:3 * ROWS].astype(BF)
        s1[:, cols] = rows[3 * ROWS:].astype(BF)


BLOCKS_OUT = [out((ROWS, D), F32)] + [out((ROWS, D), BF)] * 3


def seq_perm(dy, dz, dc):
    return [
        ((y * 4 + z) * 2 + c, (((y + dy) % 4) * 4 + (z + dz) % 4) * 2 + (c ^ dc))
        for y in range(4)
        for z in range(4)
        for c in range(2)
    ]


def head_perm(shift):
    return [(h, (h + shift) % 4) for h in range(4)]


def device_perm(target):
    pairs = []
    for chip in range(16):
        for c in range(2):
            for h in range(4):
                to = target(c, h)
                if to is None:
                    continue
                pairs.append(((chip * 2 + c) * 4 + h, (chip * 2 + to[0]) * 4 + to[1]))
    return pairs


def near_target(c, h):
    chip = 2 * c + 1 - (h & 1)
    return (c, chip) if (chip - 1) % 4 == h else (1 - c, chip)


def far_target(c, h):
    return None if h // 2 == c else (1 - c, (h + 2) % 4)


def keep_target(c, h):
    return (1 - c, h) if h // 2 == c else None


def pass_target(c, h):
    return None if h // 2 == c else (1 - c, h)


def permute_all(arrays, axes, perm):
    return [lax.ppermute(a, axes, perm) for a in arrays]


def gather_weights(w_gate_up, w_down, head):
    odd = head & 1

    def pick(index):
        return [
            lax.dynamic_index_in_dim(w_gate_up, index, 0, False),
            lax.dynamic_index_in_dim(w_down, index, 0, False),
        ]

    both = ("seq", "head")
    swap = seq_perm(0, 0, 1)
    near = permute_all(pick(1 - odd), both, device_perm(near_target))
    rest = pick(odd)
    far = permute_all(rest, both, device_perm(far_target))
    rest_other = permute_all(rest, both, device_perm(keep_target))
    near_other = permute_all(near, "seq", swap)
    far_other = permute_all(far, both, device_perm(pass_target))
    return [near, near_other, rest, rest_other, far, far_other]


def exchange(array, step):
    dy, dz = step
    return [lax.ppermute(array, "seq", seq_perm(dy * k, dz * k, 0)) for k in range(1, 4)]


def gather_head(array):
    return [array] + [lax.ppermute(array, "head", head_perm(k)) for k in range(1, 4)]


def scatter_head(blocks):
    total = blocks[0]
    for k in range(1, 4):
        total = total + lax.ppermute(blocks[k], "head", head_perm(k)).astype(F32)
    return total


def on_device(
    hidden_in, attn_gain, w_qkv, out_gain, w_out, moe_gain, routes, gate_weights, w_gate_up, w_down
):
    seq = lax.axis_index("seq")
    head = lax.axis_index("head")
    core = seq % 2
    z = (seq // 2) % 4
    y = seq // 8

    pieces = gather_weights(w_gate_up, w_down, head)
    tables = gather_head(jnp.concatenate([routes.astype(F32), gate_weights], axis=1))
    tables = jnp.concatenate(tables, axis=0)

    normed, key, value, own_state, send_state = call(
        front_kernel,
        [VMEM, VMEM, ANY, ANY],
        [
            out((TOK, D), BF),
            out((TOK, WIDE), BF),
            out((TOK, WIDE), BF),
            out((HEADS, DH, DH), F32),
            out((HEADS, DH, DH), BF),
        ],
        [pltpu.VMEM((D, WIDE), BF), pltpu.VMEM((D, WIDE), BF), pltpu.SemaphoreType.DMA((2,))],
    )(hidden_in, attn_gain[None, :], w_qkv[:, 1], w_qkv[:, 2])
    sibling = lax.ppermute(send_state, "seq", seq_perm(0, 0, 1)).astype(F32)
    prefix = jnp.where(core == 1, sibling, 0.0)
    total = own_state + sibling
    rows_z = exchange(total.astype(BF), (0, 1))
    for k, got in enumerate(rows_z):
        prefix = prefix + jnp.where(z > k, got.astype(F32), 0.0)
        total = total + got.astype(F32)
    rows_y = exchange(total.astype(BF), (1, 0))

    query, local = call(
        local_kernel, [VMEM] * 4, [out((TOK, WIDE), BF), out((TOK, WIDE), F32)]
    )(normed, w_qkv[:, 0], key, value)
    place = jnp.stack([y, head]).astype(jnp.int32)
    blocks = call(
        attend_kernel,
        [SMEM] + [VMEM] * 8,
        BLOCKS_OUT,
        [pltpu.VMEM((TOK, WIDE), BF), pltpu.VMEM((TOK, WIDE), BF)],
    )(place, prefix, *rows_y, query, local, out_gain[None, :], w_out)
    attn_rows = scatter_head(blocks)
    resid = lax.dynamic_slice_in_dim(hidden_in, head * ROWS, ROWS, 0).astype(F32) + attn_rows
    normed2 = rms_norm(resid, moe_gain).astype(BF)
    tokens = gather_head(normed2)

    named = tables[:, :TOP].astype(jnp.int32)
    wanted = jnp.arange(16, dtype=jnp.int32) * 4 + head
    hit = named[:, :, None] == wanted[None, None, :]
    chosen = jnp.sum(hit.astype(F32), axis=1)
    gates = jnp.sum(jnp.where(hit, tables[:, TOP:, None], 0.0), axis=1)
    index = jnp.arange(TOK, dtype=jnp.int32)
    group = index // ROWS
    block = (head - group) % 4
    before = (group[:, None] == group[None, :]) & (index[None, :] < index[:, None])
    rank = dot(before.astype(BF), chosen.astype(BF)).astype(jnp.int32)
    slot = jnp.where(chosen > 0, (block // 2 * 18 + block % 2 * CAP)[:, None] + rank, -1).T
    gates = gates.T
    first = (jnp.arange(2, dtype=jnp.int32) * 18)[:, None] + jnp.arange(16, dtype=jnp.int32)
    last = jnp.arange(2, dtype=jnp.int32)[:, None] + jnp.array([16, 34], jnp.int32)
    main = slot[:, None, None, :] == first[None, :, :, None]
    ends = slot[None, :, None, :] == last[:, None, :, None]
    place_rows = jnp.concatenate([main.reshape(MAIN, TOK), ends.reshape(64, TOK)], axis=0)
    weight = jnp.concatenate(
        [
            jnp.where(main, gates[:, None, None, :], 0.0).reshape(MAIN, TOK),
            jnp.where(ends, gates[None, :, None, :], 0.0).reshape(64, TOK),
        ],
        axis=0,
    ).T
    high = weight.astype(BF)
    low = (weight - high.astype(F32)).astype(BF)
    weight = jnp.concatenate([high, low], axis=0)

    sent = call(
        dispatch_kernel, [VMEM] * 5, [out((MAIN, PACKED), BF)], [pltpu.VMEM((TOK, D), BF)]
    )(place_rows.astype(BF), *tokens)[0]
    received = lax.all_to_all(sent.reshape(32, 16, PACKED), "seq", 0, 0, tiled=True)
    keep = (head // 2 == core).astype(jnp.int32)[None]
    results = call(
        expert_kernel,
        [SMEM] + [ANY] * 13,
        [out((MAIN, PACKED), BF)],
        [
            pltpu.VMEM((SLOTS, D), BF),
            pltpu.VMEM((MAIN, 256), BF),
            pltpu.VMEM((4, 2, D, 256), BF),
            pltpu.VMEM((1024, D), BF),
            pltpu.VMEM((SLOTS, 1024), BF),
            pltpu.VMEM((64, D), F32),
            pltpu.SemaphoreType.DMA((10,)),
        ],
    )(keep, received.reshape(MAIN, PACKED), *[p[0] for p in pieces], *[p[1] for p in pieces])[0]
    back = lax.all_to_all(results.reshape(32, 16, PACKED), "seq", 0, 0, tiled=True)
    blocks = call(
        combine_kernel, [VMEM] * 2, BLOCKS_OUT, [pltpu.VMEM((64, D), BF)]
    )(weight, back.reshape(MAIN, PACKED))
    moe_sum = scatter_head(blocks)
    return (resid + moe_sum).astype(BF)


def solution(mesh):
    placed = (
        P("seq", None),
        P(),
        P(None, None, "head"),
        P("head"),
        P("head", None),
        P(),
        P(("seq", "head"), None),
        P(("seq", "head"), None),
        P("seq", None, None, "head"),
        P("seq", "head", None),
    )

    return jax.shard_map(
        on_device, mesh=mesh, in_specs=placed, out_specs=P(("seq", "head"), None), check_vma=False
    )
```

```python
import jax
import jax.numpy as jnp
from jax import lax
from jax.experimental import pallas as pl
from jax.experimental.pallas import tpu as pltpu
from jax.sharding import PartitionSpec as P

D = 2048
DH = 128
HEADS = 4
WIDE = HEADS * DH
TOP = 8
CAP = 9
ROWS = 64
TOK = 256
MAIN = 512
SLOTS = 576
PACKED = D + 256
EPSILON = 1e-06
BF = jnp.bfloat16
F32 = jnp.float32


VMEM = pl.BlockSpec(memory_space=pltpu.VMEM)
SMEM = pl.BlockSpec(memory_space=pltpu.SMEM)
ANY = pl.BlockSpec(memory_space=pl.ANY)


def out(shape, dtype):
    return jax.ShapeDtypeStruct(shape, dtype)


def call(kernel, ins, outs, scratch=()):
    return pl.pallas_call(
        kernel,
        in_specs=ins,
        out_specs=[SMEM if o.dtype == jnp.int32 else VMEM for o in outs],
        out_shape=outs,
        scratch_shapes=list(scratch),
        compiler_params=pltpu.CompilerParams(vmem_limit_bytes=56 << 20),
    )


def rms_norm(values, gain):
    mean_square = jnp.mean(values * values, axis=-1, keepdims=True)
    return values * lax.rsqrt(mean_square + EPSILON) * gain


def dot(first, second):
    return jnp.dot(first, second, preferred_element_type=F32)


def dot_rows(first, second):
    return lax.dot_general(first, second, (((0,), (0,)), ((), ())), preferred_element_type=F32)


def dot_cols(first, second):
    return lax.dot_general(first, second, (((1,), (1,)), ((), ())), preferred_element_type=F32)


def of_head(h):
    return slice(h * DH, (h + 1) * DH)


def front_kernel(x_ref, gain_ref, wk_ref, wv_ref, normed_ref, k_ref, v_ref, state_ref, send_ref, zero_ref, wk, wv, sems):
    zero_ref[0] = 0
    copy_k = pltpu.make_async_copy(wk_ref, wk, sems.at[0])
    copy_v = pltpu.make_async_copy(wv_ref, wv, sems.at[1])
    copy_k.start()
    copy_v.start()
    normed = rms_norm(x_ref[...].astype(F32), gain_ref[...]).astype(BF)
    normed_ref[...] = normed
    copy_k.wait()
    key = dot(normed, wk[...]).astype(BF)
    k_ref[...] = key
    copy_v.wait()
    value = dot(normed, wv[...]).astype(BF)
    v_ref[...] = value
    for h in range(HEADS):
        state = dot_rows(key[:, of_head(h)], value[:, of_head(h)])
        state_ref[h] = state
        send_ref[h] = state.astype(BF)


def local_kernel(normed_ref, wq_ref, k_ref, v_ref, q_ref, local_ref):
    query = dot(normed_ref[...], wq_ref[...]).astype(BF)
    q_ref[...] = query
    row = lax.broadcasted_iota(jnp.int32, (TOK, TOK), 0)
    causal = lax.broadcasted_iota(jnp.int32, (TOK, TOK), 1) <= row
    for h in range(HEADS):
        scores = dot_cols(query[:, of_head(h)], k_ref[:, of_head(h)])
        scores = jnp.where(causal, scores, 0.0).astype(BF)
        local_ref[:, of_head(h)] = dot(scores, v_ref[:, of_head(h)])


def attend_kernel(
    place_ref, prefix_ref, g1, g2, g3, q_ref, local_ref, gain_ref, w_ref,
    own_ref, s1, s2, s3, mixed_ref, turned_ref,
):
    y = place_ref[0]
    head = place_ref[1]
    for h in range(HEADS):
        earlier = prefix_ref[h]
        for k, got in ((1, g1), (2, g2), (3, g3)):
            earlier = earlier + jnp.where(y >= k, got[h].astype(F32), 0.0)
        high = earlier.astype(BF)
        low = (earlier - high.astype(F32)).astype(BF)
        query = q_ref[:, of_head(h)]
        attended = local_ref[:, of_head(h)] + (dot(query, high) + dot(query, low))
        mixed_ref[:, of_head(h)] = rms_norm(attended, gain_ref[:, of_head(h)]).astype(BF)
    for k in range(4):
        start = pl.multiple_of(((head - k) % 4) * ROWS, ROWS)
        turned_ref[k * ROWS:(k + 1) * ROWS, :] = mixed_ref[pl.ds(start, ROWS), :]
    for n in range(4):
        cols = slice(n * 512, (n + 1) * 512)
        rows = dot(turned_ref[...], w_ref[:, cols])
        own_ref[:, cols] = rows[:ROWS]
        s3[:, cols] = rows[ROWS:2 * ROWS].astype(BF)
        s2[:, cols] = rows[2 * ROWS:3 * ROWS].astype(BF)
        s1[:, cols] = rows[3 * ROWS:].astype(BF)


def routing_kernel(head_ref, t0, t1, t2, t3, place_ref, weight_ref):
    head = head_ref[0]
    tables = jnp.concatenate([t0[...], t1[...], t2[...], t3[...]], axis=0)
    wanted = lax.broadcasted_iota(jnp.int32, (TOK, 16), 1) * 4 + head
    chosen = jnp.zeros((TOK, 16), F32)
    gates = jnp.zeros((TOK, 16), F32)
    for k in range(TOP):
        hit = tables[:, k:k + 1].astype(jnp.int32) == wanted
        chosen = chosen + hit.astype(F32)
        gates = gates + jnp.where(hit, tables[:, TOP + k:TOP + k + 1], 0.0)
    row = lax.broadcasted_iota(jnp.int32, (TOK, TOK), 0)
    col = lax.broadcasted_iota(jnp.int32, (TOK, TOK), 1)
    before = ((row // ROWS == col // ROWS) & (col < row)).astype(F32).astype(BF)
    rank = dot(before, chosen.astype(BF))
    block = (head - lax.broadcasted_iota(jnp.int32, (TOK, 16), 0) // ROWS) & 3
    base = ((block >> 1) * 18 + (block & 1) * CAP).astype(F32)
    slot = jnp.where(chosen > 0, base + rank, -1.0).astype(BF)
    high = gates.astype(BF)
    low = (gates - high.astype(F32)).astype(BF)

    def of_row(shape, axis):
        row = lax.broadcasted_iota(jnp.int32, shape, axis)
        is_main = row < MAIN
        chip = jnp.where(is_main, row >> 5, (row & 31) >> 1)
        core = jnp.where(is_main, (row >> 4) & 1, row & 1)
        within = jnp.where(is_main, row & 15, 16 + ((row - MAIN) >> 5))
        return chip, (core * 18 + within).astype(F32)

    chip, want = of_row((SLOTS, 16), 0)
    spread = (chip == lax.broadcasted_iota(jnp.int32, (SLOTS, 16), 1)).astype(F32).astype(BF)
    place_ref[...] = (dot_cols(spread, slot) == want[:, :1]).astype(F32).astype(BF)
    chip, want = of_row((16, SLOTS), 1)
    spread = (chip == lax.broadcasted_iota(jnp.int32, (16, SLOTS), 0)).astype(F32).astype(BF)
    at_row = dot(slot, spread) == want[:1, :]
    weight_ref[:TOK, :] = jnp.where(at_row, dot(high, spread), 0.0).astype(BF)
    weight_ref[TOK:, :] = jnp.where(at_row, dot(low, spread), 0.0).astype(BF)


def dispatch_kernel(place_ref, t0, t1, t2, t3, out_ref, tokens):
    for k, ref in enumerate((t0, t1, t2, t3)):
        tokens[k * ROWS:(k + 1) * ROWS, :] = ref[...]
    tail = []
    for n in range(4):
        cols = slice(n * 512, (n + 1) * 512)
        rows = dot(place_ref[...], tokens[:, cols])
        out_ref[:, cols] = rows[:MAIN].astype(BF)
        tail.append(rows[MAIN:])
    tail = jnp.concatenate(tail, axis=1)
    for t in range(2):
        piece = tail[t * 32:(t + 1) * 32].reshape(MAIN, 128).astype(BF)
        out_ref[:, D + t * 128:D + (t + 1) * 128] = piece


def expert_kernel(
    keep_ref, x_ref, gu0, gu1, gu2, gu3, gu4, gu5, dn0, dn1, dn2, dn3, dn4, dn5,
    out_ref, rows, ends, gate_up, down, act, tail, sems,
):
    copies = [
        pltpu.make_async_copy(x_ref.at[:, :D], rows.at[:MAIN], sems.at[8]),
        pltpu.make_async_copy(x_ref.at[:, D:], ends, sems.at[9]),
    ]

    def load(q, gu, dn):
        return [
            pltpu.make_async_copy(gu, gate_up.at[q], sems.at[q]),
            pltpu.make_async_copy(dn, down.at[q * 256:(q + 1) * 256], sems.at[4 + q]),
        ]

    copies += load(0, gu0, dn0) + load(1, gu1, dn1)
    for copy in copies:
        copy.start()
    keep = keep_ref[0] == 1

    @pl.when(keep)
    def _():
        for copy in load(2, gu2, dn2) + load(3, gu5, dn5):
            copy.start()

    @pl.when(jnp.logical_not(keep))
    def _():
        for copy in load(2, gu3, dn3) + load(3, gu4, dn4):
            copy.start()

    copies += load(2, gu2, dn2) + load(3, gu4, dn4)
    copies[1].wait()
    for t in range(2):
        piece = ends[:, t * 128:(t + 1) * 128].astype(F32).reshape(32, D)
        rows[MAIN + t * 32:MAIN + (t + 1) * 32, :] = piece.astype(BF)
    copies[0].wait()
    for q in range(4):
        copies[2 + 2 * q].wait()
        gate = dot(rows[...], gate_up[q, 0])
        up = dot(rows[...], gate_up[q, 1])
        act[:, q * 256:(q + 1) * 256] = (jax.nn.silu(gate) * up).astype(BF)
    for q in range(4):
        copies[3 + 2 * q].wait()
    for n in range(4):
        cols = slice(n * 512, (n + 1) * 512)
        result = dot(act[...], down[:, cols])
        out_ref[:, cols] = result[:MAIN].astype(BF)
        tail[:, cols] = result[MAIN:]
    for t in range(2):
        piece = tail[t * 32:(t + 1) * 32, :].reshape(MAIN, 128).astype(BF)
        out_ref[:, D + t * 128:D + (t + 1) * 128] = piece


def combine_kernel(weight_ref, y_ref, own_ref, s1, s2, s3, tail):
    for t in range(2):
        piece = y_ref[:, D + t * 128:D + (t + 1) * 128].astype(F32).reshape(32, D)
        tail[t * 32:(t + 1) * 32, :] = piece.astype(BF)
    for n in range(4):
        cols = slice(n * 512, (n + 1) * 512)
        rows = dot(weight_ref[:, :MAIN], y_ref[:, cols]) + dot(weight_ref[:, MAIN:], tail[:, cols])
        rows = rows[:TOK] + rows[TOK:]
        own_ref[:, cols] = rows[:ROWS]
        s3[:, cols] = rows[ROWS:2 * ROWS].astype(BF)
        s2[:, cols] = rows[2 * ROWS:3 * ROWS].astype(BF)
        s1[:, cols] = rows[3 * ROWS:].astype(BF)


BLOCKS_OUT = [out((ROWS, D), F32)] + [out((ROWS, D), BF)] * 3


def seq_perm(dy, dz, dc):
    return [
        ((y * 4 + z) * 2 + c, (((y + dy) % 4) * 4 + (z + dz) % 4) * 2 + (c ^ dc))
        for y in range(4)
        for z in range(4)
        for c in range(2)
    ]


def head_perm(shift):
    return [(h, (h + shift) % 4) for h in range(4)]


def device_perm(target):
    pairs = []
    for chip in range(16):
        for c in range(2):
            for h in range(4):
                to = target(c, h)
                if to is None:
                    continue
                pairs.append(((chip * 2 + c) * 4 + h, (chip * 2 + to[0]) * 4 + to[1]))
    return pairs


def near_target(c, h):
    chip = 2 * c + 1 - (h & 1)
    return (c, chip) if (chip - 1) % 4 == h else (1 - c, chip)


def far_target(c, h):
    return None if h // 2 == c else (1 - c, (h + 2) % 4)


def keep_target(c, h):
    return (1 - c, h) if h // 2 == c else None


def pass_target(c, h):
    return None if h // 2 == c else (1 - c, h)


def permute_all(arrays, axes, perm):
    return [lax.ppermute(a, axes, perm) for a in arrays]


def pick_kernel(index_ref, gu_ref, dn_ref, gu_out, dn_out, sems):
    index = index_ref[0]
    copies = []
    for half in range(2):
        for part in range(2):
            rows = pl.ds(part * (D // 2), D // 2)
            copies.append((gu_ref.at[index, half, rows], gu_out.at[half, rows]))
        rows = pl.ds(half * 128, 128)
        copies.append((dn_ref.at[index, rows], dn_out.at[rows]))
    copies = [pltpu.make_async_copy(a, b, sems.at[i]) for i, (a, b) in enumerate(copies)]
    for copy in copies:
        copy.start()
    for copy in copies:
        copy.wait()


def pick(w_gate_up, w_down, index):
    return pl.pallas_call(
        pick_kernel,
        in_specs=[SMEM, ANY, ANY],
        out_specs=[VMEM, VMEM],
        out_shape=[out((2, D, 256), BF), out((256, D), BF)],
        scratch_shapes=[pltpu.SemaphoreType.DMA((6,))],
        name="pick",
    )(index.astype(jnp.int32)[None], w_gate_up, w_down)


def exchange(array, step):
    dy, dz = step
    return [lax.ppermute(array, "seq", seq_perm(dy * k, dz * k, 0)) for k in range(1, 4)]


def gather_head(array):
    return [array] + [lax.ppermute(array, "head", head_perm(k)) for k in range(1, 4)]


def scatter_head(blocks):
    total = blocks[0]
    for k in range(1, 4):
        total = total + lax.ppermute(blocks[k], "head", head_perm(k)).astype(F32)
    return total


def on_device(
    hidden_in, attn_gain, w_qkv, out_gain, w_out, moe_gain, routes, gate_weights, w_gate_up, w_down
):
    seq = lax.axis_index("seq")
    head = lax.axis_index("head")
    core = seq % 2
    z = (seq // 2) % 4
    y = seq // 8

    both = ("seq", "head")
    near = permute_all(pick(w_gate_up, w_down, 1 - (head & 1)), both, device_perm(near_target))
    tables = gather_head(jnp.concatenate([routes.astype(F32), gate_weights], axis=1))
    place_rows, weight = call(
        routing_kernel, [SMEM] + [VMEM] * 4, [out((SLOTS, TOK), BF), out((2 * TOK, SLOTS), BF)]
    )(head.astype(jnp.int32)[None], *tables)

    normed, key, value, own_state, send_state, zero = call(
        front_kernel,
        [VMEM, VMEM, ANY, ANY],
        [
            out((TOK, D), BF),
            out((TOK, WIDE), BF),
            out((TOK, WIDE), BF),
            out((HEADS, DH, DH), F32),
            out((HEADS, DH, DH), BF),
            out((1,), jnp.int32),
        ],
        [pltpu.VMEM((D, WIDE), BF), pltpu.VMEM((D, WIDE), BF), pltpu.SemaphoreType.DMA((2,))],
    )(hidden_in, attn_gain[None, :], w_qkv[:, 1], w_qkv[:, 2])
    sibling = lax.ppermute(send_state, "seq", seq_perm(0, 0, 1)).astype(F32)
    odd = (head & 1) + zero[0]
    rest = pick(w_gate_up, w_down, odd)
    far = permute_all(rest, both, device_perm(far_target))
    rest_other = permute_all(rest, both, device_perm(keep_target))
    near_other = permute_all(near, "seq", seq_perm(0, 0, 1))
    far_other = permute_all(far, both, device_perm(pass_target))
    pieces = [near, near_other, rest, rest_other, far, far_other]
    prefix = jnp.where(core == 1, sibling, 0.0)
    total = own_state + sibling
    rows_z = exchange(total.astype(BF), (0, 1))
    for k, got in enumerate(rows_z):
        prefix = prefix + jnp.where(z > k, got.astype(F32), 0.0)
        total = total + got.astype(F32)
    rows_y = exchange(total.astype(BF), (1, 0))

    query, local = call(
        local_kernel, [VMEM] * 4, [out((TOK, WIDE), BF), out((TOK, WIDE), F32)]
    )(normed, w_qkv[:, 0], key, value)
    place = jnp.stack([y, head]).astype(jnp.int32)
    blocks = call(
        attend_kernel,
        [SMEM] + [VMEM] * 8,
        BLOCKS_OUT,
        [pltpu.VMEM((TOK, WIDE), BF), pltpu.VMEM((TOK, WIDE), BF)],
    )(place, prefix, *rows_y, query, local, out_gain[None, :], w_out)
    attn_rows = scatter_head(blocks)
    resid = lax.dynamic_slice_in_dim(hidden_in, head * ROWS, ROWS, 0).astype(F32) + attn_rows
    normed2 = rms_norm(resid, moe_gain).astype(BF)
    tokens = gather_head(normed2)

    sent = call(
        dispatch_kernel, [VMEM] * 5, [out((MAIN, PACKED), BF)], [pltpu.VMEM((TOK, D), BF)]
    )(place_rows, *tokens)[0]
    received = lax.all_to_all(sent.reshape(32, 16, PACKED), "seq", 0, 0, tiled=True)
    keep = (head // 2 == core).astype(jnp.int32)[None]
    results = call(
        expert_kernel,
        [SMEM] + [ANY] * 13,
        [out((MAIN, PACKED), BF)],
        [
            pltpu.VMEM((SLOTS, D), BF),
            pltpu.VMEM((MAIN, 256), BF),
            pltpu.VMEM((4, 2, D, 256), BF),
            pltpu.VMEM((1024, D), BF),
            pltpu.VMEM((SLOTS, 1024), BF),
            pltpu.VMEM((64, D), F32),
            pltpu.SemaphoreType.DMA((10,)),
        ],
    )(keep, received.reshape(MAIN, PACKED), *[p[0] for p in pieces], *[p[1] for p in pieces])[0]
    back = lax.all_to_all(results.reshape(32, 16, PACKED), "seq", 0, 0, tiled=True)
    blocks = call(
        combine_kernel, [VMEM] * 2, BLOCKS_OUT, [pltpu.VMEM((64, D), BF)]
    )(weight, back.reshape(MAIN, PACKED))
    moe_sum = scatter_head(blocks)
    return (resid + moe_sum).astype(BF)


def solution(mesh):
    placed = (
        P("seq", None),
        P(),
        P(None, None, "head"),
        P("head"),
        P("head", None),
        P(),
        P(("seq", "head"), None),
        P(("seq", "head"), None),
        P("seq", None, None, "head"),
        P("seq", "head", None),
    )

    return jax.shard_map(
        on_device, mesh=mesh, in_specs=placed, out_specs=P(("seq", "head"), None), check_vma=False
    )
```

```python
import jax
import jax.numpy as jnp
from jax import lax
from jax.experimental import pallas as pl
from jax.experimental.pallas import tpu as pltpu
from jax.sharding import PartitionSpec as P

D = 2048
DH = 128
HEADS = 4
WIDE = HEADS * DH
TOP = 8
CAP = 9
ROWS = 64
TOK = 256
MAIN = 512
SLOTS = 576
PACKED = D + 256
EPSILON = 1e-06
BF = jnp.bfloat16
F32 = jnp.float32


VMEM = pl.BlockSpec(memory_space=pltpu.VMEM)
SMEM = pl.BlockSpec(memory_space=pltpu.SMEM)
ANY = pl.BlockSpec(memory_space=pl.ANY)
HBM = pl.BlockSpec(memory_space=pltpu.HBM)


def out(shape, dtype):
    return jax.ShapeDtypeStruct(shape, dtype)


def call(kernel, ins, outs, scratch=()):
    return pl.pallas_call(
        kernel,
        in_specs=ins,
        out_specs=[SMEM if o.dtype == jnp.int32 else VMEM for o in outs],
        out_shape=outs,
        scratch_shapes=list(scratch),
        compiler_params=pltpu.CompilerParams(vmem_limit_bytes=56 << 20),
    )


def rms_norm(values, gain):
    mean_square = jnp.mean(values * values, axis=-1, keepdims=True)
    return values * lax.rsqrt(mean_square + EPSILON) * gain


def dot(first, second):
    return jnp.dot(first, second, preferred_element_type=F32)


def dot_rows(first, second):
    return lax.dot_general(first, second, (((0,), (0,)), ((), ())), preferred_element_type=F32)


def dot_cols(first, second):
    return lax.dot_general(first, second, (((1,), (1,)), ((), ())), preferred_element_type=F32)


def of_head(h):
    return slice(h * DH, (h + 1) * DH)


def front_kernel(x_ref, gain_ref, wk_ref, wv_ref, normed_ref, k_ref, v_ref, state_ref, send_ref, zero_ref, wk, wv, sems):
    zero_ref[0] = 0
    copy_k = pltpu.make_async_copy(wk_ref, wk, sems.at[0])
    copy_v = pltpu.make_async_copy(wv_ref, wv, sems.at[1])
    copy_k.start()
    copy_v.start()
    normed = rms_norm(x_ref[...].astype(F32), gain_ref[...]).astype(BF)
    normed_ref[...] = normed
    copy_k.wait()
    key = dot(normed, wk[...]).astype(BF)
    k_ref[...] = key
    copy_v.wait()
    value = dot(normed, wv[...]).astype(BF)
    v_ref[...] = value
    for h in range(HEADS):
        state = dot_rows(key[:, of_head(h)], value[:, of_head(h)])
        state_ref[h] = state
        send_ref[h] = state.astype(BF)


def local_kernel(normed_ref, upper_ref, lower_ref, k_ref, v_ref, q_ref, local_ref):
    query = dot(normed_ref[:, :D // 2], upper_ref[...]) + dot(normed_ref[:, D // 2:], lower_ref[...])
    query = query.astype(BF)
    q_ref[...] = query
    row = lax.broadcasted_iota(jnp.int32, (TOK, TOK), 0)
    causal = lax.broadcasted_iota(jnp.int32, (TOK, TOK), 1) <= row
    for h in range(HEADS):
        scores = dot_cols(query[:, of_head(h)], k_ref[:, of_head(h)])
        scores = jnp.where(causal, scores, 0.0).astype(BF)
        local_ref[:, of_head(h)] = dot(scores, v_ref[:, of_head(h)])


def attend_kernel(
    place_ref, prefix_ref, g1, g2, g3, q_ref, local_ref, gain_ref, w_ref,
    own_ref, s1, s2, s3, mixed_ref, turned_ref,
):
    y = place_ref[0]
    head = place_ref[1]
    for h in range(HEADS):
        earlier = prefix_ref[h]
        for k, got in ((1, g1), (2, g2), (3, g3)):
            earlier = earlier + jnp.where(y >= k, got[h].astype(F32), 0.0)
        high = earlier.astype(BF)
        low = (earlier - high.astype(F32)).astype(BF)
        query = q_ref[:, of_head(h)]
        attended = local_ref[:, of_head(h)] + (dot(query, high) + dot(query, low))
        mixed_ref[:, of_head(h)] = rms_norm(attended, gain_ref[:, of_head(h)]).astype(BF)
    for k in range(4):
        start = pl.multiple_of(((head - k) % 4) * ROWS, ROWS)
        turned_ref[k * ROWS:(k + 1) * ROWS, :] = mixed_ref[pl.ds(start, ROWS), :]
    for n in range(4):
        cols = slice(n * 512, (n + 1) * 512)
        rows = dot(turned_ref[...], w_ref[:, cols])
        own_ref[:, cols] = rows[:ROWS]
        s3[:, cols] = rows[ROWS:2 * ROWS].astype(BF)
        s2[:, cols] = rows[2 * ROWS:3 * ROWS].astype(BF)
        s1[:, cols] = rows[3 * ROWS:].astype(BF)


def routing_kernel(head_ref, t0, t1, t2, t3, place_ref, weight_ref):
    head = head_ref[0]
    tables = jnp.concatenate([t0[...], t1[...], t2[...], t3[...]], axis=0)
    wanted = lax.broadcasted_iota(jnp.int32, (TOK, 16), 1) * 4 + head
    chosen = jnp.zeros((TOK, 16), F32)
    gates = jnp.zeros((TOK, 16), F32)
    for k in range(TOP):
        hit = tables[:, k:k + 1].astype(jnp.int32) == wanted
        chosen = chosen + hit.astype(F32)
        gates = gates + jnp.where(hit, tables[:, TOP + k:TOP + k + 1], 0.0)
    row = lax.broadcasted_iota(jnp.int32, (TOK, TOK), 0)
    col = lax.broadcasted_iota(jnp.int32, (TOK, TOK), 1)
    before = ((row // ROWS == col // ROWS) & (col < row)).astype(F32).astype(BF)
    rank = dot(before, chosen.astype(BF))
    block = (head - lax.broadcasted_iota(jnp.int32, (TOK, 16), 0) // ROWS) & 3
    base = ((block >> 1) * 18 + (block & 1) * CAP).astype(F32)
    slot = jnp.where(chosen > 0, base + rank, -1.0).astype(BF)
    high = gates.astype(BF)
    low = (gates - high.astype(F32)).astype(BF)

    def of_row(shape, axis):
        row = lax.broadcasted_iota(jnp.int32, shape, axis)
        is_main = row < MAIN
        chip = jnp.where(is_main, row >> 5, (row & 31) >> 1)
        core = jnp.where(is_main, (row >> 4) & 1, row & 1)
        within = jnp.where(is_main, row & 15, 16 + ((row - MAIN) >> 5))
        return chip, (core * 18 + within).astype(F32)

    chip, want = of_row((SLOTS, 16), 0)
    spread = (chip == lax.broadcasted_iota(jnp.int32, (SLOTS, 16), 1)).astype(F32).astype(BF)
    place_ref[...] = (dot_cols(spread, slot) == want[:, :1]).astype(F32).astype(BF)
    chip, want = of_row((16, SLOTS), 1)
    spread = (chip == lax.broadcasted_iota(jnp.int32, (16, SLOTS), 0)).astype(F32).astype(BF)
    at_row = dot(slot, spread) == want[:1, :]
    weight_ref[:TOK, :] = jnp.where(at_row, dot(high, spread), 0.0).astype(BF)
    weight_ref[TOK:, :] = jnp.where(at_row, dot(low, spread), 0.0).astype(BF)


def dispatch_kernel(place_ref, t0, t1, t2, t3, out_ref, tokens):
    for k, ref in enumerate((t0, t1, t2, t3)):
        tokens[k * ROWS:(k + 1) * ROWS, :] = ref[...]
    tail = []
    for n in range(4):
        cols = slice(n * 512, (n + 1) * 512)
        rows = dot(place_ref[...], tokens[:, cols])
        out_ref[:, cols] = rows[:MAIN].astype(BF)
        tail.append(rows[MAIN:])
    tail = jnp.concatenate(tail, axis=1)
    for t in range(2):
        piece = tail[t * 32:(t + 1) * 32].reshape(MAIN, 128).astype(BF)
        out_ref[:, D + t * 128:D + (t + 1) * 128] = piece


def expert_kernel(
    keep_ref, x_ref, gu0, gu1, gu2, gu3, gu4, gu5, dn0, dn1, dn2, dn3, dn4, dn5,
    out_ref, rows, ends, gate_up, down, act, tail, sems,
):
    copies = [
        pltpu.make_async_copy(x_ref.at[:, :D], rows.at[:MAIN], sems.at[8]),
        pltpu.make_async_copy(x_ref.at[:, D:], ends, sems.at[9]),
    ]

    def load(q, gu, dn):
        return [
            pltpu.make_async_copy(gu, gate_up.at[q], sems.at[q]),
            pltpu.make_async_copy(dn, down.at[q * 256:(q + 1) * 256], sems.at[4 + q]),
        ]

    copies += load(0, gu0, dn0) + load(1, gu1, dn1)
    for copy in copies:
        copy.start()
    keep = keep_ref[0] == 1

    @pl.when(keep)
    def _():
        for copy in load(2, gu2, dn2) + load(3, gu5, dn5):
            copy.start()

    @pl.when(jnp.logical_not(keep))
    def _():
        for copy in load(2, gu3, dn3) + load(3, gu4, dn4):
            copy.start()

    copies += load(2, gu2, dn2) + load(3, gu4, dn4)
    copies[1].wait()
    for t in range(2):
        piece = ends[:, t * 128:(t + 1) * 128].astype(F32).reshape(32, D)
        rows[MAIN + t * 32:MAIN + (t + 1) * 32, :] = piece.astype(BF)
    copies[0].wait()
    for q in range(4):
        copies[2 + 2 * q].wait()
        gate = dot(rows[...], gate_up[q, 0])
        up = dot(rows[...], gate_up[q, 1])
        act[:, q * 256:(q + 1) * 256] = (jax.nn.silu(gate) * up).astype(BF)
    for q in range(4):
        copies[3 + 2 * q].wait()
    for n in range(4):
        cols = slice(n * 512, (n + 1) * 512)
        result = dot(act[...], down[:, cols])
        out_ref[:, cols] = result[:MAIN].astype(BF)
        tail[:, cols] = result[MAIN:]
    for t in range(2):
        piece = tail[t * 32:(t + 1) * 32, :].reshape(MAIN, 128).astype(BF)
        out_ref[:, D + t * 128:D + (t + 1) * 128] = piece


def combine_kernel(weight_ref, y_ref, own_ref, s1, s2, s3, tail):
    for t in range(2):
        piece = y_ref[:, D + t * 128:D + (t + 1) * 128].astype(F32).reshape(32, D)
        tail[t * 32:(t + 1) * 32, :] = piece.astype(BF)
    for n in range(4):
        cols = slice(n * 512, (n + 1) * 512)
        rows = dot(weight_ref[:, :MAIN], y_ref[:, cols]) + dot(weight_ref[:, MAIN:], tail[:, cols])
        rows = rows[:TOK] + rows[TOK:]
        own_ref[:, cols] = rows[:ROWS]
        s3[:, cols] = rows[ROWS:2 * ROWS].astype(BF)
        s2[:, cols] = rows[2 * ROWS:3 * ROWS].astype(BF)
        s1[:, cols] = rows[3 * ROWS:].astype(BF)


BLOCKS_OUT = [out((ROWS, D), F32)] + [out((ROWS, D), BF)] * 3


def seq_perm(dy, dz, dc):
    return [
        ((y * 4 + z) * 2 + c, (((y + dy) % 4) * 4 + (z + dz) % 4) * 2 + (c ^ dc))
        for y in range(4)
        for z in range(4)
        for c in range(2)
    ]


def head_perm(shift):
    return [(h, (h + shift) % 4) for h in range(4)]


def device_perm(target):
    pairs = []
    for chip in range(16):
        for c in range(2):
            for h in range(4):
                to = target(c, h)
                if to is None:
                    continue
                pairs.append(((chip * 2 + c) * 4 + h, (chip * 2 + to[0]) * 4 + to[1]))
    return pairs


def near_target(c, h):
    chip = 2 * c + 1 - (h & 1)
    return (c, chip) if (chip - 1) % 4 == h else (1 - c, chip)


def far_target(c, h):
    return None if h // 2 == c else (1 - c, (h + 2) % 4)


def keep_target(c, h):
    return (1 - c, h) if h // 2 == c else None


def pass_target(c, h):
    return None if h // 2 == c else (1 - c, h)


def permute_all(arrays, axes, perm):
    return [lax.ppermute(a, axes, perm) for a in arrays]


def pick_kernel(index_ref, gu_ref, dn_ref, gu_out, dn_out, sems):
    index = index_ref[0]
    copies = []
    for half in range(2):
        for part in range(2):
            rows = pl.ds(part * (D // 2), D // 2)
            copies.append((gu_ref.at[index, half, rows], gu_out.at[half, rows]))
        rows = pl.ds(half * 128, 128)
        copies.append((dn_ref.at[index, rows], dn_out.at[rows]))
    copies = [pltpu.make_async_copy(a, b, sems.at[i]) for i, (a, b) in enumerate(copies)]
    for copy in copies:
        copy.start()
    for copy in copies:
        copy.wait()


def pick(w_gate_up, w_down, index):
    return pl.pallas_call(
        pick_kernel,
        in_specs=[SMEM, ANY, ANY],
        out_specs=[VMEM, VMEM],
        out_shape=[out((2, D, 256), BF), out((256, D), BF)],
        scratch_shapes=[pltpu.SemaphoreType.DMA((6,))],
        name="pick",
    )(index.astype(jnp.int32)[None], w_gate_up, w_down)


def exchange(array, step):
    dy, dz = step
    return [lax.ppermute(array, "seq", seq_perm(dy * k, dz * k, 0)) for k in range(1, 4)]


def gather_head(array):
    return [array] + [lax.ppermute(array, "head", head_perm(k)) for k in range(1, 4)]


def scatter_head(blocks):
    total = blocks[0]
    for k in range(1, 4):
        total = total + lax.ppermute(blocks[k], "head", head_perm(k)).astype(F32)
    return total


def on_device(
    hidden_in, attn_gain, w_qkv, out_gain, w_out, moe_gain, routes, gate_weights, w_gate_up, w_down
):
    seq = lax.axis_index("seq")
    head = lax.axis_index("head")
    core = seq % 2
    z = (seq // 2) % 4
    y = seq // 8

    both = ("seq", "head")
    near = permute_all(pick(w_gate_up, w_down, 1 - (head & 1)), both, device_perm(near_target))
    tables = gather_head(jnp.concatenate([routes.astype(F32), gate_weights], axis=1))
    place_rows, weight = call(
        routing_kernel, [SMEM] + [VMEM] * 4, [out((SLOTS, TOK), BF), out((2 * TOK, SLOTS), BF)]
    )(head.astype(jnp.int32)[None], *tables)

    normed, key, value, own_state, send_state, zero = call(
        front_kernel,
        [VMEM, VMEM, ANY, ANY],
        [
            out((TOK, D), BF),
            out((TOK, WIDE), BF),
            out((TOK, WIDE), BF),
            out((HEADS, DH, DH), F32),
            out((HEADS, DH, DH), BF),
            out((1,), jnp.int32),
        ],
        [pltpu.VMEM((D, WIDE), BF), pltpu.VMEM((D, WIDE), BF), pltpu.SemaphoreType.DMA((2,))],
    )(hidden_in, attn_gain[None, :], w_qkv[:, 1], w_qkv[:, 2])
    sibling = lax.ppermute(send_state, "seq", seq_perm(0, 0, 1)).astype(F32)
    odd = (head & 1) + zero[0]
    rest = pick(w_gate_up, w_down, odd)
    far_down = lax.ppermute(rest[1], both, device_perm(far_target))
    far = [lax.ppermute(rest[0], both, device_perm(far_target)), far_down]
    rest_other = permute_all(rest, both, device_perm(keep_target))
    near_other = permute_all(near, "seq", seq_perm(0, 0, 1))
    far_other = permute_all(far, both, device_perm(pass_target))
    pieces = [near, near_other, rest, rest_other, far, far_other]
    prefix = jnp.where(core == 1, sibling, 0.0)
    total = own_state + sibling
    rows_z = exchange(total.astype(BF), (0, 1))
    for k, got in enumerate(rows_z):
        prefix = prefix + jnp.where(z > k, got.astype(F32), 0.0)
        total = total + got.astype(F32)
    rows_y = exchange(total.astype(BF), (1, 0))

    w_query = [
        lax.dynamic_slice_in_dim(w_qkv, zero[0] + start, D // 2, 0)[:, 0] for start in (0, D // 2)
    ]
    query, local = call(
        local_kernel, [VMEM] * 5, [out((TOK, WIDE), BF), out((TOK, WIDE), F32)]
    )(normed, *w_query, key, value)
    place = jnp.stack([y, head]).astype(jnp.int32)
    blocks = call(
        attend_kernel,
        [SMEM] + [VMEM] * 8,
        BLOCKS_OUT,
        [pltpu.VMEM((TOK, WIDE), BF), pltpu.VMEM((TOK, WIDE), BF)],
    )(place, prefix, *rows_y, query, local, out_gain[None, :], w_out)
    attn_rows = scatter_head(blocks)
    resid = lax.dynamic_slice_in_dim(hidden_in, head * ROWS, ROWS, 0).astype(F32) + attn_rows
    normed2 = rms_norm(resid, moe_gain).astype(BF)
    tokens = gather_head(normed2)

    sent = call(
        dispatch_kernel, [VMEM] * 5, [out((MAIN, PACKED), BF)], [pltpu.VMEM((TOK, D), BF)]
    )(place_rows, *tokens)[0]
    received = lax.all_to_all(sent.reshape(32, 16, PACKED), "seq", 0, 0, tiled=True)
    keep = (head // 2 == core).astype(jnp.int32)[None]
    results = call(
        expert_kernel,
        [SMEM, HBM] + [ANY] * 12,
        [out((MAIN, PACKED), BF)],
        [
            pltpu.VMEM((SLOTS, D), BF),
            pltpu.VMEM((MAIN, 256), BF),
            pltpu.VMEM((4, 2, D, 256), BF),
            pltpu.VMEM((1024, D), BF),
            pltpu.VMEM((SLOTS, 1024), BF),
            pltpu.VMEM((64, D), F32),
            pltpu.SemaphoreType.DMA((10,)),
        ],
    )(keep, received.reshape(MAIN, PACKED), *[p[0] for p in pieces], *[p[1] for p in pieces])[0]
    back = lax.all_to_all(results.reshape(32, 16, PACKED), "seq", 0, 0, tiled=True)
    blocks = call(
        combine_kernel, [VMEM] * 2, BLOCKS_OUT, [pltpu.VMEM((64, D), BF)]
    )(weight, back.reshape(MAIN, PACKED))
    moe_sum = scatter_head(blocks)
    return (resid + moe_sum).astype(BF)


def solution(mesh):
    placed = (
        P("seq", None),
        P(),
        P(None, None, "head"),
        P("head"),
        P("head", None),
        P(),
        P(("seq", "head"), None),
        P(("seq", "head"), None),
        P("seq", None, None, "head"),
        P("seq", "head", None),
    )

    return jax.shard_map(
        on_device, mesh=mesh, in_specs=placed, out_specs=P(("seq", "head"), None), check_vma=False
    )
```

```python
import jax
import jax.numpy as jnp
from jax import lax
from jax.experimental import pallas as pl
from jax.experimental.pallas import tpu as pltpu
from jax.sharding import PartitionSpec as P

D = 2048
DH = 128
HEADS = 4
WIDE = HEADS * DH
TOP = 8
CAP = 9
ROWS = 64
TOK = 256
MAIN = 512
SLOTS = 576
PACKED = D + 256
HALF = D // 2
EPSILON = 1e-06
BF = jnp.bfloat16
F32 = jnp.float32


VMEM = pl.BlockSpec(memory_space=pltpu.VMEM)
SMEM = pl.BlockSpec(memory_space=pltpu.SMEM)
ANY = pl.BlockSpec(memory_space=pl.ANY)
HBM = pl.BlockSpec(memory_space=pltpu.HBM)


def out(shape, dtype):
    return jax.ShapeDtypeStruct(shape, dtype)


def call(kernel, ins, outs, scratch=()):
    return pl.pallas_call(
        kernel,
        in_specs=ins,
        out_specs=[SMEM if o.dtype == jnp.int32 else VMEM for o in outs],
        out_shape=outs,
        scratch_shapes=list(scratch),
        compiler_params=pltpu.CompilerParams(vmem_limit_bytes=56 << 20),
    )


def rms_norm(values, gain):
    mean_square = jnp.mean(values * values, axis=-1, keepdims=True)
    return values * lax.rsqrt(mean_square + EPSILON) * gain


def dot(first, second):
    return jnp.dot(first, second, preferred_element_type=F32)


def dot_rows(first, second):
    return lax.dot_general(first, second, (((0,), (0,)), ((), ())), preferred_element_type=F32)


def dot_cols(first, second):
    return lax.dot_general(first, second, (((1,), (1,)), ((), ())), preferred_element_type=F32)


def of_head(h):
    return slice(h * DH, (h + 1) * DH)


def front_kernel(x_ref, gain_ref, wk_ref, wv_ref, normed_ref, k_ref, v_ref, state_ref, send_ref, zero_ref, wk, wv, sems):
    zero_ref[0] = 0
    copy_k = pltpu.make_async_copy(wk_ref, wk, sems.at[0])
    copy_v = pltpu.make_async_copy(wv_ref, wv, sems.at[1])
    copy_k.start()
    copy_v.start()
    normed = rms_norm(x_ref[...].astype(F32), gain_ref[...]).astype(BF)
    normed_ref[...] = normed
    copy_k.wait()
    key = dot(normed, wk[...]).astype(BF)
    k_ref[...] = key
    copy_v.wait()
    value = dot(normed, wv[...]).astype(BF)
    v_ref[...] = value
    for h in range(HEADS):
        state = dot_rows(key[:, of_head(h)], value[:, of_head(h)])
        state_ref[h] = state
        send_ref[h] = state.astype(BF)


def local_kernel(normed_ref, upper_ref, lower_ref, k_ref, v_ref, q_ref, local_ref):
    query = dot(normed_ref[:, :D // 2], upper_ref[...]) + dot(normed_ref[:, D // 2:], lower_ref[...])
    query = query.astype(BF)
    q_ref[...] = query
    row = lax.broadcasted_iota(jnp.int32, (TOK, TOK), 0)
    causal = lax.broadcasted_iota(jnp.int32, (TOK, TOK), 1) <= row
    for h in range(HEADS):
        scores = dot_cols(query[:, of_head(h)], k_ref[:, of_head(h)])
        scores = jnp.where(causal, scores, 0.0).astype(BF)
        local_ref[:, of_head(h)] = dot(scores, v_ref[:, of_head(h)])


def attend_kernel(
    place_ref, prefix_ref, g1, g2, g3, q_ref, local_ref, gain_ref, w_ref,
    own_ref, s1, s2, s3, mixed_ref, turned_ref,
):
    y = place_ref[0]
    head = place_ref[1]
    for h in range(HEADS):
        earlier = prefix_ref[h]
        for k, got in ((1, g1), (2, g2), (3, g3)):
            earlier = earlier + jnp.where(y >= k, got[h].astype(F32), 0.0)
        high = earlier.astype(BF)
        low = (earlier - high.astype(F32)).astype(BF)
        query = q_ref[:, of_head(h)]
        attended = local_ref[:, of_head(h)] + (dot(query, high) + dot(query, low))
        mixed_ref[:, of_head(h)] = rms_norm(attended, gain_ref[:, of_head(h)]).astype(BF)
    for k in range(4):
        start = pl.multiple_of(((head - k) % 4) * ROWS, ROWS)
        turned_ref[k * ROWS:(k + 1) * ROWS, :] = mixed_ref[pl.ds(start, ROWS), :]
    for n in range(4):
        cols = slice(n * 512, (n + 1) * 512)
        rows = dot(turned_ref[...], w_ref[:, cols])
        own_ref[:, cols] = rows[:ROWS]
        s3[:, cols] = rows[ROWS:2 * ROWS].astype(BF)
        s2[:, cols] = rows[2 * ROWS:3 * ROWS].astype(BF)
        s1[:, cols] = rows[3 * ROWS:].astype(BF)


def routing_kernel(head_ref, t0, t1, t2, t3, place_ref, weight_ref):
    head = head_ref[0]
    tables = jnp.concatenate([t0[...], t1[...], t2[...], t3[...]], axis=0)
    wanted = lax.broadcasted_iota(jnp.int32, (TOK, 16), 1) * 4 + head
    chosen = jnp.zeros((TOK, 16), F32)
    gates = jnp.zeros((TOK, 16), F32)
    for k in range(TOP):
        hit = tables[:, k:k + 1].astype(jnp.int32) == wanted
        chosen = chosen + hit.astype(F32)
        gates = gates + jnp.where(hit, tables[:, TOP + k:TOP + k + 1], 0.0)
    row = lax.broadcasted_iota(jnp.int32, (TOK, TOK), 0)
    col = lax.broadcasted_iota(jnp.int32, (TOK, TOK), 1)
    before = ((row // ROWS == col // ROWS) & (col < row)).astype(F32).astype(BF)
    rank = dot(before, chosen.astype(BF))
    block = (head - lax.broadcasted_iota(jnp.int32, (TOK, 16), 0) // ROWS) & 3
    base = ((block >> 1) * 18 + (block & 1) * CAP).astype(F32)
    slot = jnp.where(chosen > 0, base + rank, -1.0).astype(BF)

    def of_row(shape, axis):
        row = lax.broadcasted_iota(jnp.int32, shape, axis)
        is_main = row < MAIN
        chip = jnp.where(is_main, row >> 5, (row & 31) >> 1)
        core = jnp.where(is_main, (row >> 4) & 1, row & 1)
        within = jnp.where(is_main, row & 15, 16 + ((row - MAIN) >> 5))
        return chip, (core * 18 + within).astype(F32)

    chip, want = of_row((SLOTS, 16), 0)
    spread = (chip == lax.broadcasted_iota(jnp.int32, (SLOTS, 16), 1)).astype(F32).astype(BF)
    place_ref[...] = (dot_cols(spread, slot) == want[:, :1]).astype(F32).astype(BF)
    chip, want = of_row((16, SLOTS), 1)
    spread = (chip == lax.broadcasted_iota(jnp.int32, (16, SLOTS), 0)).astype(F32).astype(BF)
    at_row = dot(slot, spread) == want[:1, :]
    weight_ref[...] = jnp.where(at_row, dot(gates.astype(BF), spread), 0.0).astype(BF)


def dispatch_kernel(place_ref, t0, t1, t2, t3, out_ref, tokens):
    for k, ref in enumerate((t0, t1, t2, t3)):
        tokens[k * ROWS:(k + 1) * ROWS, :] = ref[...]
    tail = []
    for n in range(4):
        cols = slice(n * 512, (n + 1) * 512)
        rows = dot(place_ref[...], tokens[:, cols])
        out_ref[:, cols] = rows[:MAIN].astype(BF)
        tail.append(rows[MAIN:])
    tail = jnp.concatenate(tail, axis=1)
    for t in range(2):
        piece = tail[t * 32:(t + 1) * 32].reshape(MAIN, 128).astype(BF)
        out_ref[:, D + t * 128:D + (t + 1) * 128] = piece


def start_quarters(keep_ref, arrays, dest_of, sems, first):
    def load(q, ref):
        return pltpu.make_async_copy(ref, dest_of(q), sems.at[first + q])

    keep = keep_ref[0] == 1
    copies = [load(0, arrays[0]), load(1, arrays[1])]
    copies[0].start()
    copies[1].start()

    @pl.when(keep)
    def _():
        load(2, arrays[2]).start()
        load(3, arrays[5]).start()

    @pl.when(jnp.logical_not(keep))
    def _():
        load(2, arrays[3]).start()
        load(3, arrays[4]).start()

    return copies + [load(2, arrays[2]), load(3, arrays[4])]


def down_half(act, down, out_ref):
    tail = []
    for n in range(2):
        cols = slice(n * 512, (n + 1) * 512)
        result = dot(act, down[:, cols])
        out_ref[:, cols] = result[:MAIN].astype(BF)
        tail.append(result[MAIN:])
    tail = jnp.concatenate(tail, axis=1)
    pieces = [tail[t * 32:(t + 1) * 32].reshape(32, 8, 128) for t in range(2)]
    out_ref[:, HALF:] = jnp.concatenate(pieces, axis=1).reshape(MAIN, 128).astype(BF)


def expert_kernel(
    keep_ref, x_ref, gu0, gu1, gu2, gu3, gu4, gu5, dn0, dn1, dn2, dn3, dn4, dn5,
    out_ref, act, rows, ends, gate_up, down, sems,
):
    copy_rows = pltpu.make_async_copy(x_ref.at[:, :D], rows.at[:MAIN], sems.at[8])
    copy_ends = pltpu.make_async_copy(x_ref.at[:, D:], ends, sems.at[9])
    copy_ends.start()
    copy_rows.start()
    copies = start_quarters(
        keep_ref, (gu0, gu1, gu2, gu3, gu4, gu5), lambda q: gate_up.at[q], sems, 0
    )
    halves = [dn.at[:, :HALF] for dn in (dn0, dn1, dn2, dn3, dn4, dn5)]
    down_copies = start_quarters(
        keep_ref, halves, lambda q: down.at[q * 256:(q + 1) * 256], sems, 4
    )
    copy_ends.wait()
    for t in range(2):
        piece = ends[:, t * 128:(t + 1) * 128].astype(F32).reshape(32, D)
        rows[MAIN + t * 32:MAIN + (t + 1) * 32, :] = piece.astype(BF)
    copy_rows.wait()
    for q in range(4):
        copies[q].wait()
        gate = dot(rows[...], gate_up[q, 0])
        up = dot(rows[...], gate_up[q, 1])
        act[:, q * 256:(q + 1) * 256] = (jax.nn.silu(gate) * up).astype(BF)
    for copy in down_copies:
        copy.wait()
    down_half(act[...], down, out_ref)


def finish_kernel(keep_ref, act, dn0, dn1, dn2, dn3, dn4, dn5, out_ref, down, sems):
    halves = [dn.at[:, HALF:] for dn in (dn0, dn1, dn2, dn3, dn4, dn5)]
    copies = start_quarters(
        keep_ref, halves, lambda q: down.at[q * 256:(q + 1) * 256], sems, 0
    )
    for copy in copies:
        copy.wait()
    down_half(act[...], down, out_ref)


def combine_kernel(weight_ref, y_ref, own_ref, s1, s2, s3, tail):
    ends = y_ref[:, HALF:].astype(F32).reshape(32, 16, 128)
    for t in range(2):
        tail[t * 32:(t + 1) * 32, :] = ends[:, t * 8:(t + 1) * 8].reshape(32, HALF).astype(BF)
    for n in range(2):
        cols = slice(n * 512, (n + 1) * 512)
        rows = dot(weight_ref[:, :MAIN], y_ref[:, cols]) + dot(weight_ref[:, MAIN:], tail[:, cols])
        own_ref[:, cols] = rows[:ROWS]
        s3[:, cols] = rows[ROWS:2 * ROWS].astype(BF)
        s2[:, cols] = rows[2 * ROWS:3 * ROWS].astype(BF)
        s1[:, cols] = rows[3 * ROWS:].astype(BF)


def blocks_out(columns):
    return [out((ROWS, columns), F32)] + [out((ROWS, columns), BF)] * 3


def seq_perm(dy, dz, dc):
    return [
        ((y * 4 + z) * 2 + c, (((y + dy) % 4) * 4 + (z + dz) % 4) * 2 + (c ^ dc))
        for y in range(4)
        for z in range(4)
        for c in range(2)
    ]


def head_perm(shift):
    return [(h, (h + shift) % 4) for h in range(4)]


def device_perm(target):
    pairs = []
    for chip in range(16):
        for c in range(2):
            for h in range(4):
                to = target(c, h)
                if to is None:
                    continue
                pairs.append(((chip * 2 + c) * 4 + h, (chip * 2 + to[0]) * 4 + to[1]))
    return pairs


def near_target(c, h):
    chip = 2 * c + 1 - (h & 1)
    return (c, chip) if (chip - 1) % 4 == h else (1 - c, chip)


def far_target(c, h):
    return None if h // 2 == c else (1 - c, (h + 2) % 4)


def keep_target(c, h):
    return (1 - c, h) if h // 2 == c else None


def pass_target(c, h):
    return None if h // 2 == c else (1 - c, h)


def permute_all(arrays, axes, perm):
    return [lax.ppermute(a, axes, perm) for a in arrays]


def pick_kernel(index_ref, gu_ref, dn_ref, gu_out, dn_out, sems):
    index = index_ref[0]
    copies = []
    for half in range(2):
        for part in range(2):
            rows = pl.ds(part * (D // 2), D // 2)
            copies.append((gu_ref.at[index, half, rows], gu_out.at[half, rows]))
        rows = pl.ds(half * 128, 128)
        copies.append((dn_ref.at[index, rows], dn_out.at[rows]))
    copies = [pltpu.make_async_copy(a, b, sems.at[i]) for i, (a, b) in enumerate(copies)]
    for copy in copies:
        copy.start()
    for copy in copies:
        copy.wait()


def pick(w_gate_up, w_down, index):
    return pl.pallas_call(
        pick_kernel,
        in_specs=[SMEM, ANY, ANY],
        out_specs=[VMEM, VMEM],
        out_shape=[out((2, D, 256), BF), out((256, D), BF)],
        scratch_shapes=[pltpu.SemaphoreType.DMA((6,))],
        name="pick",
    )(index.astype(jnp.int32)[None], w_gate_up, w_down)


def exchange(array, step):
    dy, dz = step
    return [lax.ppermute(array, "seq", seq_perm(dy * k, dz * k, 0)) for k in range(1, 4)]


def gather_head(array):
    return [array] + [lax.ppermute(array, "head", head_perm(k)) for k in range(1, 4)]


def scatter_head(blocks):
    total = blocks[0]
    for k in range(1, 4):
        total = total + lax.ppermute(blocks[k], "head", head_perm(k)).astype(F32)
    return total


def on_device(
    hidden_in, attn_gain, w_qkv, out_gain, w_out, moe_gain, routes, gate_weights, w_gate_up, w_down
):
    seq = lax.axis_index("seq")
    head = lax.axis_index("head")
    core = seq % 2
    z = (seq // 2) % 4
    y = seq // 8

    both = ("seq", "head")
    near = permute_all(pick(w_gate_up, w_down, 1 - (head & 1)), both, device_perm(near_target))
    tables = gather_head(jnp.concatenate([routes.astype(F32), gate_weights], axis=1))
    place_rows, weight = call(
        routing_kernel, [SMEM] + [VMEM] * 4, [out((SLOTS, TOK), BF), out((TOK, SLOTS), BF)]
    )(head.astype(jnp.int32)[None], *tables)

    normed, key, value, own_state, send_state, zero = call(
        front_kernel,
        [VMEM, VMEM, ANY, ANY],
        [
            out((TOK, D), BF),
            out((TOK, WIDE), BF),
            out((TOK, WIDE), BF),
            out((HEADS, DH, DH), F32),
            out((HEADS, DH, DH), BF),
            out((1,), jnp.int32),
        ],
        [pltpu.VMEM((D, WIDE), BF), pltpu.VMEM((D, WIDE), BF), pltpu.SemaphoreType.DMA((2,))],
    )(hidden_in, attn_gain[None, :], w_qkv[:, 1], w_qkv[:, 2])
    sibling = lax.ppermute(send_state, "seq", seq_perm(0, 0, 1)).astype(F32)
    odd = (head & 1) + zero[0]
    rest = pick(w_gate_up, w_down, odd)
    far_down = lax.ppermute(rest[1], both, device_perm(far_target))
    far = [lax.ppermute(rest[0], both, device_perm(far_target)), far_down]
    rest_other = permute_all(rest, both, device_perm(keep_target))
    near_other = permute_all(near, "seq", seq_perm(0, 0, 1))
    far_other = permute_all(far, both, device_perm(pass_target))
    pieces = [near, near_other, rest, rest_other, far, far_other]
    prefix = jnp.where(core == 1, sibling, 0.0)
    total = own_state + sibling
    rows_z = exchange(total.astype(BF), (0, 1))
    for k, got in enumerate(rows_z):
        prefix = prefix + jnp.where(z > k, got.astype(F32), 0.0)
        total = total + got.astype(F32)
    rows_y = exchange(total.astype(BF), (1, 0))

    w_query = [
        lax.dynamic_slice_in_dim(w_qkv, zero[0] + start, D // 2, 0)[:, 0]
        for start in (0, D // 2)
    ]
    query, local = call(
        local_kernel, [VMEM] * 5, [out((TOK, WIDE), BF), out((TOK, WIDE), F32)]
    )(normed, *w_query, key, value)
    place = jnp.stack([y, head]).astype(jnp.int32)
    blocks = call(
        attend_kernel,
        [SMEM] + [VMEM] * 8,
        blocks_out(D),
        [pltpu.VMEM((TOK, WIDE), BF), pltpu.VMEM((TOK, WIDE), BF)],
    )(place, prefix, *rows_y, query, local, out_gain[None, :], w_out)
    attn_rows = scatter_head(blocks)
    resid = lax.dynamic_slice_in_dim(hidden_in, head * ROWS, ROWS, 0).astype(F32) + attn_rows
    normed2 = rms_norm(resid, moe_gain).astype(BF)
    tokens = gather_head(normed2)

    sent = call(
        dispatch_kernel, [VMEM] * 5, [out((MAIN, PACKED), BF)], [pltpu.VMEM((TOK, D), BF)]
    )(place_rows, *tokens)[0]
    received = lax.all_to_all(sent.reshape(32, 16, PACKED), "seq", 0, 0, tiled=True)
    keep = (head // 2 == core).astype(jnp.int32)[None]
    gate_ups = [p[0] for p in pieces]
    downs = [p[1] for p in pieces]
    first, act = call(
        expert_kernel,
        [SMEM, HBM] + [ANY] * 12,
        [out((MAIN, HALF + 128), BF), out((SLOTS, 1024), BF)],
        [
            pltpu.VMEM((SLOTS, D), BF),
            pltpu.VMEM((MAIN, 256), BF),
            pltpu.VMEM((4, 2, D, 256), BF),
            pltpu.VMEM((1024, HALF), BF),
            pltpu.SemaphoreType.DMA((10,)),
        ],
    )(keep, received.reshape(MAIN, PACKED), *gate_ups, *downs)
    second = call(
        finish_kernel,
        [SMEM, VMEM] + [ANY] * 6,
        [out((MAIN, HALF + 128), BF)],
        [pltpu.VMEM((1024, HALF), BF), pltpu.SemaphoreType.DMA((4,))],
    )(keep, act, *downs)[0]
    moe_sum = []
    for results in (first, second):
        back = lax.all_to_all(results.reshape(32, 16, HALF + 128), "seq", 0, 0, tiled=True)
        blocks = call(
            combine_kernel, [VMEM] * 2, blocks_out(HALF), [pltpu.VMEM((64, HALF), BF)]
        )(weight, back.reshape(MAIN, HALF + 128))
        moe_sum.append(scatter_head(blocks))
    return (resid + jnp.concatenate(moe_sum, axis=1)).astype(BF)


def solution(mesh):
    placed = (
        P("seq", None),
        P(),
        P(None, None, "head"),
        P("head"),
        P("head", None),
        P(),
        P(("seq", "head"), None),
        P(("seq", "head"), None),
        P("seq", None, None, "head"),
        P("seq", "head", None),
    )

    return jax.shard_map(
        on_device, mesh=mesh, in_specs=placed, out_specs=P(("seq", "head"), None), check_vma=False
    )
```

```python
import jax
import jax.numpy as jnp
from jax import lax
from jax.experimental import pallas as pl
from jax.experimental.pallas import tpu as pltpu
from jax.sharding import PartitionSpec as P

D = 2048
DH = 128
HEADS = 4
WIDE = HEADS * DH
TOP = 8
CAP = 9
ROWS = 64
TOK = 256
MAIN = 512
SLOTS = 576
PACKED = D + 256
EPSILON = 1e-06
BF = jnp.bfloat16
F32 = jnp.float32


VMEM = pl.BlockSpec(memory_space=pltpu.VMEM)
SMEM = pl.BlockSpec(memory_space=pltpu.SMEM)
ANY = pl.BlockSpec(memory_space=pl.ANY)
HBM = pl.BlockSpec(memory_space=pltpu.HBM)


def out(shape, dtype):
    return jax.ShapeDtypeStruct(shape, dtype)


def call(kernel, ins, outs, scratch=()):
    return pl.pallas_call(
        kernel,
        in_specs=ins,
        out_specs=[SMEM if o.dtype == jnp.int32 else VMEM for o in outs],
        out_shape=outs,
        scratch_shapes=list(scratch),
        compiler_params=pltpu.CompilerParams(vmem_limit_bytes=56 << 20),
    )


def rms_norm(values, gain):
    mean_square = jnp.mean(values * values, axis=-1, keepdims=True)
    return values * lax.rsqrt(mean_square + EPSILON) * gain


def dot(first, second):
    return jnp.dot(first, second, preferred_element_type=F32)


def dot_rows(first, second):
    return lax.dot_general(first, second, (((0,), (0,)), ((), ())), preferred_element_type=F32)


def dot_cols(first, second):
    return lax.dot_general(first, second, (((1,), (1,)), ((), ())), preferred_element_type=F32)


def of_head(h):
    return slice(h * DH, (h + 1) * DH)


def front_kernel(x_ref, gain_ref, w_ref, normed_ref, k_ref, v_ref, send_ref, zero_ref, wk, wv, sems):
    copy_k = pltpu.make_async_copy(w_ref.at[1], wk, sems.at[0])
    copy_v = pltpu.make_async_copy(w_ref.at[2], wv, sems.at[1])
    copy_k.start()
    copy_v.start()
    zero_ref[0] = 0
    normed = rms_norm(x_ref[...].astype(F32), gain_ref[...]).astype(BF)
    normed_ref[...] = normed
    copy_k.wait()
    key = dot(normed, wk[...]).astype(BF)
    k_ref[...] = key
    copy_v.wait()
    value = dot(normed, wv[...]).astype(BF)
    v_ref[...] = value
    for h in range(HEADS):
        state = dot_rows(key[:, of_head(h)], value[:, of_head(h)])
        send_ref[of_head(h), :] = state.astype(BF)


def prefix_kernel(states_ref, out_ref):
    total = jnp.zeros((16, DH), F32)
    for s in range(32):
        out_ref[s] = total.astype(BF)
        total = total + states_ref[s].astype(F32)


def local_kernel(normed_ref, w_ref, k_ref, v_ref, q_ref, local_ref, wq, sems):
    copy_q = pltpu.make_async_copy(w_ref.at[0], wq, sems.at[0])
    copy_q.start()
    row = lax.broadcasted_iota(jnp.int32, (TOK, TOK), 0)
    causal = lax.broadcasted_iota(jnp.int32, (TOK, TOK), 1) <= row
    copy_q.wait()
    query = dot(normed_ref[...], wq[...]).astype(BF)
    q_ref[...] = query
    for h in range(HEADS):
        scores = dot_cols(query[:, of_head(h)], k_ref[:, of_head(h)])
        scores = jnp.where(causal, scores, 0.0).astype(BF)
        local_ref[:, of_head(h)] = dot(scores, v_ref[:, of_head(h)])


def attend_kernel(
    head_ref, earlier_ref, q_ref, local_ref, gain_ref, w_ref,
    own_ref, s1, s2, s3, mixed_ref, turned_ref,
):
    head = head_ref[0]
    for h in range(HEADS):
        attended = local_ref[:, of_head(h)] + dot(q_ref[:, of_head(h)], earlier_ref[of_head(h), :])
        mixed_ref[:, of_head(h)] = rms_norm(attended, gain_ref[:, of_head(h)]).astype(BF)
    for k in range(4):
        start = pl.multiple_of(((head - k) % 4) * ROWS, ROWS)
        turned_ref[k * ROWS:(k + 1) * ROWS, :] = mixed_ref[pl.ds(start, ROWS), :]
    for n in range(4):
        cols = slice(n * 512, (n + 1) * 512)
        rows = dot(turned_ref[...], w_ref[:, cols])
        own_ref[:, cols] = rows[:ROWS]
        s3[:, cols] = rows[ROWS:2 * ROWS].astype(BF)
        s2[:, cols] = rows[2 * ROWS:3 * ROWS].astype(BF)
        s1[:, cols] = rows[3 * ROWS:].astype(BF)


def routing_kernel(head_ref, t0, t1, t2, t3, place_ref, weight_ref):
    head = head_ref[0]
    tables = jnp.concatenate([t0[...], t1[...], t2[...], t3[...]], axis=0)
    wanted = lax.broadcasted_iota(jnp.int32, (TOK, 16), 1) * 4 + head
    chosen = jnp.zeros((TOK, 16), F32)
    gates = jnp.zeros((TOK, 16), F32)
    for k in range(TOP):
        hit = tables[:, k:k + 1].astype(jnp.int32) == wanted
        chosen = chosen + hit.astype(F32)
        gates = gates + jnp.where(hit, tables[:, TOP + k:TOP + k + 1], 0.0)
    row = lax.broadcasted_iota(jnp.int32, (TOK, TOK), 0)
    col = lax.broadcasted_iota(jnp.int32, (TOK, TOK), 1)
    before = ((row // ROWS == col // ROWS) & (col < row)).astype(F32).astype(BF)
    rank = dot(before, chosen.astype(BF))
    block = (head - lax.broadcasted_iota(jnp.int32, (TOK, 16), 0) // ROWS) & 3
    base = ((block >> 1) * 18 + (block & 1) * CAP).astype(F32)
    slot = jnp.where(chosen > 0, base + rank, -1.0).astype(BF)

    def of_row(shape, axis):
        row = lax.broadcasted_iota(jnp.int32, shape, axis)
        is_main = row < MAIN
        chip = jnp.where(is_main, row >> 5, (row & 31) >> 1)
        core = jnp.where(is_main, (row >> 4) & 1, row & 1)
        within = jnp.where(is_main, row & 15, 16 + ((row - MAIN) >> 5))
        return chip, (core * 18 + within).astype(F32)

    chip, want = of_row((SLOTS, 16), 0)
    spread = (chip == lax.broadcasted_iota(jnp.int32, (SLOTS, 16), 1)).astype(F32).astype(BF)
    place_ref[...] = (dot_cols(spread, slot) == want[:, :1]).astype(F32).astype(BF)
    chip, want = of_row((16, SLOTS), 1)
    spread = (chip == lax.broadcasted_iota(jnp.int32, (16, SLOTS), 0)).astype(F32).astype(BF)
    at_row = dot(slot, spread) == want[:1, :]
    weight_ref[...] = jnp.where(at_row, dot(gates.astype(BF), spread), 0.0).astype(BF)


def dispatch_kernel(place_ref, t0, t1, t2, t3, out_ref, tokens):
    for k, ref in enumerate((t0, t1, t2, t3)):
        tokens[k * ROWS:(k + 1) * ROWS, :] = ref[...]
    tail = []
    for n in range(4):
        cols = slice(n * 512, (n + 1) * 512)
        rows = dot(place_ref[...], tokens[:, cols])
        out_ref[:, cols] = rows[:MAIN].astype(BF)
        tail.append(rows[MAIN:])
    tail = jnp.concatenate(tail, axis=1)
    for t in range(2):
        piece = tail[t * 32:(t + 1) * 32].reshape(MAIN, 128).astype(BF)
        out_ref[:, D + t * 128:D + (t + 1) * 128] = piece


def start_quarters(keep_ref, arrays, dest_of, sems, first):
    def load(q, ref):
        return pltpu.make_async_copy(ref, dest_of(q), sems.at[first + q])

    keep = keep_ref[0] == 1
    copies = [load(0, arrays[0]), load(1, arrays[1])]
    copies[0].start()
    copies[1].start()

    @pl.when(keep)
    def _():
        load(2, arrays[2]).start()
        load(3, arrays[5]).start()

    @pl.when(jnp.logical_not(keep))
    def _():
        load(2, arrays[3]).start()
        load(3, arrays[4]).start()

    return copies + [load(2, arrays[2]), load(3, arrays[4])]


def expert_kernel(
    keep_ref, x_ref, gu0, gu1, gu2, gu3, gu4, gu5, dn0, dn1, dn2, dn3, dn4, dn5,
    out_ref, rows, gate_up, down, act, tail, sems,
):
    copies = start_quarters(
        keep_ref, (gu0, gu1, gu2, gu3, gu4, gu5), lambda q: gate_up.at[q], sems, 0
    )
    down_copies = start_quarters(
        keep_ref,
        (dn0, dn1, dn2, dn3, dn4, dn5),
        lambda q: down.at[q * 256:(q + 1) * 256],
        sems,
        4,
    )
    rows[:MAIN, :] = x_ref[:, :D]
    for t in range(2):
        piece = x_ref[:, D + t * 128:D + (t + 1) * 128].astype(F32).reshape(32, D)
        rows[MAIN + t * 32:MAIN + (t + 1) * 32, :] = piece.astype(BF)
    for q in range(4):
        copies[q].wait()
        gate = dot(rows[...], gate_up[q, 0])
        up = dot(rows[...], gate_up[q, 1])
        act[:, q * 256:(q + 1) * 256] = (jax.nn.silu(gate) * up).astype(BF)
    for copy in down_copies:
        copy.wait()
    for n in range(4):
        cols = slice(n * 512, (n + 1) * 512)
        result = dot(act[...], down[:, cols])
        out_ref[:, cols] = result[:MAIN].astype(BF)
        tail[:, cols] = result[MAIN:]
    for t in range(2):
        piece = tail[t * 32:(t + 1) * 32, :].reshape(MAIN, 128).astype(BF)
        out_ref[:, D + t * 128:D + (t + 1) * 128] = piece


def combine_kernel(weight_ref, y_ref, own_ref, s1, s2, s3, tail):
    for t in range(2):
        piece = y_ref[:, D + t * 128:D + (t + 1) * 128].astype(F32).reshape(32, D)
        tail[t * 32:(t + 1) * 32, :] = piece.astype(BF)
    for n in range(4):
        cols = slice(n * 512, (n + 1) * 512)
        rows = dot(weight_ref[:, :MAIN], y_ref[:, cols]) + dot(weight_ref[:, MAIN:], tail[:, cols])
        own_ref[:, cols] = rows[:ROWS]
        s3[:, cols] = rows[ROWS:2 * ROWS].astype(BF)
        s2[:, cols] = rows[2 * ROWS:3 * ROWS].astype(BF)
        s1[:, cols] = rows[3 * ROWS:].astype(BF)


BLOCKS_OUT = [out((ROWS, D), F32)] + [out((ROWS, D), BF)] * 3


def seq_perm(dy, dz, dc):
    return [
        ((y * 4 + z) * 2 + c, (((y + dy) % 4) * 4 + (z + dz) % 4) * 2 + (c ^ dc))
        for y in range(4)
        for z in range(4)
        for c in range(2)
    ]


def head_perm(shift):
    return [(h, (h + shift) % 4) for h in range(4)]


def device_perm(target):
    pairs = []
    for chip in range(16):
        for c in range(2):
            for h in range(4):
                to = target(c, h)
                if to is None:
                    continue
                pairs.append(((chip * 2 + c) * 4 + h, (chip * 2 + to[0]) * 4 + to[1]))
    return pairs


def near_target(c, h):
    chip = 2 * c + 1 - (h & 1)
    return (c, chip) if (chip - 1) % 4 == h else (1 - c, chip)


def far_target(c, h):
    return None if h // 2 == c else (1 - c, (h + 2) % 4)


def keep_target(c, h):
    return (1 - c, h) if h // 2 == c else None


def pass_target(c, h):
    return None if h // 2 == c else (1 - c, h)


def permute_all(arrays, axes, perm):
    return [lax.ppermute(a, axes, perm) for a in arrays]


def pick_kernel(index_ref, gu_ref, dn_ref, gu_out, dn_out, gu_buf, dn_buf, read_sems, write_sems):
    index = index_ref[0]
    reads = []
    writes = []
    for half in range(2):
        for part in range(2):
            rows = pl.ds(part * (D // 2), D // 2)
            reads.append((gu_ref.at[index, half, rows], gu_buf.at[half, rows]))
            writes.append((gu_buf.at[half, rows], gu_out.at[half, rows]))
        rows = pl.ds(half * 128, 128)
        reads.append((dn_ref.at[index, rows], dn_buf.at[rows]))
        writes.append((dn_buf.at[rows], dn_out.at[rows]))
    reads = [pltpu.make_async_copy(a, b, read_sems.at[i]) for i, (a, b) in enumerate(reads)]
    writes = [pltpu.make_async_copy(a, b, write_sems.at[i]) for i, (a, b) in enumerate(writes)]
    for read in reads:
        read.start()
    for read, write in zip(reads, writes):
        read.wait()
        write.start()
    for write in writes:
        write.wait()


def pick(w_gate_up, w_down, index):
    return pl.pallas_call(
        pick_kernel,
        in_specs=[SMEM, ANY, ANY],
        out_specs=[HBM, HBM],
        out_shape=[out((2, D, 256), BF), out((256, D), BF)],
        scratch_shapes=[
            pltpu.VMEM((2, D, 256), BF),
            pltpu.VMEM((256, D), BF),
            pltpu.SemaphoreType.DMA((6,)),
            pltpu.SemaphoreType.DMA((6,)),
        ],
        name="pick",
    )(index.astype(jnp.int32)[None], w_gate_up, w_down)


def gather_head(array):
    return [array] + [lax.ppermute(array, "head", head_perm(k)) for k in range(1, 4)]


def scatter_head(blocks):
    total = blocks[0]
    for k in range(1, 4):
        total = total + lax.ppermute(blocks[k], "head", head_perm(k)).astype(F32)
    return total


def on_device(
    hidden_in, attn_gain, w_qkv, out_gain, w_out, moe_gain, routes, gate_weights, w_gate_up, w_down
):
    seq = lax.axis_index("seq")
    head = lax.axis_index("head")
    core = seq % 2

    both = ("seq", "head")
    near = permute_all(pick(w_gate_up, w_down, 1 - (head & 1)), both, device_perm(near_target))
    w_planes = w_qkv.transpose(1, 0, 2)
    normed, key, value, send_state, zero = call(
        front_kernel,
        [VMEM, VMEM, ANY],
        [
            out((TOK, D), BF),
            out((TOK, WIDE), BF),
            out((TOK, WIDE), BF),
            out((WIDE, DH), BF),
            out((1,), jnp.int32),
        ],
        [pltpu.VMEM((D, WIDE), BF), pltpu.VMEM((D, WIDE), BF), pltpu.SemaphoreType.DMA((2,))],
    )(hidden_in, attn_gain[None, :], w_planes)
    states = lax.all_to_all(send_state.reshape(32, 16, DH), "seq", 0, 0, tiled=True)
    sums = call(prefix_kernel, [VMEM], [out((32, 16, DH), BF)])(states)[0]
    earlier = lax.all_to_all(sums, "seq", 0, 0, tiled=True).reshape(WIDE, DH)
    odd = (head & 1) + zero[0]
    rest = pick(w_gate_up, w_down, odd)
    far_down = lax.ppermute(rest[1], both, device_perm(far_target))
    far = [lax.ppermute(rest[0], both, device_perm(far_target)), far_down]
    rest_other = permute_all(rest, both, device_perm(keep_target))
    near_other = permute_all(near, "seq", seq_perm(0, 0, 1))
    far_other = permute_all(far, both, device_perm(pass_target))
    pieces = [near, near_other, rest, rest_other, far, far_other]

    query, local = call(
        local_kernel,
        [VMEM, ANY, VMEM, VMEM],
        [out((TOK, WIDE), BF), out((TOK, WIDE), F32)],
        [pltpu.VMEM((D, WIDE), BF), pltpu.SemaphoreType.DMA((1,))],
    )(normed, w_planes, key, value)
    here = head.astype(jnp.int32)[None]
    blocks = call(
        attend_kernel,
        [SMEM] + [VMEM] * 5,
        BLOCKS_OUT,
        [pltpu.VMEM((TOK, WIDE), BF), pltpu.VMEM((TOK, WIDE), BF)],
    )(here, earlier, query, local, out_gain[None, :], w_out)
    tables = gather_head(jnp.concatenate([routes.astype(F32), gate_weights], axis=1))
    place_rows, weight = call(
        routing_kernel, [SMEM] + [VMEM] * 4, [out((SLOTS, TOK), BF), out((TOK, SLOTS), BF)]
    )(here, *tables)

    attn_rows = scatter_head(blocks)
    resid = lax.dynamic_slice_in_dim(hidden_in, head * ROWS, ROWS, 0).astype(F32) + attn_rows
    normed2 = rms_norm(resid, moe_gain).astype(BF)
    tokens = gather_head(normed2)

    sent = call(
        dispatch_kernel, [VMEM] * 5, [out((MAIN, PACKED), BF)], [pltpu.VMEM((TOK, D), BF)]
    )(place_rows, *tokens)[0]
    received = lax.all_to_all(sent.reshape(32, 16, PACKED), "seq", 0, 0, tiled=True)
    keep = (head // 2 == core).astype(jnp.int32)[None]
    results = call(
        expert_kernel,
        [SMEM, VMEM] + [ANY] * 12,
        [out((MAIN, PACKED), BF)],
        [
            pltpu.VMEM((SLOTS, D), BF),
            pltpu.VMEM((4, 2, D, 256), BF),
            pltpu.VMEM((1024, D), BF),
            pltpu.VMEM((SLOTS, 1024), BF),
            pltpu.VMEM((64, D), F32),
            pltpu.SemaphoreType.DMA((8,)),
        ],
    )(keep, received.reshape(MAIN, PACKED), *[p[0] for p in pieces], *[p[1] for p in pieces])[0]
    back = lax.all_to_all(results.reshape(32, 16, PACKED), "seq", 0, 0, tiled=True)
    blocks = call(
        combine_kernel, [VMEM] * 2, BLOCKS_OUT, [pltpu.VMEM((64, D), BF)]
    )(weight, back.reshape(MAIN, PACKED))
    moe_sum = scatter_head(blocks)
    return (resid + moe_sum).astype(BF)


def solution(mesh):
    placed = (
        P("seq", None),
        P(),
        P(None, None, "head"),
        P("head"),
        P("head", None),
        P(),
        P(("seq", "head"), None),
        P(("seq", "head"), None),
        P("seq", None, None, "head"),
        P("seq", "head", None),
    )

    return jax.shard_map(
        on_device, mesh=mesh, in_specs=placed, out_specs=P(("seq", "head"), None), check_vma=False
    )
```

```python
import jax
import jax.numpy as jnp
from jax import lax
from jax.experimental import pallas as pl
from jax.experimental.pallas import tpu as pltpu
from jax.sharding import PartitionSpec as P

D = 2048
DH = 128
HEADS = 4
WIDE = HEADS * DH
TOP = 8
CAP = 9
ROWS = 64
TOK = 256
MAIN = 512
SLOTS = 576
PACKED = D + 256
EPSILON = 1e-06
BF = jnp.bfloat16
F32 = jnp.float32


VMEM = pl.BlockSpec(memory_space=pltpu.VMEM)
SMEM = pl.BlockSpec(memory_space=pltpu.SMEM)
ANY = pl.BlockSpec(memory_space=pl.ANY)
HBM = pl.BlockSpec(memory_space=pltpu.HBM)


def on_chip(array):
    return pltpu.with_memory_space_constraint(array, pltpu.VMEM)


def out(shape, dtype):
    return jax.ShapeDtypeStruct(shape, dtype)


def chip(shape, dtype):
    return pltpu.VMEM(shape, dtype)


def spec_of(o):
    if o.dtype == jnp.int32:
        return SMEM
    return HBM if o in QUARTER else VMEM


def call(kernel, ins, outs, scratch=(), limit=54):
    return pl.pallas_call(
        kernel,
        in_specs=ins,
        out_specs=[spec_of(o) for o in outs],
        out_shape=outs,
        scratch_shapes=list(scratch),
        compiler_params=pltpu.CompilerParams(vmem_limit_bytes=limit << 20),
    )


def rms_norm(values, gain):
    mean_square = jnp.mean(values * values, axis=-1, keepdims=True)
    return values * lax.rsqrt(mean_square + EPSILON) * gain


def dot(first, second):
    return jnp.dot(first, second, preferred_element_type=F32)


def dot_rows(first, second):
    return lax.dot_general(first, second, (((0,), (0,)), ((), ())), preferred_element_type=F32)


def dot_cols(first, second):
    return lax.dot_general(first, second, (((1,), (1,)), ((), ())), preferred_element_type=F32)


def of_head(h):
    return slice(h * DH, (h + 1) * DH)


def pick_copies(index_ref, gu_ref, dn_ref, gu_out, dn_out, gu_buf, dn_buf, read_sems, write_sems):
    index = index_ref[0]
    reads = []
    writes = []
    for half in range(2):
        for part in range(2):
            rows = pl.ds(part * (D // 2), D // 2)
            reads.append((gu_ref.at[index, half, rows], gu_buf.at[half, rows]))
            writes.append((gu_buf.at[half, rows], gu_out.at[half, rows]))
        rows = pl.ds(half * 128, 128)
        reads.append((dn_ref.at[index, rows], dn_buf.at[rows]))
        writes.append((dn_buf.at[rows], dn_out.at[rows]))
    return (
        [pltpu.make_async_copy(a, b, read_sems.at[i]) for i, (a, b) in enumerate(reads)],
        [pltpu.make_async_copy(a, b, write_sems.at[i]) for i, (a, b) in enumerate(writes)],
    )


def front_kernel(
    index_ref, x_ref, gain_ref, w_ref, gu_ref, dn_ref,
    normed_ref, k_ref, v_ref, send_ref, zero_ref, gu_out, dn_out,
    wk, wv, sems, gu_buf, dn_buf, read_sems, write_sems,
):
    copy_k = pltpu.make_async_copy(w_ref.at[1], wk, sems.at[0])
    copy_v = pltpu.make_async_copy(w_ref.at[2], wv, sems.at[1])
    copy_k.start()
    copy_v.start()
    reads, writes = pick_copies(
        index_ref, gu_ref, dn_ref, gu_out, dn_out, gu_buf, dn_buf, read_sems, write_sems
    )
    for read in reads:
        read.start()
    zero_ref[0] = 0
    normed = rms_norm(x_ref[...].astype(F32), gain_ref[...]).astype(BF)
    normed_ref[...] = normed
    copy_k.wait()
    key = dot(normed, wk[...]).astype(BF)
    k_ref[...] = key
    copy_v.wait()
    for read, write in zip(reads, writes):
        read.wait()
        write.start()
    value = dot(normed, wv[...]).astype(BF)
    v_ref[...] = value
    for h in range(HEADS):
        state = dot_rows(key[:, of_head(h)], value[:, of_head(h)])
        send_ref[of_head(h), :] = state.astype(BF)
    for write in writes:
        write.wait()


def prefix_kernel(states_ref, out_ref):
    total = jnp.zeros((16, DH), F32)
    for s in range(32):
        out_ref[s] = total.astype(BF)
        total = total + states_ref[s].astype(F32)


def local_kernel(normed_ref, w_ref, k_ref, v_ref, q_ref, local_ref, wq, sems):
    copy_q = pltpu.make_async_copy(w_ref.at[0], wq, sems.at[0])
    copy_q.start()
    row = lax.broadcasted_iota(jnp.int32, (TOK, TOK), 0)
    causal = lax.broadcasted_iota(jnp.int32, (TOK, TOK), 1) <= row
    copy_q.wait()
    query = dot(normed_ref[...], wq[...]).astype(BF)
    q_ref[...] = query
    for h in range(HEADS):
        scores = dot_cols(query[:, of_head(h)], k_ref[:, of_head(h)])
        scores = jnp.where(causal, scores, 0.0).astype(BF)
        local_ref[:, of_head(h)] = dot(scores, v_ref[:, of_head(h)])


def attend_kernel(
    head_ref, earlier_ref, q_ref, local_ref, gain_ref, w_ref,
    own_ref, s1, s2, s3, mixed_ref, turned_ref,
):
    head = head_ref[0]
    for h in range(HEADS):
        attended = local_ref[:, of_head(h)] + dot(q_ref[:, of_head(h)], earlier_ref[of_head(h), :])
        mixed_ref[:, of_head(h)] = rms_norm(attended, gain_ref[:, of_head(h)]).astype(BF)
    for k in range(4):
        start = pl.multiple_of(((head - k) % 4) * ROWS, ROWS)
        turned_ref[k * ROWS:(k + 1) * ROWS, :] = mixed_ref[pl.ds(start, ROWS), :]
    for n in range(4):
        cols = slice(n * 512, (n + 1) * 512)
        rows = dot(turned_ref[...], w_ref[:, cols])
        own_ref[:, cols] = rows[:ROWS]
        s3[:, cols] = rows[ROWS:2 * ROWS].astype(BF)
        s2[:, cols] = rows[2 * ROWS:3 * ROWS].astype(BF)
        s1[:, cols] = rows[3 * ROWS:].astype(BF)


def routing_kernel(head_ref, t0, t1, t2, t3, place_ref, weight_ref):
    head = head_ref[0]
    tables = jnp.concatenate([t0[...], t1[...], t2[...], t3[...]], axis=0)
    wanted = lax.broadcasted_iota(jnp.int32, (TOK, 16), 1) * 4 + head
    chosen = jnp.zeros((TOK, 16), F32)
    gates = jnp.zeros((TOK, 16), F32)
    for k in range(TOP):
        hit = tables[:, k:k + 1].astype(jnp.int32) == wanted
        chosen = chosen + hit.astype(F32)
        gates = gates + jnp.where(hit, tables[:, TOP + k:TOP + k + 1], 0.0)
    row = lax.broadcasted_iota(jnp.int32, (TOK, TOK), 0)
    col = lax.broadcasted_iota(jnp.int32, (TOK, TOK), 1)
    before = ((row // ROWS == col // ROWS) & (col < row)).astype(F32).astype(BF)
    rank = dot(before, chosen.astype(BF))
    block = (head - lax.broadcasted_iota(jnp.int32, (TOK, 16), 0) // ROWS) & 3
    base = ((block >> 1) * 18 + (block & 1) * CAP).astype(F32)
    slot = jnp.where(chosen > 0, base + rank, -1.0).astype(BF)

    def of_row(shape, axis):
        row = lax.broadcasted_iota(jnp.int32, shape, axis)
        is_main = row < MAIN
        chip = jnp.where(is_main, row >> 5, (row & 31) >> 1)
        core = jnp.where(is_main, (row >> 4) & 1, row & 1)
        within = jnp.where(is_main, row & 15, 16 + ((row - MAIN) >> 5))
        return chip, (core * 18 + within).astype(F32)

    chip, want = of_row((SLOTS, 16), 0)
    spread = (chip == lax.broadcasted_iota(jnp.int32, (SLOTS, 16), 1)).astype(F32).astype(BF)
    place_ref[...] = (dot_cols(spread, slot) == want[:, :1]).astype(F32).astype(BF)
    chip, want = of_row((16, SLOTS), 1)
    spread = (chip == lax.broadcasted_iota(jnp.int32, (16, SLOTS), 0)).astype(F32).astype(BF)
    at_row = dot(slot, spread) == want[:1, :]
    weight_ref[...] = jnp.where(at_row, dot(gates.astype(BF), spread), 0.0).astype(BF)


def dispatch_kernel(place_ref, t0, t1, t2, t3, out_ref, tokens):
    for k, ref in enumerate((t0, t1, t2, t3)):
        tokens[k * ROWS:(k + 1) * ROWS, :] = ref[...]
    tail = []
    for n in range(4):
        cols = slice(n * 512, (n + 1) * 512)
        rows = dot(place_ref[...], tokens[:, cols])
        out_ref[:, cols] = rows[:MAIN].astype(BF)
        tail.append(rows[MAIN:])
    tail = jnp.concatenate(tail, axis=1)
    for t in range(2):
        piece = tail[t * 32:(t + 1) * 32].reshape(MAIN, 128).astype(BF)
        out_ref[:, D + t * 128:D + (t + 1) * 128] = piece


def start_quarters(keep_ref, arrays, dest_of, sems, first):
    def load(q, ref):
        return pltpu.make_async_copy(ref, dest_of(q), sems.at[first + q])

    keep = keep_ref[0] == 1
    copies = [load(0, arrays[0]), load(1, arrays[1])]
    copies[0].start()
    copies[1].start()

    @pl.when(keep)
    def _():
        load(2, arrays[2]).start()
        load(3, arrays[5]).start()

    @pl.when(jnp.logical_not(keep))
    def _():
        load(2, arrays[3]).start()
        load(3, arrays[4]).start()

    return copies + [load(2, arrays[2]), load(3, arrays[4])]


def expert_kernel(
    keep_ref, x_ref, gu0, gu1, gu2, gu3, gu4, gu5, dn0, dn1, dn2, dn3, dn4, dn5,
    out_ref, rows, gate_up, down, act, tail, sems,
):
    copies = start_quarters(
        keep_ref, (gu0, gu1, gu2, gu3, gu4, gu5), lambda q: gate_up.at[q], sems, 0
    )
    down_copies = start_quarters(
        keep_ref,
        (dn0, dn1, dn2, dn3, dn4, dn5),
        lambda q: down.at[q * 256:(q + 1) * 256],
        sems,
        4,
    )
    rows[:MAIN, :] = x_ref[:, :D]
    for t in range(2):
        piece = x_ref[:, D + t * 128:D + (t + 1) * 128].astype(F32).reshape(32, D)
        rows[MAIN + t * 32:MAIN + (t + 1) * 32, :] = piece.astype(BF)
    for q in range(4):
        copies[q].wait()
        gate = dot(rows[...], gate_up[q, 0])
        up = dot(rows[...], gate_up[q, 1])
        act[:, q * 256:(q + 1) * 256] = (jax.nn.silu(gate) * up).astype(BF)
    for copy in down_copies:
        copy.wait()
    for n in range(4):
        cols = slice(n * 512, (n + 1) * 512)
        result = dot(act[...], down[:, cols])
        out_ref[:, cols] = result[:MAIN].astype(BF)
        tail[:, cols] = result[MAIN:]
    for t in range(2):
        piece = tail[t * 32:(t + 1) * 32, :].reshape(MAIN, 128).astype(BF)
        out_ref[:, D + t * 128:D + (t + 1) * 128] = piece


def combine_kernel(weight_ref, y_ref, own_ref, s1, s2, s3, tail):
    for t in range(2):
        piece = y_ref[:, D + t * 128:D + (t + 1) * 128].astype(F32).reshape(32, D)
        tail[t * 32:(t + 1) * 32, :] = piece.astype(BF)
    for n in range(4):
        cols = slice(n * 512, (n + 1) * 512)
        rows = dot(weight_ref[:, :MAIN], y_ref[:, cols]) + dot(weight_ref[:, MAIN:], tail[:, cols])
        own_ref[:, cols] = rows[:ROWS]
        s3[:, cols] = rows[ROWS:2 * ROWS].astype(BF)
        s2[:, cols] = rows[2 * ROWS:3 * ROWS].astype(BF)
        s1[:, cols] = rows[3 * ROWS:].astype(BF)


BLOCKS_OUT = [out((ROWS, D), F32)] + [out((ROWS, D), BF)] * 3


def seq_perm(dy, dz, dc):
    return [
        ((y * 4 + z) * 2 + c, (((y + dy) % 4) * 4 + (z + dz) % 4) * 2 + (c ^ dc))
        for y in range(4)
        for z in range(4)
        for c in range(2)
    ]


def head_perm(shift):
    return [(h, (h + shift) % 4) for h in range(4)]


def device_perm(target):
    pairs = []
    for chip in range(16):
        for c in range(2):
            for h in range(4):
                to = target(c, h)
                if to is None:
                    continue
                pairs.append(((chip * 2 + c) * 4 + h, (chip * 2 + to[0]) * 4 + to[1]))
    return pairs


def near_target(c, h):
    chip = 2 * c + 1 - (h & 1)
    return (c, chip) if (chip - 1) % 4 == h else (1 - c, chip)


def far_target(c, h):
    return None if h // 2 == c else (1 - c, (h + 2) % 4)


def keep_target(c, h):
    return (1 - c, h) if h // 2 == c else None


def pass_target(c, h):
    return None if h // 2 == c else (1 - c, h)


def permute_all(arrays, axes, perm):
    return [lax.ppermute(a, axes, perm) for a in arrays]


def pick_kernel(*refs):
    reads, writes = pick_copies(*refs)
    for read in reads:
        read.start()
    for read, write in zip(reads, writes):
        read.wait()
        write.start()
    for write in writes:
        write.wait()


QUARTER = [out((2, D, 256), BF), out((256, D), BF)]
PICK_SCRATCH = [
    pltpu.VMEM((2, D, 256), BF),
    pltpu.VMEM((256, D), BF),
    pltpu.SemaphoreType.DMA((6,)),
    pltpu.SemaphoreType.DMA((6,)),
]


def pick(w_gate_up, w_down, index):
    return pl.pallas_call(
        pick_kernel,
        in_specs=[SMEM, HBM, HBM],
        out_specs=[HBM, HBM],
        out_shape=QUARTER,
        scratch_shapes=PICK_SCRATCH,
        compiler_params=pltpu.CompilerParams(vmem_limit_bytes=50 << 20),
        name="pick",
    )(index.astype(jnp.int32)[None], w_gate_up, w_down)


def gather_head(array):
    return [array] + [lax.ppermute(array, "head", head_perm(k)) for k in range(1, 4)]


def scatter_head(blocks):
    total = blocks[0]
    for k in range(1, 4):
        total = total + lax.ppermute(blocks[k], "head", head_perm(k)).astype(F32)
    return total


def on_device(
    hidden_in, attn_gain, w_qkv, out_gain, w_out, moe_gain, routes, gate_weights, w_gate_up, w_down
):
    seq = lax.axis_index("seq")
    head = lax.axis_index("head")
    core = seq % 2

    w_planes = w_qkv.transpose(1, 0, 2)
    normed, key, value, send_state, zero, *near = call(
        front_kernel,
        [SMEM, VMEM, VMEM, HBM, HBM, HBM],
        [
            chip((TOK, D), BF),
            chip((TOK, WIDE), BF),
            chip((TOK, WIDE), BF),
            out((WIDE, DH), BF),
            out((1,), jnp.int32),
        ]
        + QUARTER,
        [pltpu.VMEM((D, WIDE), BF), pltpu.VMEM((D, WIDE), BF), pltpu.SemaphoreType.DMA((2,))]
        + PICK_SCRATCH,
    )(
        (1 - (head & 1)).astype(jnp.int32)[None],
        hidden_in,
        attn_gain[None, :],
        w_planes,
        w_gate_up,
        w_down,
    )
    both = ("seq", "head")
    near = permute_all(near, both, device_perm(near_target))
    states = lax.all_to_all(send_state.reshape(32, 16, DH), "seq", 0, 0, tiled=True)
    sums = call(prefix_kernel, [VMEM], [out((32, 16, DH), BF)])(on_chip(states))[0]
    earlier = lax.all_to_all(sums, "seq", 0, 0, tiled=True).reshape(WIDE, DH)
    odd = (head & 1) + zero[0]
    rest = pick(w_gate_up, w_down, odd)
    far_down = lax.ppermute(rest[1], both, device_perm(far_target))
    far = [lax.ppermute(rest[0], both, device_perm(far_target)), far_down]
    rest_other = permute_all(rest, both, device_perm(keep_target))
    near_other = permute_all(near, "seq", seq_perm(0, 0, 1))
    far_other = permute_all(far, both, device_perm(pass_target))
    pieces = [near, near_other, rest, rest_other, far, far_other]

    query, local = call(
        local_kernel,
        [VMEM, HBM, VMEM, VMEM],
        [chip((TOK, WIDE), BF), chip((TOK, WIDE), F32)],
        [pltpu.VMEM((D, WIDE), BF), pltpu.SemaphoreType.DMA((1,))],
    )(on_chip(normed), w_planes, on_chip(key), on_chip(value))
    here = head.astype(jnp.int32)[None]
    blocks = call(
        attend_kernel,
        [SMEM] + [VMEM] * 5,
        BLOCKS_OUT,
        [pltpu.VMEM((TOK, WIDE), BF), pltpu.VMEM((TOK, WIDE), BF)],
    )(here, on_chip(earlier), on_chip(query), on_chip(local), out_gain[None, :], w_out)
    tables = gather_head(jnp.concatenate([routes.astype(F32), gate_weights], axis=1))
    place_rows, weight = call(
        routing_kernel, [SMEM] + [VMEM] * 4, [chip((SLOTS, TOK), BF), chip((TOK, SLOTS), BF)]
    )(here, *[on_chip(t) for t in tables])

    attn_rows = scatter_head(blocks)
    resid = lax.dynamic_slice_in_dim(hidden_in, head * ROWS, ROWS, 0).astype(F32) + attn_rows
    normed2 = rms_norm(resid, moe_gain).astype(BF)
    tokens = gather_head(normed2)

    sent = call(
        dispatch_kernel, [VMEM] * 5, [out((MAIN, PACKED), BF)], [pltpu.VMEM((TOK, D), BF)]
    )(on_chip(place_rows), *[on_chip(t) for t in tokens])[0]
    received = lax.all_to_all(sent.reshape(32, 16, PACKED), "seq", 0, 0, tiled=True)
    keep = (head // 2 == core).astype(jnp.int32)[None]
    results = call(
        expert_kernel,
        [SMEM, VMEM] + [ANY] * 12,
        [out((MAIN, PACKED), BF)],
        [
            pltpu.VMEM((SLOTS, D), BF),
            pltpu.VMEM((4, 2, D, 256), BF),
            pltpu.VMEM((1024, D), BF),
            pltpu.VMEM((SLOTS, 1024), BF),
            pltpu.VMEM((64, D), F32),
            pltpu.SemaphoreType.DMA((8,)),
        ],
    )(keep, on_chip(received.reshape(MAIN, PACKED)), *[p[0] for p in pieces], *[p[1] for p in pieces])[0]
    back = lax.all_to_all(results.reshape(32, 16, PACKED), "seq", 0, 0, tiled=True)
    blocks = call(
        combine_kernel, [VMEM] * 2, BLOCKS_OUT, [pltpu.VMEM((64, D), BF)]
    )(on_chip(weight), on_chip(back.reshape(MAIN, PACKED)))
    moe_sum = scatter_head(blocks)
    return (resid + moe_sum).astype(BF)


def solution(mesh):
    placed = (
        P("seq", None),
        P(),
        P(None, None, "head"),
        P("head"),
        P("head", None),
        P(),
        P(("seq", "head"), None),
        P(("seq", "head"), None),
        P("seq", None, None, "head"),
        P("seq", "head", None),
    )

    return jax.shard_map(
        on_device, mesh=mesh, in_specs=placed, out_specs=P(("seq", "head"), None), check_vma=False
    )
```

```python
import jax
import jax.numpy as jnp
from jax import lax
from jax.experimental import pallas as pl
from jax.experimental.pallas import tpu as pltpu
from jax.sharding import PartitionSpec as P

D = 2048
DH = 128
HEADS = 4
WIDE = HEADS * DH
TOP = 8
CAP = 9
ROWS = 64
TOK = 256
MAIN = 512
SLOTS = 576
PACKED = D + 256
EPSILON = 1e-06
BF = jnp.bfloat16
F32 = jnp.float32


VMEM = pl.BlockSpec(memory_space=pltpu.VMEM)
SMEM = pl.BlockSpec(memory_space=pltpu.SMEM)
ANY = pl.BlockSpec(memory_space=pl.ANY)
HBM = pl.BlockSpec(memory_space=pltpu.HBM)


def on_chip(array):
    return pltpu.with_memory_space_constraint(array, pltpu.VMEM)


def out(shape, dtype):
    return jax.ShapeDtypeStruct(shape, dtype)


def chip(shape, dtype):
    return pltpu.VMEM(shape, dtype)


def spec_of(o):
    if o.dtype == jnp.int32:
        return SMEM
    return HBM if o in QUARTER else VMEM


def call(kernel, ins, outs, scratch=(), limit=54):
    return pl.pallas_call(
        kernel,
        in_specs=ins,
        out_specs=[spec_of(o) for o in outs],
        out_shape=outs,
        scratch_shapes=list(scratch),
        compiler_params=pltpu.CompilerParams(vmem_limit_bytes=limit << 20),
    )


def rms_norm(values, gain):
    mean_square = jnp.mean(values * values, axis=-1, keepdims=True)
    return values * lax.rsqrt(mean_square + EPSILON) * gain


def dot(first, second):
    return jnp.dot(first, second, preferred_element_type=F32)


def dot_rows(first, second):
    return lax.dot_general(first, second, (((0,), (0,)), ((), ())), preferred_element_type=F32)


def dot_cols(first, second):
    return lax.dot_general(first, second, (((1,), (1,)), ((), ())), preferred_element_type=F32)


def of_head(h):
    return slice(h * DH, (h + 1) * DH)


def pick_copies(index_ref, gu_ref, dn_ref, gu_out, dn_out, gu_buf, dn_buf, read_sems, write_sems):
    index = index_ref[0]
    reads = []
    writes = []
    for half in range(2):
        for part in range(2):
            rows = pl.ds(part * (D // 2), D // 2)
            reads.append((gu_ref.at[index, half, rows], gu_buf.at[half, rows]))
            writes.append((gu_buf.at[half, rows], gu_out.at[half, rows]))
        rows = pl.ds(half * 128, 128)
        reads.append((dn_ref.at[index, rows], dn_buf.at[rows]))
        writes.append((dn_buf.at[rows], dn_out.at[rows]))
    return (
        [pltpu.make_async_copy(a, b, read_sems.at[i]) for i, (a, b) in enumerate(reads)],
        [pltpu.make_async_copy(a, b, write_sems.at[i]) for i, (a, b) in enumerate(writes)],
    )


def front_kernel(
    index_ref, x_ref, gain_ref, w_ref, gu_ref, dn_ref,
    normed_ref, k_ref, v_ref, send_ref, zero_ref, gu_out, dn_out,
    wk, wv, sems, gu_buf, dn_buf, read_sems, write_sems,
):
    copy_k = pltpu.make_async_copy(w_ref.at[1], wk, sems.at[0])
    copy_v = pltpu.make_async_copy(w_ref.at[2], wv, sems.at[1])
    copy_k.start()
    copy_v.start()
    reads, writes = pick_copies(
        index_ref, gu_ref, dn_ref, gu_out, dn_out, gu_buf, dn_buf, read_sems, write_sems
    )
    for read in reads:
        read.start()
    zero_ref[0] = 0
    normed = rms_norm(x_ref[...].astype(F32), gain_ref[...]).astype(BF)
    normed_ref[...] = normed
    copy_k.wait()
    key = dot(normed, wk[...]).astype(BF)
    k_ref[...] = key
    copy_v.wait()
    for read, write in zip(reads, writes):
        read.wait()
        write.start()
    value = dot(normed, wv[...]).astype(BF)
    v_ref[...] = value
    for h in range(HEADS):
        state = dot_rows(key[:, of_head(h)], value[:, of_head(h)])
        send_ref[of_head(h), :] = state.astype(BF)
    for write in writes:
        write.wait()


def prefix_kernel(states_ref, out_ref):
    total = jnp.zeros((16, DH), F32)
    for s in range(32):
        out_ref[s] = total.astype(BF)
        total = total + states_ref[s].astype(F32)


def local_kernel(normed_ref, w_ref, k_ref, v_ref, q_ref, local_ref, wq, sems):
    copy_q = pltpu.make_async_copy(w_ref.at[0], wq, sems.at[0])
    copy_q.start()
    row = lax.broadcasted_iota(jnp.int32, (TOK, TOK), 0)
    causal = lax.broadcasted_iota(jnp.int32, (TOK, TOK), 1) <= row
    copy_q.wait()
    query = dot(normed_ref[...], wq[...]).astype(BF)
    q_ref[...] = query
    for h in range(HEADS):
        scores = dot_cols(query[:, of_head(h)], k_ref[:, of_head(h)])
        scores = jnp.where(causal, scores, 0.0).astype(BF)
        local_ref[:, of_head(h)] = dot(scores, v_ref[:, of_head(h)])


def attend_kernel(
    head_ref, earlier_ref, q_ref, local_ref, gain_ref, w_ref,
    own_ref, s1, s2, s3, mixed_ref, turned_ref,
):
    head = head_ref[0]
    for h in range(HEADS):
        attended = local_ref[:, of_head(h)] + dot(q_ref[:, of_head(h)], earlier_ref[of_head(h), :])
        mixed_ref[:, of_head(h)] = rms_norm(attended, gain_ref[:, of_head(h)]).astype(BF)
    for k in range(4):
        start = pl.multiple_of(((head - k) % 4) * ROWS, ROWS)
        turned_ref[k * ROWS:(k + 1) * ROWS, :] = mixed_ref[pl.ds(start, ROWS), :]
    for n in range(4):
        cols = slice(n * 512, (n + 1) * 512)
        rows = dot(turned_ref[...], w_ref[:, cols])
        own_ref[:, cols] = rows[:ROWS]
        s3[:, cols] = rows[ROWS:2 * ROWS].astype(BF)
        s2[:, cols] = rows[2 * ROWS:3 * ROWS].astype(BF)
        s1[:, cols] = rows[3 * ROWS:].astype(BF)


def routing_kernel(head_ref, t0, t1, t2, t3, place_ref, weight_ref):
    head = head_ref[0]
    tables = jnp.concatenate([t0[...], t1[...], t2[...], t3[...]], axis=0)
    wanted = lax.broadcasted_iota(jnp.int32, (TOK, 16), 1) * 4 + head
    chosen = jnp.zeros((TOK, 16), F32)
    gates = jnp.zeros((TOK, 16), F32)
    for k in range(TOP):
        hit = tables[:, k:k + 1].astype(jnp.int32) == wanted
        chosen = chosen + hit.astype(F32)
        gates = gates + jnp.where(hit, tables[:, TOP + k:TOP + k + 1], 0.0)
    row = lax.broadcasted_iota(jnp.int32, (TOK, TOK), 0)
    col = lax.broadcasted_iota(jnp.int32, (TOK, TOK), 1)
    before = ((row // ROWS == col // ROWS) & (col < row)).astype(F32).astype(BF)
    rank = dot(before, chosen.astype(BF))
    block = (head - lax.broadcasted_iota(jnp.int32, (TOK, 16), 0) // ROWS) & 3
    base = ((block >> 1) * 18 + (block & 1) * CAP).astype(F32)
    slot = jnp.where(chosen > 0, base + rank, -1.0).astype(BF)

    def of_row(shape, axis):
        row = lax.broadcasted_iota(jnp.int32, shape, axis)
        is_main = row < MAIN
        chip = jnp.where(is_main, row >> 5, (row & 31) >> 1)
        core = jnp.where(is_main, (row >> 4) & 1, row & 1)
        within = jnp.where(is_main, row & 15, 16 + ((row - MAIN) >> 5))
        return chip, (core * 18 + within).astype(F32)

    chip, want = of_row((SLOTS, 16), 0)
    spread = (chip == lax.broadcasted_iota(jnp.int32, (SLOTS, 16), 1)).astype(F32).astype(BF)
    place_ref[...] = (dot_cols(spread, slot) == want[:, :1]).astype(F32).astype(BF)
    chip, want = of_row((16, SLOTS), 1)
    spread = (chip == lax.broadcasted_iota(jnp.int32, (16, SLOTS), 0)).astype(F32).astype(BF)
    at_row = dot(slot, spread) == want[:1, :]
    weight_ref[...] = jnp.where(at_row, dot(gates.astype(BF), spread), 0.0).astype(BF)


def dispatch_kernel(place_ref, t0, t1, t2, t3, out_ref, tokens):
    for k, ref in enumerate((t0, t1, t2, t3)):
        tokens[k * ROWS:(k + 1) * ROWS, :] = ref[...]
    tail = []
    for n in range(4):
        cols = slice(n * 512, (n + 1) * 512)
        rows = dot(place_ref[...], tokens[:, cols])
        out_ref[:, cols] = rows[:MAIN].astype(BF)
        tail.append(rows[MAIN:])
    tail = jnp.concatenate(tail, axis=1)
    for t in range(2):
        piece = tail[t * 32:(t + 1) * 32].reshape(MAIN, 128).astype(BF)
        out_ref[:, D + t * 128:D + (t + 1) * 128] = piece


def start_quarters(keep_ref, arrays, dest_of, sems, first):
    def load(q, ref):
        return pltpu.make_async_copy(ref, dest_of(q), sems.at[first + q])

    keep = keep_ref[0] == 1
    copies = [load(0, arrays[0]), load(1, arrays[1])]
    copies[0].start()
    copies[1].start()

    @pl.when(keep)
    def _():
        load(2, arrays[2]).start()
        load(3, arrays[5]).start()

    @pl.when(jnp.logical_not(keep))
    def _():
        load(2, arrays[3]).start()
        load(3, arrays[4]).start()

    return copies + [load(2, arrays[2]), load(3, arrays[4])]


def gate_kernel(keep_ref, x_ref, gu0, gu1, gu2, gu3, gu4, gu5, act_ref, rows, gate_up, sems):
    copies = start_quarters(
        keep_ref, (gu0, gu1, gu2, gu3, gu4, gu5), lambda q: gate_up.at[q], sems, 0
    )
    rows[:MAIN, :] = x_ref[:, :D]
    for t in range(2):
        piece = x_ref[:, D + t * 128:D + (t + 1) * 128].astype(F32).reshape(32, D)
        rows[MAIN + t * 32:MAIN + (t + 1) * 32, :] = piece.astype(BF)
    for q in range(4):
        copies[q].wait()
        gate = dot(rows[...], gate_up[q, 0])
        up = dot(rows[...], gate_up[q, 1])
        act_ref[:, q * 256:(q + 1) * 256] = (jax.nn.silu(gate) * up).astype(BF)


def down_kernel(keep_ref, act, dn0, dn1, dn2, dn3, dn4, dn5, out_ref, down, tail, sems):
    copies = []
    for n in range(4):
        cols = slice(n * 512, (n + 1) * 512)
        copies.append(
            start_quarters(
                keep_ref,
                [dn.at[:, cols] for dn in (dn0, dn1, dn2, dn3, dn4, dn5)],
                lambda q: down.at[q * 256:(q + 1) * 256, cols],
                sems,
                4 * n,
            )
        )
    for n in range(4):
        cols = slice(n * 512, (n + 1) * 512)
        for copy in copies[n]:
            copy.wait()
        result = dot(act[...], down[:, cols])
        out_ref[:, cols] = result[:MAIN].astype(BF)
        tail[:, cols] = result[MAIN:]
    for t in range(2):
        piece = tail[t * 32:(t + 1) * 32, :].reshape(MAIN, 128).astype(BF)
        out_ref[:, D + t * 128:D + (t + 1) * 128] = piece


def combine_kernel(weight_ref, y_ref, own_ref, s1, s2, s3, tail):
    for t in range(2):
        piece = y_ref[:, D + t * 128:D + (t + 1) * 128].astype(F32).reshape(32, D)
        tail[t * 32:(t + 1) * 32, :] = piece.astype(BF)
    for n in range(4):
        cols = slice(n * 512, (n + 1) * 512)
        rows = dot(weight_ref[:, :MAIN], y_ref[:, cols]) + dot(weight_ref[:, MAIN:], tail[:, cols])
        own_ref[:, cols] = rows[:ROWS]
        s3[:, cols] = rows[ROWS:2 * ROWS].astype(BF)
        s2[:, cols] = rows[2 * ROWS:3 * ROWS].astype(BF)
        s1[:, cols] = rows[3 * ROWS:].astype(BF)


BLOCKS_OUT = [out((ROWS, D), F32)] + [out((ROWS, D), BF)] * 3


def seq_perm(dy, dz, dc):
    return [
        ((y * 4 + z) * 2 + c, (((y + dy) % 4) * 4 + (z + dz) % 4) * 2 + (c ^ dc))
        for y in range(4)
        for z in range(4)
        for c in range(2)
    ]


def head_perm(shift):
    return [(h, (h + shift) % 4) for h in range(4)]


def device_perm(target):
    pairs = []
    for chip in range(16):
        for c in range(2):
            for h in range(4):
                to = target(c, h)
                if to is None:
                    continue
                pairs.append(((chip * 2 + c) * 4 + h, (chip * 2 + to[0]) * 4 + to[1]))
    return pairs


def near_target(c, h):
    chip = 2 * c + 1 - (h & 1)
    return (c, chip) if (chip - 1) % 4 == h else (1 - c, chip)


def far_target(c, h):
    return None if h // 2 == c else (1 - c, (h + 2) % 4)


def keep_target(c, h):
    return (1 - c, h) if h // 2 == c else None


def pass_target(c, h):
    return None if h // 2 == c else (1 - c, h)


def permute_all(arrays, axes, perm):
    return [lax.ppermute(a, axes, perm) for a in arrays]


def pick_kernel(*refs):
    reads, writes = pick_copies(*refs)
    for read in reads:
        read.start()
    for read, write in zip(reads, writes):
        read.wait()
        write.start()
    for write in writes:
        write.wait()


QUARTER = [out((2, D, 256), BF), out((256, D), BF)]
PICK_SCRATCH = [
    pltpu.VMEM((2, D, 256), BF),
    pltpu.VMEM((256, D), BF),
    pltpu.SemaphoreType.DMA((6,)),
    pltpu.SemaphoreType.DMA((6,)),
]


def pick(w_gate_up, w_down, index):
    return pl.pallas_call(
        pick_kernel,
        in_specs=[SMEM, HBM, HBM],
        out_specs=[HBM, HBM],
        out_shape=QUARTER,
        scratch_shapes=PICK_SCRATCH,
        compiler_params=pltpu.CompilerParams(vmem_limit_bytes=50 << 20),
        name="pick",
    )(index.astype(jnp.int32)[None], w_gate_up, w_down)


def gather_head(array):
    return [array] + [lax.ppermute(array, "head", head_perm(k)) for k in range(1, 4)]


def scatter_head(blocks):
    total = blocks[0]
    for k in range(1, 4):
        total = total + lax.ppermute(blocks[k], "head", head_perm(k)).astype(F32)
    return total


def on_device(
    hidden_in, attn_gain, w_qkv, out_gain, w_out, moe_gain, routes, gate_weights, w_gate_up, w_down
):
    seq = lax.axis_index("seq")
    head = lax.axis_index("head")
    core = seq % 2

    w_planes = w_qkv.transpose(1, 0, 2)
    normed, key, value, send_state, zero, *near = call(
        front_kernel,
        [SMEM, VMEM, VMEM, HBM, HBM, HBM],
        [
            chip((TOK, D), BF),
            chip((TOK, WIDE), BF),
            chip((TOK, WIDE), BF),
            out((WIDE, DH), BF),
            out((1,), jnp.int32),
        ]
        + QUARTER,
        [pltpu.VMEM((D, WIDE), BF), pltpu.VMEM((D, WIDE), BF), pltpu.SemaphoreType.DMA((2,))]
        + PICK_SCRATCH,
    )(
        (1 - (head & 1)).astype(jnp.int32)[None],
        hidden_in,
        attn_gain[None, :],
        w_planes,
        w_gate_up,
        w_down,
    )
    both = ("seq", "head")
    near = permute_all(near, both, device_perm(near_target))
    states = lax.all_to_all(send_state.reshape(32, 16, DH), "seq", 0, 0, tiled=True)
    sums = call(prefix_kernel, [VMEM], [out((32, 16, DH), BF)])(on_chip(states))[0]
    earlier = lax.all_to_all(sums, "seq", 0, 0, tiled=True).reshape(WIDE, DH)
    odd = (head & 1) + zero[0]
    rest = pick(w_gate_up, w_down, odd)
    far_down = lax.ppermute(rest[1], both, device_perm(far_target))
    far = [lax.ppermute(rest[0], both, device_perm(far_target)), far_down]
    rest_other = permute_all(rest, both, device_perm(keep_target))
    near_other = permute_all(near, "seq", seq_perm(0, 0, 1))
    far_other = [lax.ppermute(far[0], both, device_perm(pass_target))]
    far_other.append(lax.ppermute(far[1], both, device_perm(pass_target)))
    pieces = [near, near_other, rest, rest_other, far, far_other]

    query, local = call(
        local_kernel,
        [VMEM, HBM, VMEM, VMEM],
        [out((TOK, WIDE), BF), chip((TOK, WIDE), F32)],
        [pltpu.VMEM((D, WIDE), BF), pltpu.SemaphoreType.DMA((1,))],
    )(on_chip(normed), w_planes, on_chip(key), on_chip(value))
    here = head.astype(jnp.int32)[None]
    blocks = call(
        attend_kernel,
        [SMEM] + [VMEM] * 5,
        BLOCKS_OUT,
        [pltpu.VMEM((TOK, WIDE), BF), pltpu.VMEM((TOK, WIDE), BF)],
    )(here, on_chip(earlier), query, on_chip(local), out_gain[None, :], w_out)
    tables = gather_head(jnp.concatenate([routes.astype(F32), gate_weights], axis=1))
    place_rows, weight = call(
        routing_kernel, [SMEM] + [VMEM] * 4, [chip((SLOTS, TOK), BF), chip((TOK, SLOTS), BF)]
    )(here, *[on_chip(t) for t in tables])

    attn_rows = scatter_head(blocks)
    resid = lax.dynamic_slice_in_dim(hidden_in, head * ROWS, ROWS, 0).astype(F32) + attn_rows
    normed2 = rms_norm(resid, moe_gain).astype(BF)
    tokens = gather_head(normed2)

    sent = call(
        dispatch_kernel, [VMEM] * 5, [out((MAIN, PACKED), BF)], [pltpu.VMEM((TOK, D), BF)]
    )(on_chip(place_rows), *[on_chip(t) for t in tokens])[0]
    received = lax.all_to_all(sent.reshape(32, 16, PACKED), "seq", 0, 0, tiled=True)
    keep = (head // 2 == core).astype(jnp.int32)[None]
    act = call(
        gate_kernel,
        [SMEM, VMEM] + [ANY] * 6,
        [chip((SLOTS, 1024), BF)],
        [
            pltpu.VMEM((SLOTS, D), BF),
            pltpu.VMEM((4, 2, D, 256), BF),
            pltpu.SemaphoreType.DMA((4,)),
        ],
    )(keep, on_chip(received.reshape(MAIN, PACKED)), *[p[0] for p in pieces])[0]
    results = call(
        down_kernel,
        [SMEM, VMEM] + [ANY] * 6,
        [out((MAIN, PACKED), BF)],
        [
            pltpu.VMEM((1024, D), BF),
            pltpu.VMEM((64, D), F32),
            pltpu.SemaphoreType.DMA((16,)),
        ],
    )(keep, on_chip(act), *[p[1] for p in pieces])[0]
    back = lax.all_to_all(results.reshape(32, 16, PACKED), "seq", 0, 0, tiled=True)
    blocks = call(
        combine_kernel, [VMEM] * 2, BLOCKS_OUT, [pltpu.VMEM((64, D), BF)]
    )(on_chip(weight), on_chip(back.reshape(MAIN, PACKED)))
    moe_sum = scatter_head(blocks)
    return (resid + moe_sum).astype(BF)


def solution(mesh):
    placed = (
        P("seq", None),
        P(),
        P(None, None, "head"),
        P("head"),
        P("head", None),
        P(),
        P(("seq", "head"), None),
        P(("seq", "head"), None),
        P("seq", None, None, "head"),
        P("seq", "head", None),
    )

    return jax.shard_map(
        on_device, mesh=mesh, in_specs=placed, out_specs=P(("seq", "head"), None), check_vma=False
    )
```

```python
import jax
import jax.numpy as jnp
from jax import lax
from jax.experimental import pallas as pl
from jax.experimental.pallas import tpu as pltpu
from jax.sharding import PartitionSpec as P

D = 2048
DH = 128
HEADS = 4
WIDE = HEADS * DH
TOP = 8
CAP = 9
ROWS = 64
TOK = 256
MAIN = 512
SLOTS = 576
PACKED = D + 256
EPSILON = 1e-06
BF = jnp.bfloat16
F32 = jnp.float32


VMEM = pl.BlockSpec(memory_space=pltpu.VMEM)
SMEM = pl.BlockSpec(memory_space=pltpu.SMEM)
ANY = pl.BlockSpec(memory_space=pl.ANY)
HBM = pl.BlockSpec(memory_space=pltpu.HBM)


def on_chip(array):
    return pltpu.with_memory_space_constraint(array, pltpu.VMEM)


def out(shape, dtype):
    return jax.ShapeDtypeStruct(shape, dtype)


def chip(shape, dtype):
    return pltpu.VMEM(shape, dtype)


def spec_of(o, direct):
    if o.dtype == jnp.int32:
        return SMEM
    return HBM if o in direct else VMEM


def call(kernel, ins, outs, scratch=(), limit=54, direct=()):
    return pl.pallas_call(
        kernel,
        in_specs=ins,
        out_specs=[spec_of(o, direct) for o in outs],
        out_shape=outs,
        scratch_shapes=list(scratch),
        compiler_params=pltpu.CompilerParams(vmem_limit_bytes=limit << 20),
    )


def rms_norm(values, gain):
    mean_square = jnp.mean(values * values, axis=-1, keepdims=True)
    return values * lax.rsqrt(mean_square + EPSILON) * gain


def dot(first, second):
    return jnp.dot(first, second, preferred_element_type=F32)


def dot_rows(first, second):
    return lax.dot_general(first, second, (((0,), (0,)), ((), ())), preferred_element_type=F32)


def dot_cols(first, second):
    return lax.dot_general(first, second, (((1,), (1,)), ((), ())), preferred_element_type=F32)


def of_head(h):
    return slice(h * DH, (h + 1) * DH)


def pick_copies(index_ref, gu_ref, dn_ref, gu_buf, dn_buf, sems):
    index = index_ref[0]
    copies = []
    for half in range(2):
        for part in range(2):
            rows = pl.ds(part * (D // 2), D // 2)
            copies.append((gu_ref.at[index, half, rows], gu_buf.at[half, rows]))
        rows = pl.ds(half * 128, 128)
        copies.append((dn_ref.at[index, rows], dn_buf.at[rows]))
    return [pltpu.make_async_copy(a, b, sems.at[i]) for i, (a, b) in enumerate(copies)]


def front_kernel(
    index_ref, x_ref, gain_ref, w_ref, gu_ref, dn_ref,
    normed_ref, k_ref, v_ref, send_ref, zero_ref, gu_out, dn_out,
    wk, wv, sems, read_sems,
):
    copy_k = pltpu.make_async_copy(w_ref.at[1], wk, sems.at[0])
    copy_v = pltpu.make_async_copy(w_ref.at[2], wv, sems.at[1])
    copy_k.start()
    copy_v.start()
    reads = pick_copies(index_ref, gu_ref, dn_ref, gu_out, dn_out, read_sems)
    for read in reads:
        read.start()
    zero_ref[0] = 0
    normed = rms_norm(x_ref[...].astype(F32), gain_ref[...]).astype(BF)
    normed_ref[...] = normed
    copy_k.wait()
    key = dot(normed, wk[...]).astype(BF)
    k_ref[...] = key
    copy_v.wait()
    value = dot(normed, wv[...]).astype(BF)
    v_ref[...] = value
    for h in range(HEADS):
        state = dot_rows(key[:, of_head(h)], value[:, of_head(h)])
        send_ref[of_head(h), :] = state.astype(BF)
    for read in reads:
        read.wait()


def prefix_kernel(states_ref, out_ref):
    total = jnp.zeros((16, DH), F32)
    for s in range(32):
        out_ref[s] = total.astype(BF)
        total = total + states_ref[s].astype(F32)


def local_kernel(normed_ref, w_ref, k_ref, v_ref, q_ref, local_ref, wq, sems):
    copy_q = pltpu.make_async_copy(w_ref.at[0], wq, sems.at[0])
    copy_q.start()
    row = lax.broadcasted_iota(jnp.int32, (TOK, TOK), 0)
    causal = lax.broadcasted_iota(jnp.int32, (TOK, TOK), 1) <= row
    copy_q.wait()
    query = dot(normed_ref[...], wq[...]).astype(BF)
    q_ref[...] = query
    for h in range(HEADS):
        scores = dot_cols(query[:, of_head(h)], k_ref[:, of_head(h)])
        scores = jnp.where(causal, scores, 0.0).astype(BF)
        local_ref[:, of_head(h)] = dot(scores, v_ref[:, of_head(h)])


def attend_kernel(
    head_ref, earlier_ref, q_ref, local_ref, gain_ref, w_ref,
    own_ref, s1, s2, s3, mixed_ref, turned_ref,
):
    head = head_ref[0]
    for h in range(HEADS):
        attended = local_ref[:, of_head(h)] + dot(q_ref[:, of_head(h)], earlier_ref[of_head(h), :])
        mixed_ref[:, of_head(h)] = rms_norm(attended, gain_ref[:, of_head(h)]).astype(BF)
    for k in range(4):
        start = pl.multiple_of(((head - k) % 4) * ROWS, ROWS)
        turned_ref[k * ROWS:(k + 1) * ROWS, :] = mixed_ref[pl.ds(start, ROWS), :]
    for n in range(4):
        cols = slice(n * 512, (n + 1) * 512)
        rows = dot(turned_ref[...], w_ref[:, cols])
        own_ref[:, cols] = rows[:ROWS]
        s3[:, cols] = rows[ROWS:2 * ROWS].astype(BF)
        s2[:, cols] = rows[2 * ROWS:3 * ROWS].astype(BF)
        s1[:, cols] = rows[3 * ROWS:].astype(BF)


def norm_kernel(head_ref, x_ref, own_ref, g1, g2, g3, gain_ref, resid_ref, normed_ref, rows, sems):
    start = pl.multiple_of(head_ref[0] * ROWS, ROWS)
    copy = pltpu.make_async_copy(x_ref.at[pl.ds(start, ROWS)], rows, sems.at[0])
    copy.start()
    total = own_ref[...] + g1[...].astype(F32) + g2[...].astype(F32) + g3[...].astype(F32)
    copy.wait()
    resid = rows[...].astype(F32) + total
    resid_ref[...] = resid
    normed_ref[...] = rms_norm(resid, gain_ref[...]).astype(BF)


def routing_kernel(head_ref, t0, t1, t2, t3, place_ref, weight_ref):
    head = head_ref[0]
    tables = jnp.concatenate([t0[...], t1[...], t2[...], t3[...]], axis=0)
    wanted = lax.broadcasted_iota(jnp.int32, (TOK, 16), 1) * 4 + head
    chosen = jnp.zeros((TOK, 16), F32)
    gates = jnp.zeros((TOK, 16), F32)
    for k in range(TOP):
        hit = tables[:, k:k + 1].astype(jnp.int32) == wanted
        chosen = chosen + hit.astype(F32)
        gates = gates + jnp.where(hit, tables[:, TOP + k:TOP + k + 1], 0.0)
    row = lax.broadcasted_iota(jnp.int32, (TOK, TOK), 0)
    col = lax.broadcasted_iota(jnp.int32, (TOK, TOK), 1)
    before = ((row // ROWS == col // ROWS) & (col < row)).astype(F32).astype(BF)
    rank = dot(before, chosen.astype(BF))
    block = (head - lax.broadcasted_iota(jnp.int32, (TOK, 16), 0) // ROWS) & 3
    base = ((block >> 1) * 18 + (block & 1) * CAP).astype(F32)
    slot = jnp.where(chosen > 0, base + rank, -1.0).astype(BF)

    def of_row(shape, axis):
        row = lax.broadcasted_iota(jnp.int32, shape, axis)
        is_main = row < MAIN
        chip = jnp.where(is_main, row >> 5, (row & 31) >> 1)
        core = jnp.where(is_main, (row >> 4) & 1, row & 1)
        within = jnp.where(is_main, row & 15, 16 + ((row - MAIN) >> 5))
        return chip, (core * 18 + within).astype(F32)

    chip, want = of_row((SLOTS, 16), 0)
    spread = (chip == lax.broadcasted_iota(jnp.int32, (SLOTS, 16), 1)).astype(F32).astype(BF)
    place_ref[...] = (dot_cols(spread, slot) == want[:, :1]).astype(F32).astype(BF)
    chip, want = of_row((16, SLOTS), 1)
    spread = (chip == lax.broadcasted_iota(jnp.int32, (16, SLOTS), 0)).astype(F32).astype(BF)
    at_row = dot(slot, spread) == want[:1, :]
    weight_ref[...] = jnp.where(at_row, dot(gates.astype(BF), spread), 0.0).astype(BF)


def dispatch_kernel(place_ref, t0, t1, t2, t3, out_ref, tokens):
    for k, ref in enumerate((t0, t1, t2, t3)):
        tokens[k * ROWS:(k + 1) * ROWS, :] = ref[...]
    tail = []
    for n in range(4):
        cols = slice(n * 512, (n + 1) * 512)
        rows = dot(place_ref[...], tokens[:, cols])
        out_ref[:, cols] = rows[:MAIN].astype(BF)
        tail.append(rows[MAIN:])
    tail = jnp.concatenate(tail, axis=1)
    for t in range(2):
        piece = tail[t * 32:(t + 1) * 32].reshape(MAIN, 128).astype(BF)
        out_ref[:, D + t * 128:D + (t + 1) * 128] = piece


def start_quarters(keep_ref, arrays, dest_of, sems, first, count=4):
    def load(q, ref):
        return pltpu.make_async_copy(ref, dest_of(q), sems.at[first + q])

    keep = keep_ref[0] == 1
    copies = [load(0, arrays[0]), load(1, arrays[1]), load(2, arrays[2])]
    copies[0].start()
    copies[1].start()

    @pl.when(keep)
    def _():
        load(2, arrays[2]).start()
        if count == 4:
            load(3, arrays[5]).start()

    @pl.when(jnp.logical_not(keep))
    def _():
        load(2, arrays[3]).start()
        if count == 4:
            load(3, arrays[4]).start()

    return copies + ([load(3, arrays[4])] if count == 4 else [])


def gate_kernel(
    keep_ref, x_ref, gu0, gu1, gu2, gu3, gu4, gu5, dn0, dn1, dn2, dn3,
    act_ref, down_ref, rows, gate_up, sems,
):
    copies = start_quarters(
        keep_ref, (gu0, gu1, gu2, gu3, gu4, gu5), lambda q: gate_up.at[q], sems, 0
    )
    down_copies = start_quarters(
        keep_ref,
        (dn0, dn1, dn2, dn3),
        lambda q: down_ref.at[q * 256:(q + 1) * 256],
        sems,
        4,
        3,
    )
    rows[:MAIN, :] = x_ref[:, :D]
    for t in range(2):
        piece = x_ref[:, D + t * 128:D + (t + 1) * 128].astype(F32).reshape(32, D)
        rows[MAIN + t * 32:MAIN + (t + 1) * 32, :] = piece.astype(BF)
    for q in range(4):
        copies[q].wait()
        gate = dot(rows[...], gate_up[q, 0])
        up = dot(rows[...], gate_up[q, 1])
        act_ref[:, q * 256:(q + 1) * 256] = (jax.nn.silu(gate) * up).astype(BF)
    for copy in down_copies:
        copy.wait()


def down_kernel(keep_ref, act, down, dn4, dn5, out_ref, last, main, tail, ends, sems):
    keep = keep_ref[0] == 1

    @pl.when(keep)
    def _():
        pltpu.make_async_copy(dn5, last, sems.at[0]).start()

    @pl.when(jnp.logical_not(keep))
    def _():
        pltpu.make_async_copy(dn4, last, sems.at[0]).start()

    writes = []
    for n in range(4):
        cols = slice(n * 512, (n + 1) * 512)
        result = dot(act[:, :768], down[:, cols])
        if n == 0:
            pltpu.make_async_copy(dn4, last, sems.at[0]).wait()
        result = result + dot(act[:, 768:], last[:, cols])
        main[:, cols] = result[:MAIN].astype(BF)
        tail[:, cols] = result[MAIN:]
        write = pltpu.make_async_copy(main.at[:, cols], out_ref.at[:, cols], sems.at[1 + n])
        write.start()
        writes.append(write)
    for t in range(2):
        piece = tail[t * 32:(t + 1) * 32, :].reshape(MAIN, 128).astype(BF)
        ends[:, t * 128:(t + 1) * 128] = piece
    write = pltpu.make_async_copy(ends, out_ref.at[:, D:], sems.at[5])
    write.start()
    for write in writes + [write]:
        write.wait()


def combine_kernel(weight_ref, y_ref, own_ref, s1, s2, s3, tail):
    for t in range(2):
        piece = y_ref[:, D + t * 128:D + (t + 1) * 128].astype(F32).reshape(32, D)
        tail[t * 32:(t + 1) * 32, :] = piece.astype(BF)
    for n in range(4):
        cols = slice(n * 512, (n + 1) * 512)
        rows = dot(weight_ref[:, :MAIN], y_ref[:, cols]) + dot(weight_ref[:, MAIN:], tail[:, cols])
        own_ref[:, cols] = rows[:ROWS]
        s3[:, cols] = rows[ROWS:2 * ROWS].astype(BF)
        s2[:, cols] = rows[2 * ROWS:3 * ROWS].astype(BF)
        s1[:, cols] = rows[3 * ROWS:].astype(BF)


BLOCKS_OUT = [out((ROWS, D), F32)] + [out((ROWS, D), BF)] * 3


def seq_perm(dy, dz, dc):
    return [
        ((y * 4 + z) * 2 + c, (((y + dy) % 4) * 4 + (z + dz) % 4) * 2 + (c ^ dc))
        for y in range(4)
        for z in range(4)
        for c in range(2)
    ]


def head_perm(shift):
    return [(h, (h + shift) % 4) for h in range(4)]


def device_perm(target):
    pairs = []
    for chip in range(16):
        for c in range(2):
            for h in range(4):
                to = target(c, h)
                if to is None:
                    continue
                pairs.append(((chip * 2 + c) * 4 + h, (chip * 2 + to[0]) * 4 + to[1]))
    return pairs


def near_target(c, h):
    chip = 2 * c + 1 - (h & 1)
    return (c, chip) if (chip - 1) % 4 == h else (1 - c, chip)


def far_target(c, h):
    return None if h // 2 == c else (1 - c, (h + 2) % 4)


def keep_target(c, h):
    return (1 - c, h) if h // 2 == c else None


def pass_target(c, h):
    return None if h // 2 == c else (1 - c, h)


def permute_all(arrays, axes, perm):
    return [lax.ppermute(a, axes, perm) for a in arrays]


def pick_kernel(index_ref, gu_ref, dn_ref, gu_out, dn_out, gu_buf, dn_buf, read_sems, write_sems):
    reads = pick_copies(index_ref, gu_ref, dn_ref, gu_buf, dn_buf, read_sems)
    writes = []
    for half in range(2):
        for part in range(2):
            rows = pl.ds(part * (D // 2), D // 2)
            writes.append((gu_buf.at[half, rows], gu_out.at[half, rows]))
        rows = pl.ds(half * 128, 128)
        writes.append((dn_buf.at[rows], dn_out.at[rows]))
    writes = [pltpu.make_async_copy(a, b, write_sems.at[i]) for i, (a, b) in enumerate(writes)]
    for read in reads:
        read.start()
    for read, write in zip(reads, writes):
        read.wait()
        write.start()
    for write in writes:
        write.wait()


QUARTER = [out((2, D, 256), BF), out((256, D), BF)]
RESULTS = out((MAIN, PACKED), BF)
PICK_SCRATCH = [
    pltpu.VMEM((2, D, 256), BF),
    pltpu.VMEM((256, D), BF),
    pltpu.SemaphoreType.DMA((6,)),
    pltpu.SemaphoreType.DMA((6,)),
]


def pick(w_gate_up, w_down, index):
    return pl.pallas_call(
        pick_kernel,
        in_specs=[SMEM, HBM, HBM],
        out_specs=[HBM, HBM],
        out_shape=QUARTER,
        scratch_shapes=PICK_SCRATCH,
        compiler_params=pltpu.CompilerParams(vmem_limit_bytes=50 << 20),
        name="pick",
    )(index.astype(jnp.int32)[None], w_gate_up, w_down)


def gather_head(array):
    return [array] + [lax.ppermute(array, "head", head_perm(k)) for k in range(1, 4)]


def scatter_head(blocks):
    total = blocks[0]
    for k in range(1, 4):
        total = total + lax.ppermute(blocks[k], "head", head_perm(k)).astype(F32)
    return total


def on_device(
    hidden_in, attn_gain, w_qkv, out_gain, w_out, moe_gain, routes, gate_weights, w_gate_up, w_down
):
    seq = lax.axis_index("seq")
    head = lax.axis_index("head")
    core = seq % 2

    w_planes = w_qkv.transpose(1, 0, 2)
    normed, key, value, send_state, zero, *near = call(
        front_kernel,
        [SMEM, VMEM, VMEM, HBM, HBM, HBM],
        [
            chip((TOK, D), BF),
            chip((TOK, WIDE), BF),
            chip((TOK, WIDE), BF),
            out((WIDE, DH), BF),
            out((1,), jnp.int32),
            chip((2, D, 256), BF),
            chip((256, D), BF),
        ],
        [
            pltpu.VMEM((D, WIDE), BF),
            pltpu.VMEM((D, WIDE), BF),
            pltpu.SemaphoreType.DMA((2,)),
            pltpu.SemaphoreType.DMA((6,)),
        ],
    )(
        (1 - (head & 1)).astype(jnp.int32)[None],
        hidden_in,
        attn_gain[None, :],
        w_planes,
        w_gate_up,
        w_down,
    )
    both = ("seq", "head")
    near = permute_all(near, both, device_perm(near_target))
    states = lax.all_to_all(send_state.reshape(32, 16, DH), "seq", 0, 0, tiled=True)
    sums = call(prefix_kernel, [VMEM], [out((32, 16, DH), BF)])(on_chip(states))[0]
    earlier = lax.all_to_all(sums, "seq", 0, 0, tiled=True).reshape(WIDE, DH)
    odd = (head & 1) + zero[0]
    rest = pick(w_gate_up, w_down, odd)
    far_down = lax.ppermute(rest[1], both, device_perm(far_target))
    far = [lax.ppermute(rest[0], both, device_perm(far_target)), far_down]
    rest_other = permute_all(rest, both, device_perm(keep_target))
    near_other = permute_all(near, "seq", seq_perm(0, 0, 1))
    far_other = [lax.ppermute(far[0], both, device_perm(pass_target))]
    far_other.append(lax.ppermute(far[1], both, device_perm(pass_target)))
    pieces = [near, near_other, rest, rest_other, far, far_other]

    query, local = call(
        local_kernel,
        [VMEM, HBM, VMEM, VMEM],
        [out((TOK, WIDE), BF), chip((TOK, WIDE), F32)],
        [pltpu.VMEM((D, WIDE), BF), pltpu.SemaphoreType.DMA((1,))],
    )(on_chip(normed), w_planes, on_chip(key), on_chip(value))
    here = head.astype(jnp.int32)[None]
    blocks = call(
        attend_kernel,
        [SMEM] + [VMEM] * 5,
        [chip((ROWS, D), F32)] + BLOCKS_OUT[1:],
        [pltpu.VMEM((TOK, WIDE), BF), pltpu.VMEM((TOK, WIDE), BF)],
    )(here, on_chip(earlier), query, on_chip(local), out_gain[None, :], w_out)
    tables = gather_head(jnp.concatenate([routes.astype(F32), gate_weights], axis=1))
    place_rows, weight = call(
        routing_kernel, [SMEM] + [VMEM] * 4, [chip((SLOTS, TOK), BF), chip((TOK, SLOTS), BF)]
    )(here, *[on_chip(t) for t in tables])

    got = [lax.ppermute(blocks[k], "head", head_perm(k)) for k in range(1, 4)]
    resid, normed2 = call(
        norm_kernel,
        [SMEM, HBM] + [VMEM] * 5,
        [out((ROWS, D), F32), chip((ROWS, D), BF)],
        [pltpu.VMEM((ROWS, D), BF), pltpu.SemaphoreType.DMA((1,))],
    )(here, hidden_in, on_chip(blocks[0]), *[on_chip(g) for g in got], moe_gain[None, :])
    tokens = gather_head(normed2)

    sent = call(
        dispatch_kernel, [VMEM] * 5, [out((MAIN, PACKED), BF)], [pltpu.VMEM((TOK, D), BF)]
    )(on_chip(place_rows), *[on_chip(t) for t in tokens])[0]
    received = lax.all_to_all(sent.reshape(32, 16, PACKED), "seq", 0, 0, tiled=True)
    keep = (head // 2 == core).astype(jnp.int32)[None]
    gate_ups = [p[0] for p in pieces]
    downs = [p[1] for p in pieces]
    act, down = call(
        gate_kernel,
        [SMEM, VMEM] + [ANY] * 10,
        [chip((SLOTS, 1024), BF), chip((768, D), BF)],
        [
            pltpu.VMEM((SLOTS, D), BF),
            pltpu.VMEM((4, 2, D, 256), BF),
            pltpu.SemaphoreType.DMA((7,)),
        ],
    )(keep, on_chip(received.reshape(MAIN, PACKED)), *gate_ups, *downs[:4])
    results = call(
        down_kernel,
        [SMEM, VMEM, VMEM, ANY, ANY],
        [RESULTS],
        [
            pltpu.VMEM((256, D), BF),
            pltpu.VMEM((MAIN, D), BF),
            pltpu.VMEM((64, D), F32),
            pltpu.VMEM((MAIN, 256), BF),
            pltpu.SemaphoreType.DMA((6,)),
        ],
        direct=[RESULTS],
    )(keep, on_chip(act), on_chip(down), *downs[4:])[0]
    back = lax.all_to_all(results.reshape(32, 16, PACKED), "seq", 0, 0, tiled=True)
    blocks = call(
        combine_kernel, [VMEM] * 2, BLOCKS_OUT, [pltpu.VMEM((64, D), BF)]
    )(on_chip(weight), on_chip(back.reshape(MAIN, PACKED)))
    moe_sum = scatter_head(blocks)
    return (resid + moe_sum).astype(BF)


def solution(mesh):
    placed = (
        P("seq", None),
        P(),
        P(None, None, "head"),
        P("head"),
        P("head", None),
        P(),
        P(("seq", "head"), None),
        P(("seq", "head"), None),
        P("seq", None, None, "head"),
        P("seq", "head", None),
    )

    return jax.shard_map(
        on_device, mesh=mesh, in_specs=placed, out_specs=P(("seq", "head"), None), check_vma=False
    )
```

```python
import jax
import jax.numpy as jnp
from jax import lax
from jax.experimental import pallas as pl
from jax.experimental.pallas import tpu as pltpu
from jax.sharding import PartitionSpec as P

D = 2048
DH = 128
HEADS = 4
WIDE = HEADS * DH
TOP = 8
CAP = 9
ROWS = 64
TOK = 256
MAIN = 512
SLOTS = 576
PACKED = D + 256
EPSILON = 1e-06
BF = jnp.bfloat16
F32 = jnp.float32


VMEM = pl.BlockSpec(memory_space=pltpu.VMEM)
SMEM = pl.BlockSpec(memory_space=pltpu.SMEM)
ANY = pl.BlockSpec(memory_space=pl.ANY)
HBM = pl.BlockSpec(memory_space=pltpu.HBM)


def on_chip(array):
    return pltpu.with_memory_space_constraint(array, pltpu.VMEM)


def out(shape, dtype):
    return jax.ShapeDtypeStruct(shape, dtype)


def chip(shape, dtype):
    return pltpu.VMEM(shape, dtype)


def spec_of(o, direct):
    if o.dtype == jnp.int32:
        return SMEM
    return HBM if o in direct else VMEM


def call(kernel, ins, outs, scratch=(), limit=54, direct=()):
    return pl.pallas_call(
        kernel,
        in_specs=ins,
        out_specs=[spec_of(o, direct) for o in outs],
        out_shape=outs,
        scratch_shapes=list(scratch),
        compiler_params=pltpu.CompilerParams(vmem_limit_bytes=limit << 20),
    )


def rms_norm(values, gain):
    mean_square = jnp.mean(values * values, axis=-1, keepdims=True)
    return values * lax.rsqrt(mean_square + EPSILON) * gain


def dot(first, second):
    return jnp.dot(first, second, preferred_element_type=F32)


def dot_rows(first, second):
    return lax.dot_general(first, second, (((0,), (0,)), ((), ())), preferred_element_type=F32)


def dot_cols(first, second):
    return lax.dot_general(first, second, (((1,), (1,)), ((), ())), preferred_element_type=F32)


def of_head(h):
    return slice(h * DH, (h + 1) * DH)


def pick_copies(index, gu_ref, dn_ref, gu_buf, dn_buf, sems):
    copies = []
    for half in range(2):
        for part in range(2):
            rows = pl.ds(part * (D // 2), D // 2)
            copies.append((gu_ref.at[index, half, rows], gu_buf.at[half, rows]))
        rows = pl.ds(half * 128, 128)
        copies.append((dn_ref.at[index, rows], dn_buf.at[rows]))
    return [pltpu.make_async_copy(a, b, sems.at[i]) for i, (a, b) in enumerate(copies)]


def front_kernel(
    head_ref, x_ref, gain_ref, w_ref, gu_ref, dn_ref,
    normed_ref, k_ref, v_ref, send_ref, zero_ref, gu_out, dn_out, mine_ref,
    wk, wv, sems, read_sems,
):
    copy_k = pltpu.make_async_copy(w_ref.at[1], wk, sems.at[0])
    copy_v = pltpu.make_async_copy(w_ref.at[2], wv, sems.at[1])
    copy_k.start()
    copy_v.start()
    head = head_ref[0]
    reads = pick_copies(1 - (head & 1), gu_ref, dn_ref, gu_out, dn_out, read_sems)
    zero_ref[0] = 0
    mine_ref[...] = x_ref[pl.ds(pl.multiple_of(head * ROWS, ROWS), ROWS), :]
    normed = rms_norm(x_ref[...].astype(F32), gain_ref[...]).astype(BF)
    normed_ref[...] = normed
    copy_k.wait()
    copy_v.wait()
    for read in reads:
        read.start()
    key = dot(normed, wk[...]).astype(BF)
    k_ref[...] = key
    value = dot(normed, wv[...]).astype(BF)
    v_ref[...] = value
    for h in range(HEADS):
        state = dot_rows(key[:, of_head(h)], value[:, of_head(h)])
        send_ref[of_head(h), :] = state.astype(BF)
    for read in reads:
        read.wait()


def prefix_kernel(states_ref, out_ref):
    total = jnp.zeros((16, DH), F32)
    for s in range(32):
        out_ref[s] = total.astype(BF)
        total = total + states_ref[s].astype(F32)


def local_kernel(normed_ref, w_ref, k_ref, v_ref, q_ref, local_ref, wq, sems):
    copy_q = pltpu.make_async_copy(w_ref.at[0], wq, sems.at[0])
    copy_q.start()
    row = lax.broadcasted_iota(jnp.int32, (TOK, TOK), 0)
    causal = lax.broadcasted_iota(jnp.int32, (TOK, TOK), 1) <= row
    copy_q.wait()
    query = dot(normed_ref[...], wq[...]).astype(BF)
    q_ref[...] = query
    for h in range(HEADS):
        scores = dot_cols(query[:, of_head(h)], k_ref[:, of_head(h)])
        scores = jnp.where(causal, scores, 0.0).astype(BF)
        local_ref[:, of_head(h)] = dot(scores, v_ref[:, of_head(h)])


def attend_kernel(
    head_ref, earlier_ref, q_ref, local_ref, gain_ref, w_ref,
    own_ref, s1, s2, s3, mixed_ref, turned_ref,
):
    head = head_ref[0]
    for h in range(HEADS):
        attended = local_ref[:, of_head(h)] + dot(q_ref[:, of_head(h)], earlier_ref[of_head(h), :])
        mixed_ref[:, of_head(h)] = rms_norm(attended, gain_ref[:, of_head(h)]).astype(BF)
    for k in range(4):
        start = pl.multiple_of(((head - k) % 4) * ROWS, ROWS)
        turned_ref[k * ROWS:(k + 1) * ROWS, :] = mixed_ref[pl.ds(start, ROWS), :]
    for n in range(4):
        cols = slice(n * 512, (n + 1) * 512)
        rows = dot(turned_ref[...], w_ref[:, cols])
        own_ref[:, cols] = rows[:ROWS]
        s3[:, cols] = rows[ROWS:2 * ROWS].astype(BF)
        s2[:, cols] = rows[2 * ROWS:3 * ROWS].astype(BF)
        s1[:, cols] = rows[3 * ROWS:].astype(BF)


def norm_kernel(mine_ref, own_ref, g1, g2, g3, gain_ref, resid_ref, normed_ref):
    total = own_ref[...] + g1[...].astype(F32) + g2[...].astype(F32) + g3[...].astype(F32)
    resid = mine_ref[...].astype(F32) + total
    resid_ref[...] = resid
    normed_ref[...] = rms_norm(resid, gain_ref[...]).astype(BF)


def last_kernel(resid_ref, own_ref, g1, g2, g3, out_ref):
    total = own_ref[...] + g1[...].astype(F32) + g2[...].astype(F32) + g3[...].astype(F32)
    out_ref[...] = (resid_ref[...] + total).astype(BF)


def routing_kernel(head_ref, t0, t1, t2, t3, place_ref, weight_ref):
    head = head_ref[0]
    tables = jnp.concatenate([t0[...], t1[...], t2[...], t3[...]], axis=0)
    wanted = lax.broadcasted_iota(jnp.int32, (TOK, 16), 1) * 4 + head
    chosen = jnp.zeros((TOK, 16), F32)
    gates = jnp.zeros((TOK, 16), F32)
    for k in range(TOP):
        hit = tables[:, k:k + 1].astype(jnp.int32) == wanted
        chosen = chosen + hit.astype(F32)
        gates = gates + jnp.where(hit, tables[:, TOP + k:TOP + k + 1], 0.0)
    row = lax.broadcasted_iota(jnp.int32, (TOK, TOK), 0)
    col = lax.broadcasted_iota(jnp.int32, (TOK, TOK), 1)
    before = ((row // ROWS == col // ROWS) & (col < row)).astype(F32).astype(BF)
    rank = dot(before, chosen.astype(BF))
    block = (head - lax.broadcasted_iota(jnp.int32, (TOK, 16), 0) // ROWS) & 3
    base = ((block >> 1) * 18 + (block & 1) * CAP).astype(F32)
    slot = jnp.where(chosen > 0, base + rank, -1.0).astype(BF)

    def of_row(shape, axis):
        row = lax.broadcasted_iota(jnp.int32, shape, axis)
        is_main = row < MAIN
        chip = jnp.where(is_main, row >> 5, (row & 31) >> 1)
        core = jnp.where(is_main, (row >> 4) & 1, row & 1)
        within = jnp.where(is_main, row & 15, 16 + ((row - MAIN) >> 5))
        return chip, (core * 18 + within).astype(F32)

    chip, want = of_row((SLOTS, 16), 0)
    spread = (chip == lax.broadcasted_iota(jnp.int32, (SLOTS, 16), 1)).astype(F32).astype(BF)
    place_ref[...] = (dot_cols(spread, slot) == want[:, :1]).astype(F32).astype(BF)
    chip, want = of_row((16, SLOTS), 1)
    spread = (chip == lax.broadcasted_iota(jnp.int32, (16, SLOTS), 0)).astype(F32).astype(BF)
    at_row = dot(slot, spread) == want[:1, :]
    weight_ref[...] = jnp.where(at_row, dot(gates.astype(BF), spread), 0.0).astype(BF)


def dispatch_kernel(place_ref, t0, t1, t2, t3, out_ref, tokens):
    for k, ref in enumerate((t0, t1, t2, t3)):
        tokens[k * ROWS:(k + 1) * ROWS, :] = ref[...]
    tail = []
    for n in range(4):
        cols = slice(n * 512, (n + 1) * 512)
        rows = dot(place_ref[...], tokens[:, cols])
        out_ref[:, cols] = rows[:MAIN].astype(BF)
        tail.append(rows[MAIN:])
    tail = jnp.concatenate(tail, axis=1)
    for t in range(2):
        piece = tail[t * 32:(t + 1) * 32].reshape(MAIN, 128).astype(BF)
        out_ref[:, D + t * 128:D + (t + 1) * 128] = piece


def start_quarters(keep_ref, arrays, dest_of, sems, first, count=4):
    def load(q, ref):
        return pltpu.make_async_copy(ref, dest_of(q), sems.at[first + q])

    keep = keep_ref[0] == 1
    copies = [load(0, arrays[0]), load(1, arrays[1]), load(2, arrays[2])]
    copies[0].start()
    copies[1].start()

    @pl.when(keep)
    def _():
        load(2, arrays[2]).start()
        if count == 4:
            load(3, arrays[5]).start()

    @pl.when(jnp.logical_not(keep))
    def _():
        load(2, arrays[3]).start()
        if count == 4:
            load(3, arrays[4]).start()

    return copies + ([load(3, arrays[4])] if count == 4 else [])


def gate_kernel(
    keep_ref, x_ref, gu0, gu1, gu2, gu3, gu4, gu5, dn0, dn1, dn2, dn3,
    act_ref, down_ref, rows, gate_up, sems,
):
    copies = start_quarters(
        keep_ref, (gu0, gu1, gu2, gu3, gu4, gu5), lambda q: gate_up.at[q], sems, 0
    )
    down_copies = start_quarters(
        keep_ref,
        (dn0, dn1, dn2, dn3),
        lambda q: down_ref.at[q * 256:(q + 1) * 256],
        sems,
        4,
        3,
    )
    rows[:MAIN, :] = x_ref[:, :D]
    for t in range(2):
        piece = x_ref[:, D + t * 128:D + (t + 1) * 128].astype(F32).reshape(32, D)
        rows[MAIN + t * 32:MAIN + (t + 1) * 32, :] = piece.astype(BF)
    for q in range(4):
        copies[q].wait()
        gate = dot(rows[...], gate_up[q, 0])
        up = dot(rows[...], gate_up[q, 1])
        act_ref[:, q * 256:(q + 1) * 256] = (jax.nn.silu(gate) * up).astype(BF)
    for copy in down_copies:
        copy.wait()


def down_kernel(keep_ref, act, down, dn4, dn5, out_ref, last, main, tail, ends, sems):
    keep = keep_ref[0] == 1

    @pl.when(keep)
    def _():
        pltpu.make_async_copy(dn5, last, sems.at[0]).start()

    @pl.when(jnp.logical_not(keep))
    def _():
        pltpu.make_async_copy(dn4, last, sems.at[0]).start()

    writes = []
    for n in range(4):
        cols = slice(n * 512, (n + 1) * 512)
        result = dot(act[:, :768], down[:, cols])
        if n == 0:
            pltpu.make_async_copy(dn4, last, sems.at[0]).wait()
        result = result + dot(act[:, 768:], last[:, cols])
        main[:, cols] = result[:MAIN].astype(BF)
        tail[:, cols] = result[MAIN:]
        write = pltpu.make_async_copy(main.at[:, cols], out_ref.at[:, cols], sems.at[1 + n])
        write.start()
        writes.append(write)
    for t in range(2):
        piece = tail[t * 32:(t + 1) * 32, :].reshape(MAIN, 128).astype(BF)
        ends[:, t * 128:(t + 1) * 128] = piece
    write = pltpu.make_async_copy(ends, out_ref.at[:, D:], sems.at[5])
    write.start()
    for write in writes + [write]:
        write.wait()


def combine_kernel(weight_ref, y_ref, own_ref, s1, s2, s3, tail):
    for t in range(2):
        piece = y_ref[:, D + t * 128:D + (t + 1) * 128].astype(F32).reshape(32, D)
        tail[t * 32:(t + 1) * 32, :] = piece.astype(BF)
    for n in range(4):
        cols = slice(n * 512, (n + 1) * 512)
        rows = dot(weight_ref[:, :MAIN], y_ref[:, cols]) + dot(weight_ref[:, MAIN:], tail[:, cols])
        own_ref[:, cols] = rows[:ROWS]
        s3[:, cols] = rows[ROWS:2 * ROWS].astype(BF)
        s2[:, cols] = rows[2 * ROWS:3 * ROWS].astype(BF)
        s1[:, cols] = rows[3 * ROWS:].astype(BF)


BLOCKS_OUT = [out((ROWS, D), F32)] + [out((ROWS, D), BF)] * 3


def seq_perm(dy, dz, dc):
    return [
        ((y * 4 + z) * 2 + c, (((y + dy) % 4) * 4 + (z + dz) % 4) * 2 + (c ^ dc))
        for y in range(4)
        for z in range(4)
        for c in range(2)
    ]


def head_perm(shift):
    return [(h, (h + shift) % 4) for h in range(4)]


def device_perm(target):
    pairs = []
    for chip in range(16):
        for c in range(2):
            for h in range(4):
                to = target(c, h)
                if to is None:
                    continue
                pairs.append(((chip * 2 + c) * 4 + h, (chip * 2 + to[0]) * 4 + to[1]))
    return pairs


def near_target(c, h):
    chip = 2 * c + 1 - (h & 1)
    return (c, chip) if (chip - 1) % 4 == h else (1 - c, chip)


def far_target(c, h):
    return None if h // 2 == c else (1 - c, (h + 2) % 4)


def keep_target(c, h):
    return (1 - c, h) if h // 2 == c else None


def pass_target(c, h):
    return None if h // 2 == c else (1 - c, h)


def permute_all(arrays, axes, perm):
    return [lax.ppermute(a, axes, perm) for a in arrays]


def pick_kernel(index_ref, gu_ref, dn_ref, gu_out, dn_out, gu_buf, dn_buf, read_sems, write_sems):
    reads = pick_copies(index_ref[0], gu_ref, dn_ref, gu_buf, dn_buf, read_sems)
    writes = []
    for half in range(2):
        for part in range(2):
            rows = pl.ds(part * (D // 2), D // 2)
            writes.append((gu_buf.at[half, rows], gu_out.at[half, rows]))
        rows = pl.ds(half * 128, 128)
        writes.append((dn_buf.at[rows], dn_out.at[rows]))
    writes = [pltpu.make_async_copy(a, b, write_sems.at[i]) for i, (a, b) in enumerate(writes)]
    for read in reads:
        read.start()
    for read, write in zip(reads, writes):
        read.wait()
        write.start()
    for write in writes:
        write.wait()


QUARTER = [out((2, D, 256), BF), out((256, D), BF)]
RESULTS = out((MAIN, PACKED), BF)
PICK_SCRATCH = [
    pltpu.VMEM((2, D, 256), BF),
    pltpu.VMEM((256, D), BF),
    pltpu.SemaphoreType.DMA((6,)),
    pltpu.SemaphoreType.DMA((6,)),
]


def pick(w_gate_up, w_down, index):
    return pl.pallas_call(
        pick_kernel,
        in_specs=[SMEM, HBM, HBM],
        out_specs=[HBM, HBM],
        out_shape=QUARTER,
        scratch_shapes=PICK_SCRATCH,
        compiler_params=pltpu.CompilerParams(vmem_limit_bytes=50 << 20),
        name="pick",
    )(index.astype(jnp.int32)[None], w_gate_up, w_down)


def gather_head(array):
    return [array] + [lax.ppermute(array, "head", head_perm(k)) for k in range(1, 4)]


def on_device(
    hidden_in, attn_gain, w_qkv, out_gain, w_out, moe_gain, routes, gate_weights, w_gate_up, w_down
):
    seq = lax.axis_index("seq")
    head = lax.axis_index("head")
    core = seq % 2

    w_planes = w_qkv.transpose(1, 0, 2)
    here = head.astype(jnp.int32)[None]
    normed, key, value, send_state, zero, *near, mine = call(
        front_kernel,
        [SMEM, VMEM, VMEM, HBM, HBM, HBM],
        [
            chip((TOK, D), BF),
            chip((TOK, WIDE), BF),
            chip((TOK, WIDE), BF),
            out((WIDE, DH), BF),
            out((1,), jnp.int32),
            chip((2, D, 256), BF),
            chip((256, D), BF),
            out((ROWS, D), BF),
        ],
        [
            pltpu.VMEM((D, WIDE), BF),
            pltpu.VMEM((D, WIDE), BF),
            pltpu.SemaphoreType.DMA((2,)),
            pltpu.SemaphoreType.DMA((6,)),
        ],
    )(
        here,
        hidden_in,
        attn_gain[None, :],
        w_planes,
        w_gate_up,
        w_down,
    )
    both = ("seq", "head")
    near = permute_all(near, both, device_perm(near_target))
    states = lax.all_to_all(send_state.reshape(32, 16, DH), "seq", 0, 0, tiled=True)
    sums = call(prefix_kernel, [VMEM], [out((32, 16, DH), BF)])(on_chip(states))[0]
    earlier = lax.all_to_all(sums, "seq", 0, 0, tiled=True).reshape(WIDE, DH)
    odd = (head & 1) + zero[0]
    rest = pick(w_gate_up, w_down, odd)
    far_down = lax.ppermute(rest[1], both, device_perm(far_target))
    far = [lax.ppermute(rest[0], both, device_perm(far_target)), far_down]
    rest_other = permute_all(rest, both, device_perm(keep_target))
    near_other = permute_all(near, "seq", seq_perm(0, 0, 1))
    far_other = [lax.ppermute(far[0], both, device_perm(pass_target))]
    far_other.append(lax.ppermute(far[1], both, device_perm(pass_target)))
    pieces = [near, near_other, rest, rest_other, far, far_other]

    query, local = call(
        local_kernel,
        [VMEM, HBM, VMEM, VMEM],
        [out((TOK, WIDE), BF), chip((TOK, WIDE), F32)],
        [pltpu.VMEM((D, WIDE), BF), pltpu.SemaphoreType.DMA((1,))],
    )(on_chip(normed), w_planes, on_chip(key), on_chip(value))
    blocks = call(
        attend_kernel,
        [SMEM] + [VMEM] * 5,
        [chip((ROWS, D), F32)] + BLOCKS_OUT[1:],
        [pltpu.VMEM((TOK, WIDE), BF), pltpu.VMEM((TOK, WIDE), BF)],
    )(here, on_chip(earlier), query, on_chip(local), out_gain[None, :], w_out)
    tables = gather_head(jnp.concatenate([routes.astype(F32), gate_weights], axis=1))
    place_rows, weight = call(
        routing_kernel, [SMEM] + [VMEM] * 4, [chip((SLOTS, TOK), BF), chip((TOK, SLOTS), BF)]
    )(here, *[on_chip(t) for t in tables])

    got = [lax.ppermute(blocks[k], "head", head_perm(k)) for k in range(1, 4)]
    resid, normed2 = call(
        norm_kernel, [VMEM] * 6, [out((ROWS, D), F32), chip((ROWS, D), BF)]
    )(on_chip(mine), on_chip(blocks[0]), *[on_chip(g) for g in got], moe_gain[None, :])
    tokens = gather_head(normed2)

    sent = call(
        dispatch_kernel, [VMEM] * 5, [out((MAIN, PACKED), BF)], [pltpu.VMEM((TOK, D), BF)]
    )(on_chip(place_rows), *[on_chip(t) for t in tokens])[0]
    received = lax.all_to_all(sent.reshape(32, 16, PACKED), "seq", 0, 0, tiled=True)
    keep = (head // 2 == core).astype(jnp.int32)[None]
    gate_ups = [p[0] for p in pieces]
    downs = [p[1] for p in pieces]
    act, down = call(
        gate_kernel,
        [SMEM, VMEM] + [ANY] * 10,
        [chip((SLOTS, 1024), BF), chip((768, D), BF)],
        [
            pltpu.VMEM((SLOTS, D), BF),
            pltpu.VMEM((4, 2, D, 256), BF),
            pltpu.SemaphoreType.DMA((7,)),
        ],
    )(keep, on_chip(received.reshape(MAIN, PACKED)), *gate_ups, *downs[:4])
    results = call(
        down_kernel,
        [SMEM, VMEM, VMEM, ANY, ANY],
        [RESULTS],
        [
            pltpu.VMEM((256, D), BF),
            pltpu.VMEM((MAIN, D), BF),
            pltpu.VMEM((64, D), F32),
            pltpu.VMEM((MAIN, 256), BF),
            pltpu.SemaphoreType.DMA((6,)),
        ],
        direct=[RESULTS],
    )(keep, on_chip(act), on_chip(down), *downs[4:])[0]
    back = lax.all_to_all(results.reshape(32, 16, PACKED), "seq", 0, 0, tiled=True)
    blocks = call(
        combine_kernel,
        [VMEM] * 2,
        [chip((ROWS, D), F32)] + BLOCKS_OUT[1:],
        [pltpu.VMEM((64, D), BF)],
    )(on_chip(weight), on_chip(back.reshape(MAIN, PACKED)))
    got = [lax.ppermute(blocks[k], "head", head_perm(k)) for k in range(1, 4)]
    return call(last_kernel, [VMEM] * 5, [out((ROWS, D), BF)])(
        on_chip(resid), on_chip(blocks[0]), *[on_chip(g) for g in got]
    )[0]


def solution(mesh):
    placed = (
        P("seq", None),
        P(),
        P(None, None, "head"),
        P("head"),
        P("head", None),
        P(),
        P(("seq", "head"), None),
        P(("seq", "head"), None),
        P("seq", None, None, "head"),
        P("seq", "head", None),
    )

    return jax.shard_map(
        on_device, mesh=mesh, in_specs=placed, out_specs=P(("seq", "head"), None), check_vma=False
    )
```

```python
import jax
import jax.numpy as jnp
from jax import lax
from jax.experimental import pallas as pl
from jax.experimental.pallas import tpu as pltpu
from jax.sharding import PartitionSpec as P

D = 2048
DH = 128
HEADS = 4
WIDE = HEADS * DH
TOP = 8
CAP = 9
ROWS = 64
TOK = 256
MAIN = 512
SLOTS = 576
PACKED = D + 256
EPSILON = 1e-06
BF = jnp.bfloat16
F32 = jnp.float32


VMEM = pl.BlockSpec(memory_space=pltpu.VMEM)
SMEM = pl.BlockSpec(memory_space=pltpu.SMEM)
ANY = pl.BlockSpec(memory_space=pl.ANY)
HBM = pl.BlockSpec(memory_space=pltpu.HBM)


def on_chip(array):
    return pltpu.with_memory_space_constraint(array, pltpu.VMEM)


def out(shape, dtype):
    return jax.ShapeDtypeStruct(shape, dtype)


def chip(shape, dtype):
    return pltpu.VMEM(shape, dtype)


def spec_of(o, direct):
    if o.dtype == jnp.int32:
        return SMEM
    return HBM if o in direct else VMEM


def call(kernel, ins, outs, scratch=(), limit=54, direct=()):
    return pl.pallas_call(
        kernel,
        in_specs=ins,
        out_specs=[spec_of(o, direct) for o in outs],
        out_shape=outs,
        scratch_shapes=list(scratch),
        compiler_params=pltpu.CompilerParams(vmem_limit_bytes=limit << 20),
    )


def rms_norm(values, gain):
    mean_square = jnp.mean(values * values, axis=-1, keepdims=True)
    return values * lax.rsqrt(mean_square + EPSILON) * gain


def dot(first, second):
    return jnp.dot(first, second, preferred_element_type=F32)


def dot_rows(first, second):
    return lax.dot_general(first, second, (((0,), (0,)), ((), ())), preferred_element_type=F32)


def dot_cols(first, second):
    return lax.dot_general(first, second, (((1,), (1,)), ((), ())), preferred_element_type=F32)


def of_head(h):
    return slice(h * DH, (h + 1) * DH)


def pick_copies(index, gu_ref, dn_ref, gu_buf, dn_buf, sems):
    copies = []
    for half in range(2):
        for part in range(2):
            rows = pl.ds(part * (D // 2), D // 2)
            copies.append((gu_ref.at[index, half, rows], gu_buf.at[half, rows]))
        rows = pl.ds(half * 128, 128)
        copies.append((dn_ref.at[index, rows], dn_buf.at[rows]))
    return [pltpu.make_async_copy(a, b, sems.at[i]) for i, (a, b) in enumerate(copies)]


def front_kernel(
    head_ref, x_ref, gain_ref, w_ref, gu_ref, dn_ref,
    normed_ref, k_ref, v_ref, send_ref, zero_ref, gu_out, dn_out,
    wk, wv, sems, read_sems,
):
    copy_k = pltpu.make_async_copy(w_ref.at[1], wk, sems.at[0])
    copy_v = pltpu.make_async_copy(w_ref.at[2], wv, sems.at[1])
    copy_k.start()
    copy_v.start()
    head = head_ref[0]
    reads = pick_copies(1 - (head & 1), gu_ref, dn_ref, gu_out, dn_out, read_sems)
    zero_ref[0] = 0
    normed = rms_norm(x_ref[...].astype(F32), gain_ref[...]).astype(BF)
    normed_ref[...] = normed
    copy_k.wait()
    for read in reads:
        read.start()
    key = dot(normed, wk[...]).astype(BF)
    k_ref[...] = key
    copy_v.wait()
    value = dot(normed, wv[...]).astype(BF)
    v_ref[...] = value
    for h in range(HEADS):
        state = dot_rows(key[:, of_head(h)], value[:, of_head(h)])
        send_ref[of_head(h), :] = state.astype(BF)
    for read in reads:
        read.wait()


def prefix_kernel(states_ref, out_ref):
    total = jnp.zeros((16, DH), F32)
    for s in range(32):
        out_ref[s] = total.astype(BF)
        total = total + states_ref[s].astype(F32)


def local_kernel(normed_ref, w_ref, k_ref, v_ref, q_ref, local_ref, wq, sems):
    copy_q = pltpu.make_async_copy(w_ref.at[0], wq, sems.at[0])
    copy_q.start()
    row = lax.broadcasted_iota(jnp.int32, (TOK, TOK), 0)
    causal = lax.broadcasted_iota(jnp.int32, (TOK, TOK), 1) <= row
    copy_q.wait()
    query = dot(normed_ref[...], wq[...]).astype(BF)
    q_ref[...] = query
    for h in range(HEADS):
        scores = dot_cols(query[:, of_head(h)], k_ref[:, of_head(h)])
        scores = jnp.where(causal, scores, 0.0).astype(BF)
        local_ref[:, of_head(h)] = dot(scores, v_ref[:, of_head(h)])


def attend_kernel(
    head_ref, earlier_ref, q_ref, local_ref, gain_ref, w_ref,
    own_ref, s1, s2, s3, mixed_ref, turned_ref,
):
    head = head_ref[0]
    for h in range(HEADS):
        attended = local_ref[:, of_head(h)] + dot(q_ref[:, of_head(h)], earlier_ref[of_head(h), :])
        mixed_ref[:, of_head(h)] = rms_norm(attended, gain_ref[:, of_head(h)]).astype(BF)
    for k in range(4):
        start = pl.multiple_of(((head - k) % 4) * ROWS, ROWS)
        turned_ref[k * ROWS:(k + 1) * ROWS, :] = mixed_ref[pl.ds(start, ROWS), :]
    for n in range(4):
        cols = slice(n * 512, (n + 1) * 512)
        rows = dot(turned_ref[...], w_ref[:, cols])
        own_ref[:, cols] = rows[:ROWS]
        s3[:, cols] = rows[ROWS:2 * ROWS].astype(BF)
        s2[:, cols] = rows[2 * ROWS:3 * ROWS].astype(BF)
        s1[:, cols] = rows[3 * ROWS:].astype(BF)


def norm_kernel(mine_ref, own_ref, g1, g2, g3, gain_ref, resid_ref, normed_ref):
    total = own_ref[...] + g1[...].astype(F32) + g2[...].astype(F32) + g3[...].astype(F32)
    resid = mine_ref[...].astype(F32) + total
    resid_ref[...] = resid
    normed_ref[...] = rms_norm(resid, gain_ref[...]).astype(BF)


def last_kernel(resid_ref, own_ref, g1, g2, g3, out_ref):
    total = own_ref[...] + g1[...].astype(F32) + g2[...].astype(F32) + g3[...].astype(F32)
    out_ref[...] = (resid_ref[...] + total).astype(BF)


def routing_kernel(head_ref, t0, t1, t2, t3, place_ref, weight_ref):
    head = head_ref[0]
    tables = jnp.concatenate([t0[...], t1[...], t2[...], t3[...]], axis=0)
    wanted = lax.broadcasted_iota(jnp.int32, (TOK, 16), 1) * 4 + head
    chosen = jnp.zeros((TOK, 16), F32)
    gates = jnp.zeros((TOK, 16), F32)
    for k in range(TOP):
        hit = tables[:, k:k + 1].astype(jnp.int32) == wanted
        chosen = chosen + hit.astype(F32)
        gates = gates + jnp.where(hit, tables[:, TOP + k:TOP + k + 1], 0.0)
    row = lax.broadcasted_iota(jnp.int32, (TOK, TOK), 0)
    col = lax.broadcasted_iota(jnp.int32, (TOK, TOK), 1)
    before = ((row // ROWS == col // ROWS) & (col < row)).astype(F32).astype(BF)
    rank = dot(before, chosen.astype(BF))
    block = (head - lax.broadcasted_iota(jnp.int32, (TOK, 16), 0) // ROWS) & 3
    base = ((block >> 1) * 18 + (block & 1) * CAP).astype(F32)
    slot = jnp.where(chosen > 0, base + rank, -1.0).astype(BF)

    def of_row(shape, axis):
        row = lax.broadcasted_iota(jnp.int32, shape, axis)
        is_main = row < MAIN
        chip = jnp.where(is_main, row >> 5, (row & 31) >> 1)
        core = jnp.where(is_main, (row >> 4) & 1, row & 1)
        within = jnp.where(is_main, row & 15, 16 + ((row - MAIN) >> 5))
        return chip, (core * 18 + within).astype(F32)

    chip, want = of_row((SLOTS, 16), 0)
    spread = (chip == lax.broadcasted_iota(jnp.int32, (SLOTS, 16), 1)).astype(F32).astype(BF)
    place_ref[...] = (dot_cols(spread, slot) == want[:, :1]).astype(F32).astype(BF)
    chip, want = of_row((16, SLOTS), 1)
    spread = (chip == lax.broadcasted_iota(jnp.int32, (16, SLOTS), 0)).astype(F32).astype(BF)
    at_row = dot(slot, spread) == want[:1, :]
    weight_ref[...] = jnp.where(at_row, dot(gates.astype(BF), spread), 0.0).astype(BF)


def dispatch_kernel(place_ref, t0, t1, t2, t3, out_ref, tokens):
    for k, ref in enumerate((t0, t1, t2, t3)):
        tokens[k * ROWS:(k + 1) * ROWS, :] = ref[...]
    tail = []
    for n in range(4):
        cols = slice(n * 512, (n + 1) * 512)
        rows = dot(place_ref[...], tokens[:, cols])
        out_ref[:, cols] = rows[:MAIN].astype(BF)
        tail.append(rows[MAIN:])
    tail = jnp.concatenate(tail, axis=1)
    for t in range(2):
        piece = tail[t * 32:(t + 1) * 32].reshape(MAIN, 128).astype(BF)
        out_ref[:, D + t * 128:D + (t + 1) * 128] = piece


def start_quarters(keep_ref, arrays, dest_of, sems, first, count=4):
    def load(q, ref):
        return pltpu.make_async_copy(ref, dest_of(q), sems.at[first + q])

    keep = keep_ref[0] == 1
    copies = [load(0, arrays[0]), load(1, arrays[1]), load(2, arrays[2])]
    copies[0].start()
    copies[1].start()

    @pl.when(keep)
    def _():
        load(2, arrays[2]).start()
        if count == 4:
            load(3, arrays[5]).start()

    @pl.when(jnp.logical_not(keep))
    def _():
        load(2, arrays[3]).start()
        if count == 4:
            load(3, arrays[4]).start()

    return copies + ([load(3, arrays[4])] if count == 4 else [])


def gate_kernel(
    keep_ref, x_ref, gu0, gu1, gu2, gu3, gu4, gu5, dn0, dn1, dn2, dn3,
    act_ref, down_ref, rows, gate_up, sems,
):
    copies = start_quarters(
        keep_ref, (gu0, gu1, gu2, gu3, gu4, gu5), lambda q: gate_up.at[q], sems, 0
    )
    down_copies = start_quarters(
        keep_ref,
        (dn0, dn1, dn2, dn3),
        lambda q: down_ref.at[q * 256:(q + 1) * 256],
        sems,
        4,
        3,
    )
    rows[:MAIN, :] = x_ref[:, :D]
    for t in range(2):
        piece = x_ref[:, D + t * 128:D + (t + 1) * 128].astype(F32).reshape(32, D)
        rows[MAIN + t * 32:MAIN + (t + 1) * 32, :] = piece.astype(BF)
    for q in range(4):
        copies[q].wait()
        gate = dot(rows[...], gate_up[q, 0])
        up = dot(rows[...], gate_up[q, 1])
        act_ref[:, q * 256:(q + 1) * 256] = (jax.nn.silu(gate) * up).astype(BF)
    for copy in down_copies:
        copy.wait()


def down_kernel(keep_ref, act, down, dn4, dn5, out_ref, last, main, tail, ends, sems):
    keep = keep_ref[0] == 1

    @pl.when(keep)
    def _():
        pltpu.make_async_copy(dn5, last, sems.at[0]).start()

    @pl.when(jnp.logical_not(keep))
    def _():
        pltpu.make_async_copy(dn4, last, sems.at[0]).start()

    writes = []
    for n in range(4):
        cols = slice(n * 512, (n + 1) * 512)
        result = dot(act[:, :768], down[:, cols])
        if n == 0:
            pltpu.make_async_copy(dn4, last, sems.at[0]).wait()
        result = result + dot(act[:, 768:], last[:, cols])
        main[:, cols] = result[:MAIN].astype(BF)
        tail[:, cols] = result[MAIN:]
        write = pltpu.make_async_copy(main.at[:, cols], out_ref.at[:, cols], sems.at[1 + n])
        write.start()
        writes.append(write)
    for t in range(2):
        piece = tail[t * 32:(t + 1) * 32, :].reshape(MAIN, 128).astype(BF)
        ends[:, t * 128:(t + 1) * 128] = piece
    write = pltpu.make_async_copy(ends, out_ref.at[:, D:], sems.at[5])
    write.start()
    for write in writes + [write]:
        write.wait()


def combine_kernel(weight_ref, y_ref, own_ref, s1, s2, s3, tail):
    for t in range(2):
        piece = y_ref[:, D + t * 128:D + (t + 1) * 128].astype(F32).reshape(32, D)
        tail[t * 32:(t + 1) * 32, :] = piece.astype(BF)
    for n in range(4):
        cols = slice(n * 512, (n + 1) * 512)
        rows = dot(weight_ref[:, :MAIN], y_ref[:, cols]) + dot(weight_ref[:, MAIN:], tail[:, cols])
        own_ref[:, cols] = rows[:ROWS]
        s3[:, cols] = rows[ROWS:2 * ROWS].astype(BF)
        s2[:, cols] = rows[2 * ROWS:3 * ROWS].astype(BF)
        s1[:, cols] = rows[3 * ROWS:].astype(BF)


BLOCKS_OUT = [out((ROWS, D), F32)] + [out((ROWS, D), BF)] * 3


def seq_perm(dy, dz, dc):
    return [
        ((y * 4 + z) * 2 + c, (((y + dy) % 4) * 4 + (z + dz) % 4) * 2 + (c ^ dc))
        for y in range(4)
        for z in range(4)
        for c in range(2)
    ]


def head_perm(shift):
    return [(h, (h + shift) % 4) for h in range(4)]


def device_perm(target):
    pairs = []
    for chip in range(16):
        for c in range(2):
            for h in range(4):
                to = target(c, h)
                if to is None:
                    continue
                pairs.append(((chip * 2 + c) * 4 + h, (chip * 2 + to[0]) * 4 + to[1]))
    return pairs


def near_target(c, h):
    chip = 2 * c + 1 - (h & 1)
    return (c, chip) if (chip - 1) % 4 == h else (1 - c, chip)


def far_target(c, h):
    return None if h // 2 == c else (1 - c, (h + 2) % 4)


def keep_target(c, h):
    return (1 - c, h) if h // 2 == c else None


def pass_target(c, h):
    return None if h // 2 == c else (1 - c, h)


def permute_all(arrays, axes, perm):
    return [lax.ppermute(a, axes, perm) for a in arrays]


def pick_kernel(index_ref, gu_ref, dn_ref, gu_out, dn_out, gu_buf, dn_buf, read_sems, write_sems):
    reads = pick_copies(index_ref[0], gu_ref, dn_ref, gu_buf, dn_buf, read_sems)
    writes = []
    for half in range(2):
        for part in range(2):
            rows = pl.ds(part * (D // 2), D // 2)
            writes.append((gu_buf.at[half, rows], gu_out.at[half, rows]))
        rows = pl.ds(half * 128, 128)
        writes.append((dn_buf.at[rows], dn_out.at[rows]))
    writes = [pltpu.make_async_copy(a, b, write_sems.at[i]) for i, (a, b) in enumerate(writes)]
    for read in reads:
        read.start()
    for read, write in zip(reads, writes):
        read.wait()
        write.start()
    for write in writes:
        write.wait()


QUARTER = [out((2, D, 256), BF), out((256, D), BF)]
RESULTS = out((MAIN, PACKED), BF)
PICK_SCRATCH = [
    pltpu.VMEM((2, D, 256), BF),
    pltpu.VMEM((256, D), BF),
    pltpu.SemaphoreType.DMA((6,)),
    pltpu.SemaphoreType.DMA((6,)),
]


def pick(w_gate_up, w_down, index):
    return pl.pallas_call(
        pick_kernel,
        in_specs=[SMEM, HBM, HBM],
        out_specs=[HBM, HBM],
        out_shape=QUARTER,
        scratch_shapes=PICK_SCRATCH,
        compiler_params=pltpu.CompilerParams(vmem_limit_bytes=50 << 20),
        name="pick",
    )(index.astype(jnp.int32)[None], w_gate_up, w_down)


def gather_head(array):
    return [array] + [lax.ppermute(array, "head", head_perm(k)) for k in range(1, 4)]


def on_device(
    hidden_in, attn_gain, w_qkv, out_gain, w_out, moe_gain, routes, gate_weights, w_gate_up, w_down
):
    seq = lax.axis_index("seq")
    head = lax.axis_index("head")
    core = seq % 2

    w_planes = w_qkv.transpose(1, 0, 2)
    here = head.astype(jnp.int32)[None]
    normed, key, value, send_state, zero, *near = call(
        front_kernel,
        [SMEM, VMEM, VMEM, HBM, HBM, HBM],
        [
            chip((TOK, D), BF),
            chip((TOK, WIDE), BF),
            out((TOK, WIDE), BF),
            out((WIDE, DH), BF),
            out((1,), jnp.int32),
            chip((2, D, 256), BF),
            chip((256, D), BF),
        ],
        [
            pltpu.VMEM((D, WIDE), BF),
            pltpu.VMEM((D, WIDE), BF),
            pltpu.SemaphoreType.DMA((2,)),
            pltpu.SemaphoreType.DMA((6,)),
        ],
    )(
        here,
        hidden_in,
        attn_gain[None, :],
        w_planes,
        w_gate_up,
        w_down,
    )
    both = ("seq", "head")
    near = permute_all(near, both, device_perm(near_target))
    states = lax.all_to_all(send_state.reshape(32, 16, DH), "seq", 0, 0, tiled=True)
    sums = call(prefix_kernel, [VMEM], [out((32, 16, DH), BF)])(on_chip(states))[0]
    earlier = lax.all_to_all(sums, "seq", 0, 0, tiled=True).reshape(WIDE, DH)
    odd = (head & 1) + zero[0]
    rest = pick(w_gate_up, w_down, odd)
    far_down = lax.ppermute(rest[1], both, device_perm(far_target))
    far = [lax.ppermute(rest[0], both, device_perm(far_target)), far_down]
    rest_other = permute_all(rest, both, device_perm(keep_target))
    near_other = permute_all(near, "seq", seq_perm(0, 0, 1))
    far_other = [lax.ppermute(far[0], both, device_perm(pass_target))]
    far_other.append(lax.ppermute(far[1], both, device_perm(pass_target)))
    pieces = [near, near_other, rest, rest_other, far, far_other]

    query, local = call(
        local_kernel,
        [VMEM, HBM, VMEM, VMEM],
        [out((TOK, WIDE), BF), chip((TOK, WIDE), F32)],
        [pltpu.VMEM((D, WIDE), BF), pltpu.SemaphoreType.DMA((1,))],
    )(on_chip(normed), w_planes, on_chip(key), value)
    blocks = call(
        attend_kernel,
        [SMEM] + [VMEM] * 5,
        [chip((ROWS, D), F32)] + BLOCKS_OUT[1:],
        [pltpu.VMEM((TOK, WIDE), BF), pltpu.VMEM((TOK, WIDE), BF)],
    )(here, on_chip(earlier), query, on_chip(local), out_gain[None, :], w_out)
    tables = gather_head(jnp.concatenate([routes.astype(F32), gate_weights], axis=1))
    place_rows, weight = call(
        routing_kernel, [SMEM] + [VMEM] * 4, [chip((SLOTS, TOK), BF), chip((TOK, SLOTS), BF)]
    )(here, *[on_chip(t) for t in tables])

    got = [lax.ppermute(blocks[k], "head", head_perm(k)) for k in range(1, 4)]
    mine = lax.dynamic_slice_in_dim(hidden_in, head * ROWS + zero[0], ROWS, 0)
    resid, normed2 = call(
        norm_kernel, [VMEM] * 6, [out((ROWS, D), F32), chip((ROWS, D), BF)]
    )(on_chip(mine), on_chip(blocks[0]), *[on_chip(g) for g in got], moe_gain[None, :])
    tokens = gather_head(normed2)

    sent = call(
        dispatch_kernel, [VMEM] * 5, [out((MAIN, PACKED), BF)], [pltpu.VMEM((TOK, D), BF)]
    )(on_chip(place_rows), *[on_chip(t) for t in tokens])[0]
    received = lax.all_to_all(sent.reshape(32, 16, PACKED), "seq", 0, 0, tiled=True)
    keep = (head // 2 == core).astype(jnp.int32)[None]
    gate_ups = [p[0] for p in pieces]
    downs = [p[1] for p in pieces]
    act, down = call(
        gate_kernel,
        [SMEM, VMEM] + [ANY] * 10,
        [chip((SLOTS, 1024), BF), chip((768, D), BF)],
        [
            pltpu.VMEM((SLOTS, D), BF),
            pltpu.VMEM((4, 2, D, 256), BF),
            pltpu.SemaphoreType.DMA((7,)),
        ],
    )(keep, on_chip(received.reshape(MAIN, PACKED)), *gate_ups, *downs[:4])
    results = call(
        down_kernel,
        [SMEM, VMEM, VMEM, ANY, ANY],
        [RESULTS],
        [
            pltpu.VMEM((256, D), BF),
            pltpu.VMEM((MAIN, D), BF),
            pltpu.VMEM((64, D), F32),
            pltpu.VMEM((MAIN, 256), BF),
            pltpu.SemaphoreType.DMA((6,)),
        ],
        direct=[RESULTS],
    )(keep, on_chip(act), on_chip(down), *downs[4:])[0]
    back = lax.all_to_all(results.reshape(32, 16, PACKED), "seq", 0, 0, tiled=True)
    blocks = call(
        combine_kernel,
        [VMEM] * 2,
        [chip((ROWS, D), F32)] + BLOCKS_OUT[1:],
        [pltpu.VMEM((64, D), BF)],
    )(on_chip(weight), on_chip(back.reshape(MAIN, PACKED)))
    got = [lax.ppermute(blocks[k], "head", head_perm(k)) for k in range(1, 4)]
    return call(last_kernel, [VMEM] * 5, [out((ROWS, D), BF)])(
        on_chip(resid), on_chip(blocks[0]), *[on_chip(g) for g in got]
    )[0]


def solution(mesh):
    placed = (
        P("seq", None),
        P(),
        P(None, None, "head"),
        P("head"),
        P("head", None),
        P(),
        P(("seq", "head"), None),
        P(("seq", "head"), None),
        P("seq", None, None, "head"),
        P("seq", "head", None),
    )

    return jax.shard_map(
        on_device, mesh=mesh, in_specs=placed, out_specs=P(("seq", "head"), None), check_vma=False
    )
```

```python
import jax
import jax.numpy as jnp
from jax import lax
from jax.experimental import pallas as pl
from jax.experimental.pallas import tpu as pltpu
from jax.sharding import PartitionSpec as P

D = 2048
DH = 128
HEADS = 4
WIDE = HEADS * DH
TOP = 8
CAP = 9
ROWS = 64
TOK = 256
MAIN = 512
SLOTS = 576
PACKED = D + 256
EPSILON = 1e-06
BF = jnp.bfloat16
F32 = jnp.float32


VMEM = pl.BlockSpec(memory_space=pltpu.VMEM)
SMEM = pl.BlockSpec(memory_space=pltpu.SMEM)
ANY = pl.BlockSpec(memory_space=pl.ANY)
HBM = pl.BlockSpec(memory_space=pltpu.HBM)


def on_chip(array):
    return pltpu.with_memory_space_constraint(array, pltpu.VMEM)


def out(shape, dtype):
    return jax.ShapeDtypeStruct(shape, dtype)


def chip(shape, dtype):
    return pltpu.VMEM(shape, dtype)


def spec_of(o, direct):
    if o.dtype == jnp.int32:
        return SMEM
    return HBM if o in direct else VMEM


def call(kernel, ins, outs, scratch=(), limit=54, direct=()):
    return pl.pallas_call(
        kernel,
        in_specs=ins,
        out_specs=[spec_of(o, direct) for o in outs],
        out_shape=outs,
        scratch_shapes=list(scratch),
        compiler_params=pltpu.CompilerParams(vmem_limit_bytes=limit << 20),
    )


def rms_norm(values, gain):
    mean_square = jnp.mean(values * values, axis=-1, keepdims=True)
    return values * lax.rsqrt(mean_square + EPSILON) * gain


def dot(first, second):
    return jnp.dot(first, second, preferred_element_type=F32)


def dot_rows(first, second):
    return lax.dot_general(first, second, (((0,), (0,)), ((), ())), preferred_element_type=F32)


def dot_cols(first, second):
    return lax.dot_general(first, second, (((1,), (1,)), ((), ())), preferred_element_type=F32)


def of_head(h):
    return slice(h * DH, (h + 1) * DH)


def pick_copies(index, gu_ref, dn_ref, gu_buf, dn_buf, sems):
    copies = []
    for half in range(2):
        for part in range(2):
            rows = pl.ds(part * (D // 2), D // 2)
            copies.append((gu_ref.at[index, half, rows], gu_buf.at[half, rows]))
        rows = pl.ds(half * 128, 128)
        copies.append((dn_ref.at[index, rows], dn_buf.at[rows]))
    return [pltpu.make_async_copy(a, b, sems.at[i]) for i, (a, b) in enumerate(copies)]


def front_kernel(
    head_ref, x_ref, gain_ref, w_ref, gu_ref, dn_ref,
    normed_ref, k_ref, v_ref, send_ref, zero_ref, gu_out, dn_out,
    wk, wv, sems, read_sems,
):
    copy_k = pltpu.make_async_copy(w_ref.at[1], wk, sems.at[0])
    copy_v = pltpu.make_async_copy(w_ref.at[2], wv, sems.at[1])
    copy_k.start()
    copy_v.start()
    head = head_ref[0]
    reads = pick_copies(1 - (head & 1), gu_ref, dn_ref, gu_out, dn_out, read_sems)
    zero_ref[0] = 0
    normed = rms_norm(x_ref[...].astype(F32), gain_ref[...]).astype(BF)
    normed_ref[...] = normed
    copy_k.wait()
    for read in reads:
        read.start()
    key = dot(normed, wk[...]).astype(BF)
    k_ref[...] = key
    copy_v.wait()
    value = dot(normed, wv[...]).astype(BF)
    v_ref[...] = value
    for h in range(HEADS):
        state = dot_rows(key[:, of_head(h)], value[:, of_head(h)])
        send_ref[of_head(h), :] = state.astype(BF)
    for read in reads:
        read.wait()


def prefix_kernel(states_ref, out_ref):
    total = jnp.zeros((16, DH), F32)
    for s in range(32):
        out_ref[s] = total.astype(BF)
        total = total + states_ref[s].astype(F32)


def local_kernel(normed_ref, w_ref, k_ref, v_ref, q_ref, local_ref, wq, sems):
    copy_q = pltpu.make_async_copy(w_ref.at[0], wq, sems.at[0])
    copy_q.start()
    row = lax.broadcasted_iota(jnp.int32, (TOK, TOK), 0)
    causal = lax.broadcasted_iota(jnp.int32, (TOK, TOK), 1) <= row
    copy_q.wait()
    query = dot(normed_ref[...], wq[...]).astype(BF)
    q_ref[...] = query
    for h in range(HEADS):
        scores = dot_cols(query[:, of_head(h)], k_ref[:, of_head(h)])
        scores = jnp.where(causal, scores, 0.0).astype(BF)
        local_ref[:, of_head(h)] = dot(scores, v_ref[:, of_head(h)])


def attend_kernel(
    head_ref, earlier_ref, q_ref, local_ref, gain_ref, w_ref,
    own_ref, s1, s2, s3, mixed_ref, turned_ref,
):
    head = head_ref[0]
    for h in range(HEADS):
        attended = local_ref[:, of_head(h)] + dot(q_ref[:, of_head(h)], earlier_ref[of_head(h), :])
        mixed_ref[:, of_head(h)] = rms_norm(attended, gain_ref[:, of_head(h)]).astype(BF)
    for k in range(4):
        start = pl.multiple_of(((head - k) % 4) * ROWS, ROWS)
        turned_ref[k * ROWS:(k + 1) * ROWS, :] = mixed_ref[pl.ds(start, ROWS), :]
    for n in range(4):
        cols = slice(n * 512, (n + 1) * 512)
        rows = dot(turned_ref[...], w_ref[:, cols])
        own_ref[:, cols] = rows[:ROWS]
        s3[:, cols] = rows[ROWS:2 * ROWS].astype(BF)
        s2[:, cols] = rows[2 * ROWS:3 * ROWS].astype(BF)
        s1[:, cols] = rows[3 * ROWS:].astype(BF)


def norm_kernel(mine_ref, own_ref, g1, g2, g3, gain_ref, resid_ref, normed_ref):
    total = own_ref[...] + g1[...].astype(F32) + g2[...].astype(F32) + g3[...].astype(F32)
    resid = mine_ref[...].astype(F32) + total
    resid_ref[...] = resid
    normed_ref[...] = rms_norm(resid, gain_ref[...]).astype(BF)


def last_kernel(resid_ref, own_ref, g1, g2, g3, out_ref):
    total = own_ref[...] + g1[...].astype(F32) + g2[...].astype(F32) + g3[...].astype(F32)
    out_ref[...] = (resid_ref[...] + total).astype(BF)


def routing_kernel(head_ref, t0, t1, t2, t3, place_ref, weight_ref):
    head = head_ref[0]
    tables = jnp.concatenate([t0[...], t1[...], t2[...], t3[...]], axis=0)
    wanted = lax.broadcasted_iota(jnp.int32, (TOK, 16), 1) * 4 + head
    chosen = jnp.zeros((TOK, 16), F32)
    gates = jnp.zeros((TOK, 16), F32)
    for k in range(TOP):
        hit = tables[:, k:k + 1].astype(jnp.int32) == wanted
        chosen = chosen + hit.astype(F32)
        gates = gates + jnp.where(hit, tables[:, TOP + k:TOP + k + 1], 0.0)
    row = lax.broadcasted_iota(jnp.int32, (TOK, TOK), 0)
    col = lax.broadcasted_iota(jnp.int32, (TOK, TOK), 1)
    before = ((row // ROWS == col // ROWS) & (col < row)).astype(F32).astype(BF)
    rank = dot(before, chosen.astype(BF))
    block = (head - lax.broadcasted_iota(jnp.int32, (TOK, 16), 0) // ROWS) & 3
    base = ((block >> 1) * 18 + (block & 1) * CAP).astype(F32)
    slot = jnp.where(chosen > 0, base + rank, -1.0).astype(BF)

    def of_row(shape, axis):
        row = lax.broadcasted_iota(jnp.int32, shape, axis)
        is_main = row < MAIN
        chip = jnp.where(is_main, row >> 5, (row & 31) >> 1)
        core = jnp.where(is_main, (row >> 4) & 1, row & 1)
        within = jnp.where(is_main, row & 15, 16 + ((row - MAIN) >> 5))
        return chip, (core * 18 + within).astype(F32)

    chip, want = of_row((SLOTS, 16), 0)
    spread = (chip == lax.broadcasted_iota(jnp.int32, (SLOTS, 16), 1)).astype(F32).astype(BF)
    place_ref[...] = (dot_cols(spread, slot) == want[:, :1]).astype(F32).astype(BF)
    chip, want = of_row((16, SLOTS), 1)
    spread = (chip == lax.broadcasted_iota(jnp.int32, (16, SLOTS), 0)).astype(F32).astype(BF)
    at_row = dot(slot, spread) == want[:1, :]
    weight_ref[...] = jnp.where(at_row, dot(gates.astype(BF), spread), 0.0).astype(BF)


def dispatch_kernel(place_ref, t0, t1, t2, t3, out_ref, tokens):
    for k, ref in enumerate((t0, t1, t2, t3)):
        tokens[k * ROWS:(k + 1) * ROWS, :] = ref[...]
    tail = []
    for n in range(4):
        cols = slice(n * 512, (n + 1) * 512)
        rows = dot(place_ref[...], tokens[:, cols])
        out_ref[:, cols] = rows[:MAIN].astype(BF)
        tail.append(rows[MAIN:])
    tail = jnp.concatenate(tail, axis=1)
    for t in range(2):
        piece = tail[t * 32:(t + 1) * 32].reshape(MAIN, 128).astype(BF)
        out_ref[:, D + t * 128:D + (t + 1) * 128] = piece


def start_quarters(keep_ref, arrays, dest_of, sems, first, count=4):
    def load(q, ref):
        return pltpu.make_async_copy(ref, dest_of(q), sems.at[first + q])

    keep = keep_ref[0] == 1
    copies = [load(0, arrays[0]), load(1, arrays[1]), load(2, arrays[2])]
    copies[0].start()
    copies[1].start()

    @pl.when(keep)
    def _():
        load(2, arrays[2]).start()
        if count == 4:
            load(3, arrays[5]).start()

    @pl.when(jnp.logical_not(keep))
    def _():
        load(2, arrays[3]).start()
        if count == 4:
            load(3, arrays[4]).start()

    return copies + ([load(3, arrays[4])] if count == 4 else [])


def gate_kernel(
    keep_ref, x_ref, gu0, gu1, gu2, gu3, gu4, gu5, dn0, dn1, dn2, dn3,
    act_ref, down_ref, rows, gate_up, sems,
):
    copies = start_quarters(
        keep_ref, (gu0, gu1, gu2, gu3, gu4, gu5), lambda q: gate_up.at[q], sems, 0
    )
    down_copies = start_quarters(
        keep_ref,
        (dn0, dn1, dn2, dn3),
        lambda q: down_ref.at[q * 256:(q + 1) * 256],
        sems,
        4,
        3,
    )
    rows[:MAIN, :] = x_ref[:, :D]
    for t in range(2):
        piece = x_ref[:, D + t * 128:D + (t + 1) * 128].astype(F32).reshape(32, D)
        rows[MAIN + t * 32:MAIN + (t + 1) * 32, :] = piece.astype(BF)
    for q in range(4):
        copies[q].wait()
        gate = dot(rows[...], gate_up[q, 0])
        up = dot(rows[...], gate_up[q, 1])
        act_ref[:, q * 256:(q + 1) * 256] = (jax.nn.silu(gate) * up).astype(BF)
    for copy in down_copies:
        copy.wait()


def down_kernel(keep_ref, act, down, dn4, dn5, out_ref, last, main, tail, ends, sems):
    keep = keep_ref[0] == 1

    @pl.when(keep)
    def _():
        pltpu.make_async_copy(dn5, last, sems.at[0]).start()

    @pl.when(jnp.logical_not(keep))
    def _():
        pltpu.make_async_copy(dn4, last, sems.at[0]).start()

    writes = []
    for n in range(4):
        cols = slice(n * 512, (n + 1) * 512)
        result = dot(act[:, :768], down[:, cols])
        if n == 0:
            pltpu.make_async_copy(dn4, last, sems.at[0]).wait()
        result = result + dot(act[:, 768:], last[:, cols])
        main[:, cols] = result[:MAIN].astype(BF)
        tail[:, cols] = result[MAIN:]
        write = pltpu.make_async_copy(main.at[:, cols], out_ref.at[:, cols], sems.at[1 + n])
        write.start()
        writes.append(write)
    for t in range(2):
        piece = tail[t * 32:(t + 1) * 32, :].reshape(MAIN, 128).astype(BF)
        ends[:, t * 128:(t + 1) * 128] = piece
    write = pltpu.make_async_copy(ends, out_ref.at[:, D:], sems.at[5])
    write.start()
    for write in writes + [write]:
        write.wait()


def combine_kernel(weight_ref, y_ref, own_ref, s1, s2, s3, tail):
    for t in range(2):
        piece = y_ref[:, D + t * 128:D + (t + 1) * 128].astype(F32).reshape(32, D)
        tail[t * 32:(t + 1) * 32, :] = piece.astype(BF)
    for n in range(4):
        cols = slice(n * 512, (n + 1) * 512)
        rows = dot(weight_ref[:, :MAIN], y_ref[:, cols]) + dot(weight_ref[:, MAIN:], tail[:, cols])
        own_ref[:, cols] = rows[:ROWS]
        s3[:, cols] = rows[ROWS:2 * ROWS].astype(BF)
        s2[:, cols] = rows[2 * ROWS:3 * ROWS].astype(BF)
        s1[:, cols] = rows[3 * ROWS:].astype(BF)


BLOCKS_OUT = [out((ROWS, D), F32)] + [out((ROWS, D), BF)] * 3


def seq_perm(dy, dz, dc):
    return [
        ((y * 4 + z) * 2 + c, (((y + dy) % 4) * 4 + (z + dz) % 4) * 2 + (c ^ dc))
        for y in range(4)
        for z in range(4)
        for c in range(2)
    ]


def head_perm(shift):
    return [(h, (h + shift) % 4) for h in range(4)]


def device_perm(target):
    pairs = []
    for chip in range(16):
        for c in range(2):
            for h in range(4):
                to = target(c, h)
                if to is None:
                    continue
                pairs.append(((chip * 2 + c) * 4 + h, (chip * 2 + to[0]) * 4 + to[1]))
    return pairs


def near_target(c, h):
    chip = 2 * c + 1 - (h & 1)
    return (c, chip) if (chip - 1) % 4 == h else (1 - c, chip)


def far_target(c, h):
    return None if h // 2 == c else (1 - c, (h + 2) % 4)


def keep_target(c, h):
    return (1 - c, h) if h // 2 == c else None


def pass_target(c, h):
    return None if h // 2 == c else (1 - c, h)


def permute_all(arrays, axes, perm):
    return [lax.ppermute(a, axes, perm) for a in arrays]


def pick_kernel(index_ref, gu_ref, dn_ref, gu_out, dn_out, gu_buf, dn_buf, read_sems, write_sems):
    reads = pick_copies(index_ref[0], gu_ref, dn_ref, gu_buf, dn_buf, read_sems)
    writes = []
    for half in range(2):
        for part in range(2):
            rows = pl.ds(part * (D // 2), D // 2)
            writes.append((gu_buf.at[half, rows], gu_out.at[half, rows]))
        rows = pl.ds(half * 128, 128)
        writes.append((dn_buf.at[rows], dn_out.at[rows]))
    writes = [pltpu.make_async_copy(a, b, write_sems.at[i]) for i, (a, b) in enumerate(writes)]
    for read in reads:
        read.start()
    for read, write in zip(reads, writes):
        read.wait()
        write.start()
    for write in writes:
        write.wait()


QUARTER = [out((2, D, 256), BF), out((256, D), BF)]
RESULTS = out((MAIN, PACKED), BF)
PICK_SCRATCH = [
    pltpu.VMEM((2, D, 256), BF),
    pltpu.VMEM((256, D), BF),
    pltpu.SemaphoreType.DMA((6,)),
    pltpu.SemaphoreType.DMA((6,)),
]


def pick(w_gate_up, w_down, index):
    return pl.pallas_call(
        pick_kernel,
        in_specs=[SMEM, HBM, HBM],
        out_specs=[HBM, HBM],
        out_shape=QUARTER,
        scratch_shapes=PICK_SCRATCH,
        compiler_params=pltpu.CompilerParams(vmem_limit_bytes=50 << 20),
        name="pick",
    )(index.astype(jnp.int32)[None], w_gate_up, w_down)


def send_head(blocks):
    got = [None] * 3
    for k in (2, 1, 3):
        got[k - 1] = lax.ppermute(blocks[k - 1], "head", head_perm(k))
    return got


def gather_head(array):
    return [array] + send_head([array] * 3)


def on_device(
    hidden_in, attn_gain, w_qkv, out_gain, w_out, moe_gain, routes, gate_weights, w_gate_up, w_down
):
    seq = lax.axis_index("seq")
    head = lax.axis_index("head")
    core = seq % 2

    w_planes = w_qkv.transpose(1, 0, 2)
    here = head.astype(jnp.int32)[None]
    normed, key, value, send_state, zero, *near = call(
        front_kernel,
        [SMEM, VMEM, VMEM, HBM, HBM, HBM],
        [
            chip((TOK, D), BF),
            chip((TOK, WIDE), BF),
            out((TOK, WIDE), BF),
            out((WIDE, DH), BF),
            out((1,), jnp.int32),
            chip((2, D, 256), BF),
            chip((256, D), BF),
        ],
        [
            pltpu.VMEM((D, WIDE), BF),
            pltpu.VMEM((D, WIDE), BF),
            pltpu.SemaphoreType.DMA((2,)),
            pltpu.SemaphoreType.DMA((6,)),
        ],
    )(
        here,
        hidden_in,
        attn_gain[None, :],
        w_planes,
        w_gate_up,
        w_down,
    )
    both = ("seq", "head")
    near = permute_all(near, both, device_perm(near_target))
    states = lax.all_to_all(send_state.reshape(32, 16, DH), "seq", 0, 0, tiled=True)
    sums = call(prefix_kernel, [VMEM], [out((32, 16, DH), BF)])(on_chip(states))[0]
    earlier = lax.all_to_all(sums, "seq", 0, 0, tiled=True).reshape(WIDE, DH)
    odd = (head & 1) + zero[0]
    rest = pick(w_gate_up, w_down, odd)
    far_down = lax.ppermute(rest[1], both, device_perm(far_target))
    far = [lax.ppermute(rest[0], both, device_perm(far_target)), far_down]
    rest_other = permute_all(rest, both, device_perm(keep_target))
    near_other = permute_all(near, "seq", seq_perm(0, 0, 1))
    far_other = [lax.ppermute(far[0], both, device_perm(pass_target))]
    far_other.append(lax.ppermute(far[1], both, device_perm(pass_target)))
    pieces = [near, near_other, rest, rest_other, far, far_other]

    query, local = call(
        local_kernel,
        [VMEM, HBM, VMEM, VMEM],
        [out((TOK, WIDE), BF), chip((TOK, WIDE), F32)],
        [pltpu.VMEM((D, WIDE), BF), pltpu.SemaphoreType.DMA((1,))],
    )(on_chip(normed), w_planes, on_chip(key), value)
    blocks = call(
        attend_kernel,
        [SMEM] + [VMEM] * 5,
        [chip((ROWS, D), F32)] + BLOCKS_OUT[1:],
        [pltpu.VMEM((TOK, WIDE), BF), pltpu.VMEM((TOK, WIDE), BF)],
    )(here, on_chip(earlier), query, on_chip(local), out_gain[None, :], w_out)
    tables = gather_head(jnp.concatenate([routes.astype(F32), gate_weights], axis=1))
    place_rows, weight = call(
        routing_kernel, [SMEM] + [VMEM] * 4, [chip((SLOTS, TOK), BF), chip((TOK, SLOTS), BF)]
    )(here, *[on_chip(t) for t in tables])

    got = send_head(blocks[1:])
    mine = lax.dynamic_slice_in_dim(hidden_in, head * ROWS + zero[0], ROWS, 0)
    resid, normed2 = call(
        norm_kernel, [VMEM] * 6, [out((ROWS, D), F32), chip((ROWS, D), BF)]
    )(on_chip(mine), on_chip(blocks[0]), *[on_chip(g) for g in got], moe_gain[None, :])
    tokens = gather_head(normed2)

    sent = call(
        dispatch_kernel, [VMEM] * 5, [out((MAIN, PACKED), BF)], [pltpu.VMEM((TOK, D), BF)]
    )(on_chip(place_rows), *[on_chip(t) for t in tokens])[0]
    received = lax.all_to_all(sent.reshape(32, 16, PACKED), "seq", 0, 0, tiled=True)
    keep = (head // 2 == core).astype(jnp.int32)[None]
    gate_ups = [p[0] for p in pieces]
    downs = [p[1] for p in pieces]
    act, down = call(
        gate_kernel,
        [SMEM, VMEM] + [ANY] * 10,
        [chip((SLOTS, 1024), BF), chip((768, D), BF)],
        [
            pltpu.VMEM((SLOTS, D), BF),
            pltpu.VMEM((4, 2, D, 256), BF),
            pltpu.SemaphoreType.DMA((7,)),
        ],
    )(keep, on_chip(received.reshape(MAIN, PACKED)), *gate_ups, *downs[:4])
    results = call(
        down_kernel,
        [SMEM, VMEM, VMEM, ANY, ANY],
        [RESULTS],
        [
            pltpu.VMEM((256, D), BF),
            pltpu.VMEM((MAIN, D), BF),
            pltpu.VMEM((64, D), F32),
            pltpu.VMEM((MAIN, 256), BF),
            pltpu.SemaphoreType.DMA((6,)),
        ],
        direct=[RESULTS],
    )(keep, on_chip(act), on_chip(down), *downs[4:])[0]
    back = lax.all_to_all(results.reshape(32, 16, PACKED), "seq", 0, 0, tiled=True)
    blocks = call(
        combine_kernel,
        [VMEM] * 2,
        [chip((ROWS, D), F32)] + BLOCKS_OUT[1:],
        [pltpu.VMEM((64, D), BF)],
    )(on_chip(weight), on_chip(back.reshape(MAIN, PACKED)))
    got = send_head(blocks[1:])
    return call(last_kernel, [VMEM] * 5, [out((ROWS, D), BF)])(
        on_chip(resid), on_chip(blocks[0]), *[on_chip(g) for g in got]
    )[0]


def solution(mesh):
    placed = (
        P("seq", None),
        P(),
        P(None, None, "head"),
        P("head"),
        P("head", None),
        P(),
        P(("seq", "head"), None),
        P(("seq", "head"), None),
        P("seq", None, None, "head"),
        P("seq", "head", None),
    )

    return jax.shard_map(
        on_device, mesh=mesh, in_specs=placed, out_specs=P(("seq", "head"), None), check_vma=False
    )
```
